32 devices in a mesh: seq: 8 (over z, x), head: 4 (over y, core).
Axes of the slice: x: 2, y: 2, z: 4, core: 2. Of those that a mesh axis runs over, the one named last changes fastest.
Arguments:
- tokens: bfloat16 [2048, 2048], P('seq'), may hold values from -6 to 6
- input_gain: float32 [2048], replicated, may hold values from 0.1 to 1.9
- w_query: bfloat16 [2048, 4096], P(None, 'head'), may hold values from -0.125 to 0.125
- w_key: bfloat16 [2048, 512], P(None, 'head'), may hold values from -0.125 to 0.125
- w_value: bfloat16 [2048, 512], P(None, 'head'), may hold values from -0.125 to 0.125
- query_gain: float32 [128], replicated, may hold values from 1 to 8
- key_gain: float32 [128], replicated, may hold values from 1 to 8
- w_out: bfloat16 [4096, 2048], P('head'), may hold values from -0.09375 to 0.09375
- post_gain: float32 [2048], replicated, may hold values from 0.1 to 1.9
- expert_ids: int32 [2048, 8], P(('seq', 'head')), may hold values from 0 to 31, all different within a row; in each aligned block of 64 rows (0 to 63, 64 to 127, ...) at most 24 rows name the same one
- route_weights: float32 [2048, 8], P(('seq', 'head')), may hold values from 0.05 to 1
- w_gate: bfloat16 [32, 2048, 768], P(('seq', 'head')), may hold values from -0.125 to 0.125
- w_up: bfloat16 [32, 2048, 768], P(('seq', 'head')), may hold values from -0.125 to 0.125
- w_down: bfloat16 [32, 768, 2048], P(('seq', 'head')), may hold values from -0.21875 to 0.21875
Outputs:
- layer_out: bfloat16 [2048, 2048], P(('seq', 'head'))
The draws below stay inside these ranges and needn't reach their ends.
Inputs may be any that keep to these rules, and one draw needn't show every extreme that they name: `expert_ids`: the 8 experts of a token differ. In the rows of one device (64 tokens, aligned blocks), no expert is named more than 24 times.
All inputs are finite; a program needn't handle non-finite values.
Results may differ from the reference program's by a relative error of at most 0.012.
The reference program's roundings to bfloat16 on the way (of `normed`, `value_rows`, `probs`, `attended`, `routed`, `hidden` and `expert_rows`) count: a program that leaves them out, or rounds other values in their place, can miss the bound.
Values may be sent and summed in bfloat16 or wider, within the bound.
No kernel may reach another device: no remote copies, remote signals or barrier semaphores. Data moves between devices by JAX's collectives and lax.ppermute only.
A program may use at most 128 MiB of HBM per device.

```python
import math
import jax
import jax.numpy as jnp
import numpy as np
from jax import lax

D = 2048
HEADS = 32
KV_HEADS = 4
HEAD_DIM = 128
FF = 768
TOPK = 8
TOKENS = 2048
EXPERTS = 32
ROWS = 64
CAP = 24


def gain_values(base_key):
    return jnp.exp(jax.random.uniform(base_key, (HEAD_DIM,), jnp.float32, 0.0, 1.0986))


def draw_query_gain(key, part):
    return gain_values(jax.random.fold_in(key, 11))


def draw_key_gain(key, part):
    return gain_values(jax.random.fold_in(key, 23))


def block_scale(key, shape, cuts, low, high):
    def one(dim, parts):
        heights = jax.random.uniform(jax.random.fold_in(jax.random.fold_in(key, 6), dim), (parts,), jnp.float32, low / len(cuts), high / len(cuts))
        return jnp.repeat(jnp.exp(heights), shape[dim] // parts).reshape((-1,) + (1,) * (len(shape) - dim - 1))

    factor_of = one(*cuts[0])
    for cut in cuts[1:]:
        factor_of = factor_of * one(*cut)
    return factor_of


def routed_block(stream_key, own, number, rows, count, top, limit, slope):
    ranking = jax.random.permutation(stream_key, count)
    packed, common = portions_of(count, rows * top, limit, slope, True), portions_of(count, rows * top, limit, slope, False)
    places = jnp.arange(count)

    def named(tallies, turn):
        used = int((tallies > 0).sum())
        fixed = max(1, used // 4)
        passed = fixed + (places - fixed + turn * (used - fixed)) % max(1, count - fixed)
        return jnp.zeros((count,), jnp.int32).at[ranking[jnp.where(places < fixed, places, passed)]].set(jnp.asarray(tallies, jnp.int32))

    tallies = jnp.where(number % 4 == 0, named(packed, number // 4), named(common, number - number // 4 - 1))
    mixed = jax.random.permutation(jax.random.fold_in(own, 3), count)
    giver, receiver = mixed[0:count // 2 * 2:2], mixed[1:count // 2 * 2:2]
    margin = jnp.minimum(tallies[giver] - 1, limit - tallies[receiver]) // 2
    margin = jnp.where((giver == ranking[0]) | (receiver == ranking[0]) | (tallies[receiver] == 0), 0, jnp.maximum(margin, 0))
    passed = jax.random.randint(jax.random.fold_in(own, 4), (count // 2,), 0, 1 << 20) % (margin + 1)
    tallies = tallies.at[giver].add(-passed).at[receiver].add(passed)
    labels = jnp.searchsorted(jnp.cumsum(tallies), jnp.arange(rows * top), side="right").astype(jnp.int32)
    listing = labels.reshape(top, rows).T
    listing = listing[jax.random.permutation(jax.random.fold_in(own, 1), rows)]
    turn = jax.random.randint(jax.random.fold_in(own, 2), (rows, 1), 0, top)
    return jnp.take_along_axis(listing, (jnp.arange(top)[None, :] + turn) % top, axis=1)


def portions_of(count, total, most, slope, full):
    weights = [(1 << 20) // math.isqrt(rank ** slope) + 1 for rank in range(1, count + 1)]
    largest = most if full else min(most, max(-(-total // count), total * weights[0] // sum(weights)))
    least = 1 if total - largest >= count - 1 else 0
    counts, surplus = [largest] + [least] * (count - 1), total - largest - least * (count - 1)
    while surplus > 0:
        candidates = [i for i in range(1, count) if counts[i] < largest] or [i for i in range(1, count) if counts[i] < most]
        whole, left = sum([weights[i] for i in candidates]), surplus
        for i in candidates:
            more = min(most - counts[i], max(1, left * weights[i] // whole), surplus)
            counts[i] = counts[i] + more
            surplus = surplus - more
    return np.array(counts)


def bell_draw(rng, shape, scale, reach, shards=(), kind=jnp.bfloat16):
    level = block_scale(rng, shape, shards, -0.22, 0.18) if shards else 1.0
    result = jax.random.normal(rng, shape, jnp.float32) * scale * level
    return jnp.minimum(jnp.maximum(result, -reach), reach).astype(kind)


def setup_inputs(seed: int = 0) -> dict:
    arg_keys = jax.random.split(jax.random.key(seed), 15)
    tokens = bell_draw(arg_keys[0], (TOKENS, D), 1.0, 6.0, ((0, 8),))
    input_gain = jnp.clip(1.0 + 0.18 * jax.random.normal(arg_keys[1], (D,), jnp.float32), 0.1, 1.9)
    w_query = bell_draw(arg_keys[2], (D, HEADS * HEAD_DIM), D ** -0.5, 0.125, ((1, 4),))
    w_key = bell_draw(arg_keys[3], (D, KV_HEADS * HEAD_DIM), D ** -0.5, 0.125, ((1, 4),))
    w_value = bell_draw(arg_keys[4], (D, KV_HEADS * HEAD_DIM), D ** -0.5, 0.125, ((1, 4),))
    query_gain = draw_query_gain(jax.random.fold_in(arg_keys[14], 71), 0)
    key_gain = draw_key_gain(jax.random.fold_in(arg_keys[14], 71), 0)
    w_out = bell_draw(arg_keys[7], (HEADS * HEAD_DIM, D), (HEADS * HEAD_DIM) ** -0.5, 0.09375, ((0, 4),))
    post_gain = jnp.clip(1.0 + 0.18 * jax.random.normal(arg_keys[8], (D,), jnp.float32), 0.1, 1.9)
    expert_ids_keys = jax.random.split(jax.random.fold_in(arg_keys[9], 1), TOKENS // ROWS)
    expert_ids_turns = jax.random.permutation(jax.random.fold_in(arg_keys[9], 3), TOKENS // ROWS)
    expert_ids = jax.vmap(lambda own, number: routed_block(jax.random.fold_in(arg_keys[9], 2), own, number, ROWS, EXPERTS, TOPK, CAP, 2))(expert_ids_keys, expert_ids_turns).reshape((TOKENS, TOPK))
    route_weights = jnp.clip(jnp.exp(math.log(1.0) - 2.9957323 * jax.random.uniform(arg_keys[10], (TOKENS, TOPK), jnp.float32) ** block_scale(arg_keys[10], (TOKENS, TOPK), ((0, 32),), -0.2, 0.2)), 0.05, 1.0)
    w_gate = bell_draw(arg_keys[11], (EXPERTS, D, FF), D ** -0.5, 0.125, ((0, 32),))
    w_up = bell_draw(arg_keys[12], (EXPERTS, D, FF), D ** -0.5, 0.125, ((0, 32),))
    w_down = bell_draw(arg_keys[13], (EXPERTS, FF, D), FF ** -0.5, 0.21875, ((0, 32),))
    return {"tokens": tokens, "input_gain": input_gain, "w_query": w_query, "w_key": w_key, "w_value": w_value, "query_gain": query_gain, "key_gain": key_gain, "w_out": w_out, "post_gain": post_gain, "expert_ids": expert_ids, "route_weights": route_weights, "w_gate": w_gate, "w_up": w_up, "w_down": w_down}


EPSILON = 1e-06
THETA = 1000000.0

def rms_scale(vectors, gain_vector):
    mean_sq = lax.optimization_barrier(jnp.mean(vectors * vectors, axis=-1, keepdims=True))
    return vectors * lax.rsqrt(mean_sq + EPSILON) * gain_vector

def rotate(vectors, positions):
    half_dim = vectors.shape[-1] // 2
    frequency = THETA ** (-jnp.arange(half_dim, dtype=jnp.float32) * 2.0 / vectors.shape[-1])
    angles = positions[:, None] * frequency[None, :]
    cosine_table = jnp.cos(angles)[:, None, :]
    sine_table = jnp.sin(angles)[:, None, :]
    front_half = vectors[..., :half_dim]
    back_half = vectors[..., half_dim:]
    return jnp.concatenate([front_half * cosine_table - back_half * sine_table, back_half * cosine_table + front_half * sine_table], axis=-1)

def reference(tokens, input_gain, w_query, w_key, w_value, query_gain, key_gain, w_out, post_gain, expert_ids, route_weights, w_gate, w_up, w_down):
    normed = rms_scale(tokens.astype(jnp.float32), input_gain).astype(jnp.bfloat16)
    positions = jnp.arange(TOKENS, dtype=jnp.int32).astype(jnp.float32)
    queries = jnp.dot(normed, w_query, preferred_element_type=jnp.float32).reshape(TOKENS, HEADS, HEAD_DIM)
    key_rows = jnp.dot(normed, w_key, preferred_element_type=jnp.float32).reshape(TOKENS, KV_HEADS, HEAD_DIM)
    value_rows = jnp.dot(normed, w_value, preferred_element_type=jnp.float32).astype(jnp.bfloat16).reshape(TOKENS, KV_HEADS, HEAD_DIM)
    rot_q = rotate(rms_scale(queries, query_gain), positions).astype(jnp.bfloat16)
    rot_k = rotate(rms_scale(key_rows, key_gain), positions).astype(jnp.bfloat16)
    group_size = HEADS // KV_HEADS
    block_rows = math.gcd(TOKENS, 512)
    block_count = TOKENS // block_rows
    score_scale = HEAD_DIM ** (-0.5)
    key_float = rot_k.astype(jnp.float32)
    value_float = value_rows.astype(jnp.float32)
    key_positions = jnp.arange(TOKENS, dtype=jnp.int32)

    def attend(block_index):
        row_start = (block_index * block_rows).astype(jnp.int32)
        query_block = lax.dynamic_slice_in_dim(rot_q, row_start, block_rows, 0).astype(jnp.float32)
        query_positions = row_start + jnp.arange(block_rows, dtype=jnp.int32)
        allowed = key_positions[None, :] <= query_positions[:, None]
        outputs = []
        for kv_head in range(KV_HEADS):
            query_part = query_block[:, kv_head * group_size:(kv_head + 1) * group_size, :]
            scores = jnp.einsum('bhd,ud->hbu', query_part, key_float[:, kv_head, :], precision=lax.Precision.HIGHEST) * score_scale
            scores = jnp.where(allowed[None], scores, -jnp.inf)
            row_max = lax.optimization_barrier(jnp.max(scores, axis=-1, keepdims=True))
            expw = jnp.exp(scores - row_max)
            weight_sum = lax.optimization_barrier(jnp.sum(expw, axis=-1))
            probs = expw.astype(jnp.bfloat16).astype(jnp.float32)
            mixed = jnp.einsum('hbu,ud->bhd', probs, value_float[:, kv_head, :], precision=lax.Precision.HIGHEST)
            outputs.append(mixed / jnp.transpose(weight_sum)[:, :, None])
        return jnp.concatenate(outputs, axis=1).reshape(block_rows, HEADS * HEAD_DIM).astype(jnp.bfloat16)
    attended = lax.map(attend, jnp.arange(block_count, dtype=jnp.int32)).reshape(TOKENS, HEADS * HEAD_DIM)
    residual = tokens.astype(jnp.float32) + jnp.dot(attended, w_out, preferred_element_type=jnp.float32)
    routed = rms_scale(residual, post_gain).astype(jnp.bfloat16)
    mixing = route_weights / lax.optimization_barrier(jnp.sum(route_weights, axis=-1, keepdims=True))
    part_count = TOKENS // ROWS
    grouped_ids = expert_ids.reshape(part_count, ROWS * TOPK)
    onehot = (grouped_ids[..., None] == jnp.arange(EXPERTS, dtype=jnp.int32)[None, None, :]).astype(jnp.int32)
    rank_table = jnp.cumsum(onehot, axis=1) - onehot
    slot_index = lax.optimization_barrier(jnp.sum(rank_table * onehot, axis=-1))
    slot_place = (jnp.arange(part_count, dtype=jnp.int32)[:, None] * CAP + slot_index).reshape(-1).astype(jnp.int32)
    flat_experts = expert_ids.reshape(-1).astype(jnp.int32)
    copy_index = jnp.arange(TOKENS * TOPK, dtype=jnp.int32)
    copy_table = jnp.full((EXPERTS, part_count * CAP), TOKENS * TOPK, jnp.int32).at[flat_experts, slot_place].set(copy_index)
    padded_rows = jnp.concatenate([routed, jnp.zeros((1, D), jnp.bfloat16)], axis=0)
    mix_flat = jnp.concatenate([mixing.reshape(-1), jnp.zeros((1,), jnp.float32)])

    def run_expert(combined, inputs):
        copy_ids, gate_weight, up_weight, down_weight = inputs
        token_ids = copy_ids // TOPK
        rows_in = padded_rows[token_ids].astype(jnp.float32)
        gate_proj = jnp.dot(rows_in, gate_weight.astype(jnp.float32), precision=lax.Precision.HIGHEST)
        up_proj = jnp.dot(rows_in, up_weight.astype(jnp.float32), precision=lax.Precision.HIGHEST)
        hidden = (jax.nn.silu(gate_proj) * up_proj).astype(jnp.bfloat16).astype(jnp.float32)
        expert_rows = jnp.dot(hidden, down_weight.astype(jnp.float32), precision=lax.Precision.HIGHEST).astype(jnp.bfloat16)
        weighted = expert_rows.astype(jnp.float32) * mix_flat[copy_ids][:, None]
        return (combined.at[token_ids].add(weighted), None)
    combined, _ = lax.scan(run_expert, jnp.zeros((TOKENS + 1, D), jnp.float32), (copy_table, w_gate, w_up, w_down))
    return (residual + combined[:TOKENS]).astype(jnp.bfloat16)
```

```python
import functools

import jax
import jax.numpy as jnp
from jax import lax
from jax.experimental import pallas as pl
from jax.experimental.pallas import tpu as pltpu
from jax.sharding import PartitionSpec as P

EPSILON = 1e-06
THETA = 1000000.0
NEGATIVE = -1e30
LOG2E = 1.4426950408889634
BOTH = ("seq", "head")
VMEM = pl.BlockSpec(memory_space=pltpu.VMEM)


def rms_scale(vectors, gain_vector):
    mean_sq = jnp.mean(vectors * vectors, axis=-1, keepdims=True)
    return vectors * lax.rsqrt(mean_sq + EPSILON) * gain_vector


def turn(vectors, cos_ref, sin_ref):
    half = vectors.shape[-1] // 2
    return vectors * cos_ref[...] + pltpu.roll(vectors, half, 1) * sin_ref[...]


def first_kernel(x_ref, gain_ref, wk_ref, wv_ref, kgain_ref, cos_ref, sin_ref, normed_ref, kv_ref):
    head_dim = wk_ref.shape[1]
    normed = rms_scale(x_ref[...].astype(jnp.float32), gain_ref[...]).astype(jnp.bfloat16)
    normed_ref[...] = normed
    keys = jnp.dot(normed, wk_ref[...], preferred_element_type=jnp.float32)
    keys = turn(rms_scale(keys, kgain_ref[...]), cos_ref, sin_ref)
    kv_ref[:, :head_dim] = keys.astype(jnp.bfloat16)
    values = jnp.dot(normed, wv_ref[...], preferred_element_type=jnp.float32)
    kv_ref[:, head_dim:] = values.astype(jnp.bfloat16)


def query_kernel(head_dim, normed_ref, wq_ref, qgain_ref, cos_ref, sin_ref, q_ref):
    wide = jnp.dot(normed_ref[...], wq_ref[...], preferred_element_type=jnp.float32)
    for i in range(wide.shape[1] // head_dim):
        part = slice(i * head_dim, (i + 1) * head_dim)
        q_ref[:, part] = turn(rms_scale(wide[:, part], qgain_ref[...]), cos_ref, sin_ref).astype(
            jnp.bfloat16
        )


def attend_kernel(head_dim, blocks, bias_ref, q_ref, *rest):
    kv_refs, out_ref, s_ref = rest[:blocks], rest[blocks], rest[blocks + 1]
    rows = q_ref.shape[0]
    queries = q_ref[...]
    top = None
    for j, kv in enumerate(kv_refs):
        raw = lax.dot_general(
            queries,
            kv[:, :head_dim],
            (((1,), (1,)), ((), ())),
            preferred_element_type=jnp.float32,
        )
        if j == 0:
            row = lax.broadcasted_iota(jnp.int32, raw.shape, 0)
            col = lax.broadcasted_iota(jnp.int32, raw.shape, 1)
            raw = jnp.where(col <= row, raw, NEGATIVE)
        else:
            raw = raw + bias_ref[j]
        s_ref[:, j * rows : (j + 1) * rows] = raw
        top = raw if top is None else jnp.maximum(top, raw)
    row_max = jnp.max(top, axis=1, keepdims=True)
    scale = head_dim ** (-0.5) * LOG2E
    total = jnp.zeros((rows, rows), jnp.float32)
    mixed = jnp.zeros((rows, head_dim), jnp.float32)
    for j, kv in enumerate(kv_refs):
        weights = jnp.exp2((s_ref[:, j * rows : (j + 1) * rows] - row_max) * scale)
        total = total + weights
        mixed = mixed + jnp.dot(
            weights.astype(jnp.bfloat16), kv[:, head_dim:], preferred_element_type=jnp.float32
        )
    out_ref[...] = (mixed / jnp.sum(total, axis=1, keepdims=True)).astype(jnp.bfloat16)


def pairs(seq_count, head_count, step):
    made = []
    for s in range(seq_count):
        for h in range(head_count):
            to = step(s, h)
            if to is not None:
                made.append((s * head_count + h, to[0] * head_count + to[1]))
    return made


def split_exact(values):
    high = values.astype(jnp.bfloat16)
    low = (values - high.astype(jnp.float32)).astype(jnp.bfloat16)
    return high, low


def body(
    tokens,
    input_gain,
    w_query,
    w_key,
    w_value,
    query_gain,
    key_gain,
    w_out,
    post_gain,
    expert_ids,
    route_weights,
    w_gate,
    w_up,
    w_down,
):
    tok_rows, width = tokens.shape
    head_dim = query_gain.shape[0]
    heads_here = w_query.shape[1] // head_dim
    seq_count = lax.axis_size("seq")
    seq_index = lax.axis_index("seq")
    head_count = lax.axis_size("head")
    head_index = lax.axis_index("head")
    side = 2 if seq_count % 2 == 0 else 1
    line = seq_count // side
    cores = 2 if head_count % 2 == 0 else 1
    towers = head_count // cores
    line_index, side_index = seq_index // side, seq_index % side
    tower_index, core_index = head_index // cores, head_index % cores
    make_pairs = functools.partial(pairs, seq_count, head_count)

    half_dim = head_dim // 2
    offset = seq_index * tok_rows
    positions = (offset + jnp.arange(tok_rows, dtype=jnp.int32)).astype(jnp.float32)
    frequency = THETA ** (-jnp.arange(half_dim, dtype=jnp.float32) * 2.0 / head_dim)
    angles = positions[:, None] * frequency[None, :]
    cosine, sine = jnp.cos(angles), jnp.sin(angles)
    cos_table = jnp.concatenate([cosine, cosine], axis=1)
    sin_table = jnp.concatenate([-sine, sine], axis=1)

    normed, own_kv = pl.pallas_call(
        first_kernel,
        out_shape=(
            jax.ShapeDtypeStruct((tok_rows, width), jnp.bfloat16),
            jax.ShapeDtypeStruct((tok_rows, 2 * head_dim), jnp.bfloat16),
        ),
        in_specs=[VMEM] * 7,
        out_specs=(VMEM, VMEM),
        name="norm_kv",
    )(tokens, input_gain[None], w_key, w_value, key_gain[None], cos_table, sin_table)

    kv_blocks, kv_bias = [own_kv], [jnp.float32(0.0)]
    for k in range(1, line):
        up = make_pairs(
            lambda s, h, k=k: (s + k * side, h) if s + k * side < seq_count else None
        )
        kv_blocks.append(lax.ppermute(own_kv, BOTH, up))
        kv_bias.append(jnp.where(line_index >= k, 0.0, NEGATIVE))
    if side == 2:
        swap = make_pairs(lambda s, h: (s ^ 1, h))
        for k in range(line):
            kv_blocks.append(lax.ppermute(kv_blocks[k], BOTH, swap))
            seen = line_index >= k if k else side_index == 1
            kv_bias.append(jnp.where(seen, 0.0, NEGATIVE))

    query_step = 2 * head_dim if heads_here % 2 == 0 else head_dim
    rot_q = pl.pallas_call(
        functools.partial(query_kernel, head_dim),
        grid=(w_query.shape[1] // query_step,),
        out_shape=jax.ShapeDtypeStruct((tok_rows, w_query.shape[1]), jnp.bfloat16),
        in_specs=[
            pl.BlockSpec((tok_rows, width), lambda i: (0, 0)),
            pl.BlockSpec((width, query_step), lambda i: (0, i)),
            pl.BlockSpec((1, head_dim), lambda i: (0, 0)),
            pl.BlockSpec((tok_rows, head_dim), lambda i: (0, 0)),
            pl.BlockSpec((tok_rows, head_dim), lambda i: (0, 0)),
        ],
        out_specs=pl.BlockSpec((tok_rows, query_step), lambda i: (0, i)),
        name="queries",
    )(normed, w_query, query_gain[None], cos_table, sin_table)

    blocks = len(kv_blocks)
    attended = pl.pallas_call(
        functools.partial(attend_kernel, head_dim, blocks),
        grid=(heads_here,),
        out_shape=jax.ShapeDtypeStruct((tok_rows, heads_here * head_dim), jnp.bfloat16),
        in_specs=[
            pl.BlockSpec(memory_space=pltpu.SMEM),
            pl.BlockSpec((tok_rows, head_dim), lambda i: (0, i)),
        ]
        + [pl.BlockSpec((tok_rows, 2 * head_dim), lambda i: (0, 0))] * blocks,
        out_specs=pl.BlockSpec((tok_rows, head_dim), lambda i: (0, i)),
        scratch_shapes=[pltpu.VMEM((tok_rows, blocks * tok_rows), jnp.float32)],
        name="attend",
    )(jnp.stack(kv_bias), rot_q, *kv_blocks)

    rows_here = tok_rows // head_count
    partial_out = jnp.dot(attended, w_out, preferred_element_type=jnp.float32).reshape(
        towers, cores, rows_here, width
    )
    if cores == 2:
        keep = lax.dynamic_index_in_dim(partial_out, core_index, 1, keepdims=False)
        give = lax.dynamic_index_in_dim(partial_out, 1 - core_index, 1, keepdims=False)
        swap = make_pairs(lambda s, h: (s, h ^ 1))
        came = lax.ppermute(give.astype(jnp.bfloat16), BOTH, swap)
        tower_sums = keep + came.astype(jnp.float32)
    else:
        tower_sums = partial_out[:, 0]
    attn_part = lax.dynamic_index_in_dim(tower_sums, tower_index, 0, keepdims=False)
    for k in range(1, towers):
        give = lax.dynamic_index_in_dim(
            tower_sums, (tower_index + k) % towers, 0, keepdims=False
        ).astype(jnp.bfloat16)
        shift = make_pairs(lambda s, h, k=k: (s, (h + k * cores) % head_count))
        attn_part = attn_part + lax.ppermute(give, BOTH, shift).astype(jnp.float32)

    own_rows = lax.dynamic_slice_in_dim(tokens, head_index * rows_here, rows_here, 0)
    residual = own_rows.astype(jnp.float32) + attn_part
    routed = rms_scale(residual, post_gain).astype(jnp.bfloat16)

    local_count = w_gate.shape[0]
    experts_all = local_count * seq_count * head_count
    top_count = expert_ids.shape[1]
    copies = rows_here * top_count
    capacity = max(2, 3 * rows_here * top_count // (2 * experts_all))
    named = expert_ids[:, :, None] == jnp.arange(experts_all, dtype=jnp.int32)[None, None, :]
    counts = jnp.sum(named, axis=1).astype(jnp.bfloat16)
    earlier = (
        jnp.arange(rows_here)[:, None] > jnp.arange(rows_here)[None, :]
    ).astype(jnp.bfloat16)
    rank_table = jnp.dot(earlier, counts, preferred_element_type=jnp.float32)
    mixing = route_weights / jnp.sum(route_weights, axis=1, keepdims=True)
    mix_table = jnp.sum(jnp.where(named, mixing[:, :, None], 0.0), axis=1)
    place = jnp.where(counts > 0, rank_table, -1.0).astype(jnp.int32)
    in_slot = place[:, :, None] == jnp.arange(capacity, dtype=jnp.int32)[None, None, :]
    slots = experts_all * capacity
    pick = in_slot.astype(jnp.bfloat16).reshape(rows_here, slots)
    mix_slots = jnp.where(in_slot, mix_table[:, :, None], 0.0).reshape(rows_here, slots)
    mix_high, mix_low = split_exact(mix_slots)

    outgoing = lax.dot_general(
        pick, routed, (((0,), (0,)), ((), ())), preferred_element_type=jnp.float32
    ).astype(jnp.bfloat16)
    outgoing = outgoing.reshape(experts_all, capacity, width)
    slot_batch = lax.all_to_all(outgoing, BOTH, split_axis=0, concat_axis=0, tiled=True)
    sources = experts_all // local_count
    grouped = (
        slot_batch.reshape(sources, local_count, capacity, width)
        .transpose(1, 0, 2, 3)
        .reshape(local_count, sources * capacity, width)
    )
    gate_proj = jnp.einsum("erd,edf->erf", grouped, w_gate, preferred_element_type=jnp.float32)
    up_proj = jnp.einsum("erd,edf->erf", grouped, w_up, preferred_element_type=jnp.float32)
    hidden = (jax.nn.silu(gate_proj) * up_proj).astype(jnp.bfloat16)
    result = jnp.einsum("erf,efd->erd", hidden, w_down, preferred_element_type=jnp.float32).astype(
        jnp.bfloat16
    )
    returned = lax.all_to_all(
        result.reshape(local_count, sources, capacity, width)
        .transpose(1, 0, 2, 3)
        .reshape(experts_all, capacity, width),
        BOTH,
        split_axis=0,
        concat_axis=0,
        tiled=True,
    ).reshape(slots, width)
    both = jnp.dot(
        jnp.concatenate([mix_high, mix_low], axis=0), returned, preferred_element_type=jnp.float32
    )
    expert_sum = both[:rows_here] + both[rows_here:]
    return (residual + expert_sum).astype(jnp.bfloat16)


def solution(mesh):
    placed = (
        P("seq", None),
        P(),
        P(None, "head"),
        P(None, "head"),
        P(None, "head"),
        P(),
        P(),
        P("head", None),
        P(),
        P(("seq", "head"), None),
        P(("seq", "head"), None),
        P(("seq", "head"), None, None),
        P(("seq", "head"), None, None),
        P(("seq", "head"), None, None),
    )
    return jax.shard_map(
        body, mesh=mesh, in_specs=placed, out_specs=P(("seq", "head"), None), check_vma=False
    )
```

```python
import functools

import jax
import jax.numpy as jnp
from jax import lax
from jax.experimental import pallas as pl
from jax.experimental.pallas import tpu as pltpu
from jax.sharding import PartitionSpec as P

EPSILON = 1e-06
THETA = 1000000.0
NEGATIVE = -1e30
LOG2E = 1.4426950408889634
BOTH = ("seq", "head")
VMEM = pl.BlockSpec(memory_space=pltpu.VMEM)


def rms_scale(vectors, gain_vector):
    mean_sq = jnp.mean(vectors * vectors, axis=-1, keepdims=True)
    return vectors * lax.rsqrt(mean_sq + EPSILON) * gain_vector


def turn(vectors, cos_ref, sin_ref):
    half = vectors.shape[-1] // 2
    return vectors * cos_ref[...] + pltpu.roll(vectors, half, 1) * sin_ref[...]


def first_kernel(x_ref, gain_ref, wk_ref, wv_ref, kgain_ref, cos_ref, sin_ref, normed_ref, kv_ref):
    head_dim = wk_ref.shape[1]
    normed = rms_scale(x_ref[...].astype(jnp.float32), gain_ref[...]).astype(jnp.bfloat16)
    normed_ref[...] = normed
    keys = jnp.dot(normed, wk_ref[...], preferred_element_type=jnp.float32)
    keys = turn(rms_scale(keys, kgain_ref[...]), cos_ref, sin_ref)
    kv_ref[:, :head_dim] = keys.astype(jnp.bfloat16)
    values = jnp.dot(normed, wv_ref[...], preferred_element_type=jnp.float32)
    kv_ref[:, head_dim:] = values.astype(jnp.bfloat16)


def query_kernel(head_dim, normed_ref, wq_ref, qgain_ref, cos_ref, sin_ref, q_ref):
    wide = jnp.dot(normed_ref[...], wq_ref[...], preferred_element_type=jnp.float32)
    for i in range(wide.shape[1] // head_dim):
        part = slice(i * head_dim, (i + 1) * head_dim)
        q_ref[:, part] = turn(rms_scale(wide[:, part], qgain_ref[...]), cos_ref, sin_ref).astype(
            jnp.bfloat16
        )


def attend_kernel(head_dim, blocks, bias_ref, q_ref, *rest):
    kv_refs, out_ref, s_ref = rest[:blocks], rest[blocks], rest[blocks + 1]
    rows = q_ref.shape[0]
    queries = q_ref[...]
    top = None
    for j, kv in enumerate(kv_refs):
        raw = lax.dot_general(
            queries,
            kv[:, :head_dim],
            (((1,), (1,)), ((), ())),
            preferred_element_type=jnp.float32,
        )
        if j == 0:
            row = lax.broadcasted_iota(jnp.int32, raw.shape, 0)
            col = lax.broadcasted_iota(jnp.int32, raw.shape, 1)
            raw = jnp.where(col <= row, raw, NEGATIVE)
        else:
            raw = raw + bias_ref[j]
        s_ref[:, j * rows : (j + 1) * rows] = raw
        top = raw if top is None else jnp.maximum(top, raw)
    row_max = jnp.max(top, axis=1, keepdims=True)
    scale = head_dim ** (-0.5) * LOG2E
    total = jnp.zeros((rows, rows), jnp.float32)
    mixed = jnp.zeros((rows, head_dim), jnp.float32)
    for j, kv in enumerate(kv_refs):
        weights = jnp.exp2((s_ref[:, j * rows : (j + 1) * rows] - row_max) * scale)
        total = total + weights
        mixed = mixed + jnp.dot(
            weights.astype(jnp.bfloat16), kv[:, head_dim:], preferred_element_type=jnp.float32
        )
    out_ref[...] = (mixed / jnp.sum(total, axis=1, keepdims=True)).astype(jnp.bfloat16)


def expert_kernel(count, up_steps, *refs):
    rows_refs, (wg_ref, wu_ref, wd_ref), out_refs = refs[:count], refs[count : count + 3], refs[count + 3 : -1]
    hidden_ref = refs[-1]
    step = pl.program_id(1)
    rows = rows_refs[0].shape[0]

    for now in range(up_steps):

        @pl.when(step == now)
        def _():
            part = wg_ref.shape[1]
            for i, ref in enumerate(rows_refs):
                gate = jnp.dot(ref[...], wg_ref[...], preferred_element_type=jnp.float32)
                up = jnp.dot(ref[...], wu_ref[...], preferred_element_type=jnp.float32)
                hidden = (gate / (1.0 + jnp.exp(-gate))) * up
                hidden_ref[i * rows : (i + 1) * rows, now * part : (now + 1) * part] = hidden.astype(
                    jnp.bfloat16
                )

    @pl.when(step >= up_steps)
    def _():
        for i, ref in enumerate(out_refs):
            ref[...] = jnp.dot(
                hidden_ref[i * rows : (i + 1) * rows, :],
                wd_ref[...],
                preferred_element_type=jnp.float32,
            ).astype(jnp.bfloat16)


def run_experts(arrived, w_gate, w_up, w_down):
    count = len(arrived)
    experts, rows, width = arrived[0].shape
    ff = w_gate.shape[2]
    part = ff // 3 if ff % 384 == 0 else ff
    out_part = width // 4 if width % 512 == 0 else width
    up_steps, down_steps = ff // part, width // out_part
    return pl.pallas_call(
        functools.partial(expert_kernel, count, up_steps),
        grid=(experts, up_steps + down_steps),
        out_shape=[jax.ShapeDtypeStruct((experts, rows, width), jnp.bfloat16)] * count,
        in_specs=[pl.BlockSpec((None, rows, width), lambda e, i: (e, 0, 0))] * count
        + [pl.BlockSpec((None, width, part), lambda e, i: (e, 0, jnp.minimum(i, up_steps - 1)))] * 2
        + [pl.BlockSpec((None, ff, out_part), lambda e, i: (e, 0, jnp.maximum(i - up_steps, 0)))],
        out_specs=[
            pl.BlockSpec((None, rows, out_part), lambda e, i: (e, 0, jnp.maximum(i - up_steps, 0)))
        ]
        * count,
        scratch_shapes=[pltpu.VMEM((count * rows, ff), jnp.bfloat16)],
        name="experts",
    )(*arrived, w_gate, w_up, w_down)


def pairs(seq_count, head_count, step):
    made = []
    for s in range(seq_count):
        for h in range(head_count):
            to = step(s, h)
            if to is not None:
                made.append((s * head_count + h, to[0] * head_count + to[1]))
    return made


def split_exact(values):
    high = values.astype(jnp.bfloat16)
    low = (values - high.astype(jnp.float32)).astype(jnp.bfloat16)
    return high, low


def body(
    tokens,
    input_gain,
    w_query,
    w_key,
    w_value,
    query_gain,
    key_gain,
    w_out,
    post_gain,
    expert_ids,
    route_weights,
    w_gate,
    w_up,
    w_down,
):
    tok_rows, width = tokens.shape
    head_dim = query_gain.shape[0]
    heads_here = w_query.shape[1] // head_dim
    seq_count = lax.axis_size("seq")
    seq_index = lax.axis_index("seq")
    head_count = lax.axis_size("head")
    head_index = lax.axis_index("head")
    side = 2 if seq_count % 2 == 0 else 1
    line = seq_count // side
    cores = 2 if head_count % 2 == 0 else 1
    towers = head_count // cores
    line_index, side_index = seq_index // side, seq_index % side
    tower_index, core_index = head_index // cores, head_index % cores
    make_pairs = functools.partial(pairs, seq_count, head_count)

    half_dim = head_dim // 2
    offset = seq_index * tok_rows
    positions = (offset + jnp.arange(tok_rows, dtype=jnp.int32)).astype(jnp.float32)
    frequency = THETA ** (-jnp.arange(half_dim, dtype=jnp.float32) * 2.0 / head_dim)
    angles = positions[:, None] * frequency[None, :]
    cosine, sine = jnp.cos(angles), jnp.sin(angles)
    cos_table = jnp.concatenate([cosine, cosine], axis=1)
    sin_table = jnp.concatenate([-sine, sine], axis=1)

    normed, own_kv = pl.pallas_call(
        first_kernel,
        out_shape=(
            jax.ShapeDtypeStruct((tok_rows, width), jnp.bfloat16),
            jax.ShapeDtypeStruct((tok_rows, 2 * head_dim), jnp.bfloat16),
        ),
        in_specs=[VMEM] * 7,
        out_specs=(VMEM, VMEM),
        name="norm_kv",
    )(tokens, input_gain[None], w_key, w_value, key_gain[None], cos_table, sin_table)

    kv_blocks, kv_bias = [own_kv], [jnp.float32(0.0)]
    for k in range(1, line):
        up = make_pairs(
            lambda s, h, k=k: (s + k * side, h) if s + k * side < seq_count else None
        )
        kv_blocks.append(lax.ppermute(own_kv, BOTH, up))
        kv_bias.append(jnp.where(line_index >= k, 0.0, NEGATIVE))
    if side == 2:
        swap = make_pairs(lambda s, h: (s ^ 1, h))
        for k in range(line):
            kv_blocks.append(lax.ppermute(kv_blocks[k], BOTH, swap))
            seen = line_index >= k if k else side_index == 1
            kv_bias.append(jnp.where(seen, 0.0, NEGATIVE))

    query_step = 2 * head_dim if heads_here % 2 == 0 else head_dim
    rot_q = pl.pallas_call(
        functools.partial(query_kernel, head_dim),
        grid=(w_query.shape[1] // query_step,),
        out_shape=jax.ShapeDtypeStruct((tok_rows, w_query.shape[1]), jnp.bfloat16),
        in_specs=[
            pl.BlockSpec((tok_rows, width), lambda i: (0, 0)),
            pl.BlockSpec((width, query_step), lambda i: (0, i)),
            pl.BlockSpec((1, head_dim), lambda i: (0, 0)),
            pl.BlockSpec((tok_rows, head_dim), lambda i: (0, 0)),
            pl.BlockSpec((tok_rows, head_dim), lambda i: (0, 0)),
        ],
        out_specs=pl.BlockSpec((tok_rows, query_step), lambda i: (0, i)),
        name="queries",
    )(normed, w_query, query_gain[None], cos_table, sin_table)

    blocks = len(kv_blocks)
    attended = pl.pallas_call(
        functools.partial(attend_kernel, head_dim, blocks),
        grid=(heads_here,),
        out_shape=jax.ShapeDtypeStruct((tok_rows, heads_here * head_dim), jnp.bfloat16),
        in_specs=[
            pl.BlockSpec(memory_space=pltpu.SMEM),
            pl.BlockSpec((tok_rows, head_dim), lambda i: (0, i)),
        ]
        + [pl.BlockSpec((tok_rows, 2 * head_dim), lambda i: (0, 0))] * blocks,
        out_specs=pl.BlockSpec((tok_rows, head_dim), lambda i: (0, i)),
        scratch_shapes=[pltpu.VMEM((tok_rows, blocks * tok_rows), jnp.float32)],
        name="attend",
    )(jnp.stack(kv_bias), rot_q, *kv_blocks)

    rows_here = tok_rows // head_count
    partial_out = jnp.dot(attended, w_out, preferred_element_type=jnp.float32).reshape(
        towers, cores, rows_here, width
    )
    if cores == 2:
        keep = lax.dynamic_index_in_dim(partial_out, core_index, 1, keepdims=False)
        give = lax.dynamic_index_in_dim(partial_out, 1 - core_index, 1, keepdims=False)
        swap = make_pairs(lambda s, h: (s, h ^ 1))
        came = lax.ppermute(give.astype(jnp.bfloat16), BOTH, swap)
        tower_sums = keep + came.astype(jnp.float32)
    else:
        tower_sums = partial_out[:, 0]
    attn_part = lax.dynamic_index_in_dim(tower_sums, tower_index, 0, keepdims=False)
    for k in range(1, towers):
        give = lax.dynamic_index_in_dim(
            tower_sums, (tower_index + k) % towers, 0, keepdims=False
        ).astype(jnp.bfloat16)
        shift = make_pairs(lambda s, h, k=k: (s, (h + k * cores) % head_count))
        attn_part = attn_part + lax.ppermute(give, BOTH, shift).astype(jnp.float32)

    own_rows = lax.dynamic_slice_in_dim(tokens, head_index * rows_here, rows_here, 0)
    residual = own_rows.astype(jnp.float32) + attn_part
    routed = rms_scale(residual, post_gain).astype(jnp.bfloat16)

    top_count = expert_ids.shape[1]
    halves = 2 if line % 2 == 0 else 1
    local_count = w_gate.shape[0]
    experts_all = local_count * seq_count * head_count
    experts_half = experts_all // halves
    members = seq_count * head_count // halves
    capacity = max(2, 3 * rows_here * top_count // (2 * experts_all))
    slots = experts_half * capacity
    first_expert = (seq_index // (seq_count // halves)) * experts_half
    mirror = make_pairs(lambda s, h: ((line - 1 - s // side) * side + s % side, h))
    mixing = route_weights / jnp.sum(route_weights, axis=1, keepdims=True)
    routes = [(expert_ids, mixing)]
    if halves == 2:
        sent = jnp.concatenate([expert_ids.astype(jnp.float32), mixing], axis=1)
        seen = lax.ppermute(sent, BOTH, mirror)
        routes.append((seen[:, :top_count].astype(jnp.int32), seen[:, top_count:]))

    def slot_tables(ids, weights):
        here = first_expert + jnp.arange(experts_half, dtype=jnp.int32)
        named = ids[:, :, None] == here[None, None, :]
        counts = jnp.sum(named, axis=1).astype(jnp.bfloat16)
        earlier = (
            jnp.arange(rows_here)[:, None] > jnp.arange(rows_here)[None, :]
        ).astype(jnp.bfloat16)
        rank_table = jnp.dot(earlier, counts, preferred_element_type=jnp.float32)
        mix_table = jnp.sum(jnp.where(named, weights[:, :, None], 0.0), axis=1)
        place = jnp.where(counts > 0, rank_table, -1.0).astype(jnp.int32)
        in_slot = place[:, :, None] == jnp.arange(capacity, dtype=jnp.int32)[None, None, :]
        pick = in_slot.astype(jnp.bfloat16).reshape(rows_here, slots)
        mix = jnp.where(in_slot, mix_table[:, :, None], 0.0).reshape(rows_here, slots)
        return pick, jnp.concatenate(split_exact(mix), axis=0)

    tables = [slot_tables(*route) for route in routes]
    groups = [list(range(g * members, (g + 1) * members)) for g in range(halves)]

    def exchange(rows):
        return lax.all_to_all(
            rows.reshape(members, local_count * capacity, width),
            BOTH,
            split_axis=0,
            concat_axis=0,
            axis_index_groups=groups,
            tiled=True,
        )

    def dispatch(rows, pick):
        outgoing = lax.dot_general(
            pick, rows, (((0,), (0,)), ((), ())), preferred_element_type=jnp.float32
        ).astype(jnp.bfloat16)
        return (
            exchange(outgoing)
            .reshape(members, local_count, capacity, width)
            .transpose(1, 0, 2, 3)
            .reshape(local_count, members * capacity, width)
        )

    def give_back(result, mix):
        came = exchange(
            result.reshape(local_count, members, capacity, width).transpose(1, 0, 2, 3)
        ).reshape(slots, width)
        both = jnp.dot(mix, came, preferred_element_type=jnp.float32)
        return both[:rows_here] + both[rows_here:]

    arrived = []
    if halves == 2:
        mirrored = lax.ppermute(routed, BOTH, mirror)
    arrived.append(dispatch(routed, tables[0][0]))
    if halves == 2:
        mirrored, _ = lax.optimization_barrier((mirrored, arrived[0]))
        arrived.append(dispatch(mirrored, tables[1][0]))
    results = run_experts(arrived, w_gate, w_up, w_down)
    if halves == 2:
        foreign = give_back(results[1], tables[1][1]).astype(jnp.bfloat16)
        far_sum = lax.ppermute(foreign, BOTH, mirror)
        own_result, foreign = lax.optimization_barrier((results[0], foreign))
        expert_sum = give_back(own_result, tables[0][1]) + far_sum.astype(jnp.float32)
    else:
        expert_sum = give_back(results[0], tables[0][1])
    return (residual + expert_sum).astype(jnp.bfloat16)


def solution(mesh):
    placed = (
        P("seq", None),
        P(),
        P(None, "head"),
        P(None, "head"),
        P(None, "head"),
        P(),
        P(),
        P("head", None),
        P(),
        P(("seq", "head"), None),
        P(("seq", "head"), None),
        P(("seq", "head"), None, None),
        P(("seq", "head"), None, None),
        P(("seq", "head"), None, None),
    )
    return jax.shard_map(
        body, mesh=mesh, in_specs=placed, out_specs=P(("seq", "head"), None), check_vma=False
    )
```

```python
import functools

import jax
import jax.numpy as jnp
from jax import lax
from jax.experimental import pallas as pl
from jax.experimental.pallas import tpu as pltpu
from jax.sharding import PartitionSpec as P


EPSILON = 1e-06
THETA = 1000000.0
NEGATIVE = -1e30
LOG2E = 1.4426950408889634
BOTH = ("seq", "head")
VMEM = pl.BlockSpec(memory_space=pltpu.VMEM)


def rms_scale(vectors, gain_vector):
    mean_sq = jnp.mean(vectors * vectors, axis=-1, keepdims=True)
    return vectors * lax.rsqrt(mean_sq + EPSILON) * gain_vector


def turn(vectors, cos_ref, sin_ref):
    half = vectors.shape[-1] // 2
    return vectors * cos_ref[...] + pltpu.roll(vectors, half, 1) * sin_ref[...]


def first_kernel(x_ref, gain_ref, wk_ref, wv_ref, kgain_ref, cos_ref, sin_ref, normed_ref, kv_ref):
    head_dim = wk_ref.shape[1]
    normed = rms_scale(x_ref[...].astype(jnp.float32), gain_ref[...]).astype(jnp.bfloat16)
    normed_ref[...] = normed
    keys = jnp.dot(normed, wk_ref[...], preferred_element_type=jnp.float32)
    keys = turn(rms_scale(keys, kgain_ref[...]), cos_ref, sin_ref)
    kv_ref[:, :head_dim] = keys.astype(jnp.bfloat16)
    values = jnp.dot(normed, wv_ref[...], preferred_element_type=jnp.float32)
    kv_ref[:, head_dim:] = values.astype(jnp.bfloat16)


def query_kernel(head_dim, normed_ref, wq_ref, qgain_ref, cos_ref, sin_ref, q_ref):
    wide = jnp.dot(normed_ref[...], wq_ref[...], preferred_element_type=jnp.float32)
    for i in range(wide.shape[1] // head_dim):
        part = slice(i * head_dim, (i + 1) * head_dim)
        q_ref[:, part] = turn(rms_scale(wide[:, part], qgain_ref[...]), cos_ref, sin_ref).astype(
            jnp.bfloat16
        )


def attend_kernel(head_dim, blocks, first, last, bias_ref, q_ref, *rest):
    kv_refs, rest = rest[:blocks], rest[blocks:]
    s_ref = rest[-1]
    rows = q_ref.shape[0]
    queries = q_ref[...]
    scale = head_dim ** (-0.5) * LOG2E
    tops = []
    for j, kv in enumerate(kv_refs):
        raw = lax.dot_general(
            queries,
            kv[:, :head_dim],
            (((1,), (1,)), ((), ())),
            preferred_element_type=jnp.float32,
        )
        if first and j == 0:
            row = lax.broadcasted_iota(jnp.int32, raw.shape, 0)
            col = lax.broadcasted_iota(jnp.int32, raw.shape, 1)
            raw = jnp.where(col <= row, raw, NEGATIVE)
        s_ref[:, j * rows : (j + 1) * rows] = raw
        top = raw[:, :head_dim]
        for i in range(1, rows // head_dim):
            top = jnp.maximum(top, raw[:, i * head_dim : (i + 1) * head_dim])
        tops.append(top + bias_ref[j])
    if first:
        total = jnp.zeros((rows, 1), jnp.float32)
        mixed = jnp.zeros((rows, head_dim), jnp.float32)
    else:
        stat_in, mixed_in = rest[0], rest[1]
        rest = rest[2:]
        old_max, old_total = stat_in[:, 0:1], stat_in[:, 1:2]
        tops.append(jnp.broadcast_to(old_max, tops[0].shape))
    row_max = jnp.max(functools.reduce(jnp.maximum, tops), axis=1, keepdims=True)
    if not first:
        shrink = jnp.exp2((old_max - row_max) * scale)
        total = old_total * shrink
        mixed = mixed_in[...] * shrink
    sums = jnp.zeros((rows, head_dim), jnp.float32)
    for j, kv in enumerate(kv_refs):
        floor = row_max - bias_ref[j]
        weights = jnp.exp2((s_ref[:, j * rows : (j + 1) * rows] - floor) * scale)
        for i in range(rows // head_dim):
            sums = sums + weights[:, i * head_dim : (i + 1) * head_dim]
        mixed = mixed + jnp.dot(
            weights.astype(jnp.bfloat16), kv[:, head_dim:], preferred_element_type=jnp.float32
        )
    total = total + jnp.sum(sums, axis=1, keepdims=True)
    if last:
        rest[0][...] = (mixed / total).astype(jnp.bfloat16)
    else:
        lane = lax.broadcasted_iota(jnp.int32, (rows, head_dim), 1)
        rest[0][...] = jnp.where(lane == 0, row_max, total)
        rest[1][...] = mixed


def attend(rot_q, head_dim, kv_blocks, bias, state, last):
    rows, wide = rot_q.shape
    blocks = len(kv_blocks)
    column = pl.BlockSpec((rows, head_dim), lambda i: (0, i))
    if last:
        out_shape, out_specs = jax.ShapeDtypeStruct((rows, wide), jnp.bfloat16), column
    else:
        out_shape = (jax.ShapeDtypeStruct((rows, wide), jnp.float32),) * 2
        out_specs = (column, column)
    return pl.pallas_call(
        functools.partial(attend_kernel, head_dim, blocks, not state, last),
        grid=(wide // head_dim,),
        out_shape=out_shape,
        in_specs=[pl.BlockSpec(memory_space=pltpu.SMEM), column]
        + [pl.BlockSpec((rows, 2 * head_dim), lambda i: (0, 0))] * blocks
        + [column] * len(state),
        out_specs=out_specs,
        scratch_shapes=[pltpu.VMEM((rows, blocks * rows), jnp.float32)],
        name="attend",
    )(jnp.stack(bias), rot_q, *kv_blocks, *state)


def expert_kernel(count, up_steps, *refs):
    rows_refs, (wg_ref, wu_ref, wd_ref), out_refs = refs[:count], refs[count : count + 3], refs[count + 3 : -1]
    hidden_ref = refs[-1]
    step = pl.program_id(1)
    rows = rows_refs[0].shape[0]

    for now in range(up_steps):

        @pl.when(step == now)
        def _():
            part = wg_ref.shape[1]
            for i, ref in enumerate(rows_refs):
                gate = jnp.dot(ref[...], wg_ref[...], preferred_element_type=jnp.float32)
                up = jnp.dot(ref[...], wu_ref[...], preferred_element_type=jnp.float32)
                hidden = (gate / (1.0 + jnp.exp(-gate))) * up
                hidden_ref[i * rows : (i + 1) * rows, now * part : (now + 1) * part] = hidden.astype(
                    jnp.bfloat16
                )

    @pl.when(step >= up_steps)
    def _():
        for i, ref in enumerate(out_refs):
            ref[...] = jnp.dot(
                hidden_ref[i * rows : (i + 1) * rows, :],
                wd_ref[...],
                preferred_element_type=jnp.float32,
            ).astype(jnp.bfloat16)


def run_experts(arrived, w_gate, w_up, w_down):
    count = len(arrived)
    experts, rows, width = arrived[0].shape
    ff = w_gate.shape[2]
    part = ff // 3 if ff % 384 == 0 else ff
    out_part = width // 4 if width % 512 == 0 else width
    up_steps, down_steps = ff // part, width // out_part
    return pl.pallas_call(
        functools.partial(expert_kernel, count, up_steps),
        grid=(experts, up_steps + down_steps),
        out_shape=[jax.ShapeDtypeStruct((experts, rows, width), jnp.bfloat16)] * count,
        in_specs=[pl.BlockSpec((None, rows, width), lambda e, i: (e, 0, 0))] * count
        + [pl.BlockSpec((None, width, part), lambda e, i: (e, 0, jnp.minimum(i, up_steps - 1)))] * 2
        + [pl.BlockSpec((None, ff, out_part), lambda e, i: (e, 0, jnp.maximum(i - up_steps, 0)))],
        out_specs=[
            pl.BlockSpec((None, rows, out_part), lambda e, i: (e, 0, jnp.maximum(i - up_steps, 0)))
        ]
        * count,
        scratch_shapes=[pltpu.VMEM((count * rows, ff), jnp.bfloat16)],
        name="experts",
    )(*arrived, w_gate, w_up, w_down)


def pairs(seq_count, head_count, step):
    made = []
    for s in range(seq_count):
        for h in range(head_count):
            to = step(s, h)
            if to is not None:
                made.append((s * head_count + h, to[0] * head_count + to[1]))
    return made


def split_exact(values):
    high = values.astype(jnp.bfloat16)
    low = (values - high.astype(jnp.float32)).astype(jnp.bfloat16)
    return high, low


def body(
    tokens,
    input_gain,
    w_query,
    w_key,
    w_value,
    query_gain,
    key_gain,
    w_out,
    post_gain,
    expert_ids,
    route_weights,
    w_gate,
    w_up,
    w_down,
):
    tok_rows, width = tokens.shape
    head_dim = query_gain.shape[0]
    heads_here = w_query.shape[1] // head_dim
    seq_count = lax.axis_size("seq")
    seq_index = lax.axis_index("seq")
    head_count = lax.axis_size("head")
    head_index = lax.axis_index("head")
    side = 2 if seq_count % 2 == 0 else 1
    line = seq_count // side
    cores = 2 if head_count % 2 == 0 else 1
    towers = head_count // cores
    line_index, side_index = seq_index // side, seq_index % side
    tower_index, core_index = head_index // cores, head_index % cores
    make_pairs = functools.partial(pairs, seq_count, head_count)

    half_dim = head_dim // 2
    offset = seq_index * tok_rows
    positions = (offset + jnp.arange(tok_rows, dtype=jnp.int32)).astype(jnp.float32)
    frequency = THETA ** (-jnp.arange(half_dim, dtype=jnp.float32) * 2.0 / head_dim)
    angles = positions[:, None] * frequency[None, :]
    cosine, sine = jnp.cos(angles), jnp.sin(angles)
    cos_table = jnp.concatenate([cosine, cosine], axis=1)
    sin_table = jnp.concatenate([-sine, sine], axis=1)

    normed, own_kv = pl.pallas_call(
        first_kernel,
        out_shape=(
            jax.ShapeDtypeStruct((tok_rows, width), jnp.bfloat16),
            jax.ShapeDtypeStruct((tok_rows, 2 * head_dim), jnp.bfloat16),
        ),
        in_specs=[VMEM] * 7,
        out_specs=(VMEM, VMEM),
        name="norm_kv",
    )(tokens, input_gain[None], w_key, w_value, key_gain[None], cos_table, sin_table)

    kv_blocks, kv_bias = [own_kv], [jnp.float32(0.0)]
    for k in range(1, line):
        up = make_pairs(
            lambda s, h, k=k: (s + k * side, h) if s + k * side < seq_count else None
        )
        kv_blocks.append(lax.ppermute(own_kv, BOTH, up))
        kv_bias.append(jnp.where(line_index >= k, 0.0, NEGATIVE))
    if side == 2:
        swap = make_pairs(lambda s, h: (s ^ 1, h))
        for k in range(line):
            kv_blocks.append(lax.ppermute(kv_blocks[k], BOTH, swap))
            seen = line_index >= k if k else side_index == 1
            kv_bias.append(jnp.where(seen, 0.0, NEGATIVE))

    rows_here = tok_rows // head_count
    top_count = expert_ids.shape[1]
    halves = 2 if line % 2 == 0 else 1
    local_count = w_gate.shape[0]
    experts_all = local_count * seq_count * head_count
    experts_half = experts_all // halves
    members = seq_count * head_count // halves
    capacity = max(2, 3 * rows_here * top_count // (2 * experts_all))
    slots = experts_half * capacity
    first_expert = (seq_index // (seq_count // halves)) * experts_half
    mirror = make_pairs(lambda s, h: ((line - 1 - s // side) * side + s % side, h))
    mixing = route_weights / jnp.sum(route_weights, axis=1, keepdims=True)
    routes = [(expert_ids, mixing)]
    if halves == 2:
        sent = jnp.concatenate([expert_ids.astype(jnp.float32), mixing], axis=1)
        seen = lax.ppermute(sent, BOTH, mirror)
        routes.append((seen[:, :top_count].astype(jnp.int32), seen[:, top_count:]))

    def slot_tables(ids, weights):
        here = first_expert + jnp.arange(experts_half, dtype=jnp.int32)
        named = ids[:, :, None] == here[None, None, :]
        counts = jnp.sum(named, axis=1).astype(jnp.bfloat16)
        earlier = (
            jnp.arange(rows_here)[:, None] > jnp.arange(rows_here)[None, :]
        ).astype(jnp.bfloat16)
        rank_table = jnp.dot(earlier, counts, preferred_element_type=jnp.float32)
        mix_table = jnp.sum(jnp.where(named, weights[:, :, None], 0.0), axis=1)
        place = jnp.where(counts > 0, rank_table, -1.0).astype(jnp.int32)
        in_slot = place[:, :, None] == jnp.arange(capacity, dtype=jnp.int32)[None, None, :]
        pick = in_slot.astype(jnp.bfloat16).reshape(rows_here, slots)
        mix = jnp.where(in_slot, mix_table[:, :, None], 0.0).reshape(rows_here, slots)
        return pick, jnp.concatenate(split_exact(mix), axis=0)

    tables = [slot_tables(*route) for route in routes]
    query_step = 2 * head_dim if heads_here % 2 == 0 else head_dim
    rot_q = pl.pallas_call(
        functools.partial(query_kernel, head_dim),
        grid=(w_query.shape[1] // query_step,),
        out_shape=jax.ShapeDtypeStruct((tok_rows, w_query.shape[1]), jnp.bfloat16),
        in_specs=[
            pl.BlockSpec((tok_rows, width), lambda i: (0, 0)),
            pl.BlockSpec((width, query_step), lambda i: (0, i)),
            pl.BlockSpec((1, head_dim), lambda i: (0, 0)),
            pl.BlockSpec((tok_rows, head_dim), lambda i: (0, 0)),
            pl.BlockSpec((tok_rows, head_dim), lambda i: (0, 0)),
        ],
        out_specs=pl.BlockSpec((tok_rows, query_step), lambda i: (0, i)),
        name="queries",
    )(normed, w_query, query_gain[None], cos_table, sin_table)

    if side == 2:
        state = attend(rot_q, head_dim, kv_blocks[:line], kv_bias[:line], (), False)
        attended = attend(rot_q, head_dim, kv_blocks[line:], kv_bias[line:], state, True)
    else:
        attended = attend(rot_q, head_dim, kv_blocks, kv_bias, (), True)

    by_tower = attended.reshape(towers, cores * rows_here, attended.shape[1])
    core_swap = make_pairs(lambda s, h: (s, h ^ 1))

    def tower_sum(k):
        rows = lax.dynamic_index_in_dim(
            by_tower, (tower_index + k) % towers, 0, keepdims=False
        )
        part = jnp.dot(rows, w_out, preferred_element_type=jnp.float32).reshape(
            cores, rows_here, width
        )
        if cores == 1:
            return part[0]
        keep = lax.dynamic_index_in_dim(part, core_index, 0, keepdims=False)
        give = lax.dynamic_index_in_dim(part, 1 - core_index, 0, keepdims=False)
        came = lax.ppermute(give.astype(jnp.bfloat16), BOTH, core_swap)
        return keep + came.astype(jnp.float32)

    attn_part = None
    for k in range(1, towers):
        shift = make_pairs(lambda s, h, k=k: (s, (h + k * cores) % head_count))
        came = lax.ppermute(tower_sum(k).astype(jnp.bfloat16), BOTH, shift)
        came = came.astype(jnp.float32)
        attn_part = came if attn_part is None else attn_part + came
    own_sum = tower_sum(0)
    attn_part = own_sum if attn_part is None else own_sum + attn_part

    own_rows = lax.dynamic_slice_in_dim(tokens, head_index * rows_here, rows_here, 0)
    residual = own_rows.astype(jnp.float32) + attn_part
    routed = rms_scale(residual, post_gain).astype(jnp.bfloat16)

    groups = [list(range(g * members, (g + 1) * members)) for g in range(halves)]

    def exchange(rows):
        return lax.all_to_all(
            rows.reshape(members, local_count * capacity, width),
            BOTH,
            split_axis=0,
            concat_axis=0,
            axis_index_groups=groups,
            tiled=True,
        )

    def dispatch(rows, pick):
        outgoing = lax.dot_general(
            pick, rows, (((0,), (0,)), ((), ())), preferred_element_type=jnp.float32
        ).astype(jnp.bfloat16)
        return (
            exchange(outgoing)
            .reshape(members, local_count, capacity, width)
            .transpose(1, 0, 2, 3)
            .reshape(local_count, members * capacity, width)
        )

    def give_back(result, mix):
        came = exchange(
            result.reshape(local_count, members, capacity, width).transpose(1, 0, 2, 3)
        ).reshape(slots, width)
        both = jnp.dot(mix, came, preferred_element_type=jnp.float32)
        return both[:rows_here] + both[rows_here:]

    weights = (w_gate, w_up, w_down)
    if halves == 2:
        mirrored = lax.ppermute(routed, BOTH, mirror)
        own_rows_in = dispatch(routed, tables[0][0])
        far_rows_in = dispatch(mirrored, tables[1][0])
        own_result = run_experts([own_rows_in], *weights)[0]
        far_result = run_experts([far_rows_in], *weights)[0]
        foreign = give_back(far_result, tables[1][1]).astype(jnp.bfloat16)
        far_sum = lax.ppermute(foreign, BOTH, mirror)
        expert_sum = give_back(own_result, tables[0][1])
        expert_sum = expert_sum + far_sum.astype(jnp.float32)
    else:
        result = run_experts([dispatch(routed, tables[0][0])], *weights)[0]
        expert_sum = give_back(result, tables[0][1])
    return (residual + expert_sum).astype(jnp.bfloat16)


def solution(mesh):
    placed = (
        P("seq", None),
        P(),
        P(None, "head"),
        P(None, "head"),
        P(None, "head"),
        P(),
        P(),
        P("head", None),
        P(),
        P(("seq", "head"), None),
        P(("seq", "head"), None),
        P(("seq", "head"), None, None),
        P(("seq", "head"), None, None),
        P(("seq", "head"), None, None),
    )

    return jax.shard_map(
        body, mesh=mesh, in_specs=placed, out_specs=P(("seq", "head"), None), check_vma=False
    )
```

```python
import functools

import jax
import jax.numpy as jnp
from jax import lax
from jax.experimental import pallas as pl
from jax.experimental.pallas import tpu as pltpu
from jax.sharding import PartitionSpec as P


EPSILON = 1e-06
THETA = 1000000.0
NEGATIVE = -1e30
LOG2E = 1.4426950408889634
BOTH = ("seq", "head")
VMEM = pl.BlockSpec(memory_space=pltpu.VMEM)


def rms_scale(vectors, gain_vector):
    mean_sq = jnp.mean(vectors * vectors, axis=-1, keepdims=True)
    return vectors * lax.rsqrt(mean_sq + EPSILON) * gain_vector


def turn(vectors, cos_ref, sin_ref):
    half = vectors.shape[-1] // 2
    return vectors * cos_ref[...] + pltpu.roll(vectors, half, 1) * sin_ref[...]


def room(mib):
    return pltpu.CompilerParams(vmem_limit_bytes=mib * 2**20)


def first_kernel(x_ref, gain_ref, wk_ref, wv_ref, kgain_ref, cos_ref, sin_ref, normed_ref, kv_ref):
    rows, head_dim = x_ref.shape[0], wk_ref.shape[1]
    normed = rms_scale(x_ref[...].astype(jnp.float32), gain_ref[...]).astype(jnp.bfloat16)
    normed_ref[...] = normed
    keys = jnp.dot(normed, wk_ref[...], preferred_element_type=jnp.float32)
    keys = turn(rms_scale(keys, kgain_ref[...]), cos_ref, sin_ref)
    kv_ref[:rows, :] = keys.astype(jnp.bfloat16)
    values = jnp.dot(normed, wv_ref[...], preferred_element_type=jnp.float32)
    for i in range(0, rows, head_dim):
        kv_ref[rows + i : rows + i + head_dim, :] = values[i : i + head_dim, :].T.astype(jnp.bfloat16)


def query_kernel(head_dim, step, normed_ref, wq_ref, qgain_ref, cos_ref, sin_ref, q_ref):
    for start in range(0, wq_ref.shape[1], step):
        wide = jnp.dot(
            normed_ref[...], wq_ref[:, start : start + step], preferred_element_type=jnp.float32
        )
        for i in range(0, step, head_dim):
            q_ref[:, start + i : start + i + head_dim] = turn(
                rms_scale(wide[:, i : i + head_dim], qgain_ref[...]), cos_ref, sin_ref
            ).astype(jnp.bfloat16)


def attend_kernel(head_dim, blocks, first, last, bias_ref, q_ref, *rest):
    kv_refs, rest = rest[:blocks], rest[blocks:]
    s_ref = rest[-1]
    rows, heads = q_ref.shape[0], q_ref.shape[1] // head_dim
    scale = head_dim ** (-0.5) * LOG2E

    def values(kv):
        return jnp.concatenate(
            [kv[rows + i : rows + i + head_dim, :] for i in range(0, rows, head_dim)], axis=1
        )

    def score(h):
        queries = q_ref[:, h * head_dim : (h + 1) * head_dim]
        tops = []
        for j, kv in enumerate(kv_refs):
            raw = lax.dot_general(
                kv[:rows, :],
                queries,
                (((1,), (1,)), ((), ())),
                preferred_element_type=jnp.float32,
            )
            if first and j == 0:
                key = lax.broadcasted_iota(jnp.int32, raw.shape, 0)
                asked = lax.broadcasted_iota(jnp.int32, raw.shape, 1)
                raw = jnp.where(key <= asked, raw, NEGATIVE)
            s_ref[h % 2, j * rows : (j + 1) * rows, :] = raw
            tops.append(jnp.max(raw.reshape(rows // 8, 8, rows), axis=0) + bias_ref[j])
        return jnp.max(functools.reduce(jnp.maximum, tops), axis=0, keepdims=True)

    def mix(h, row_max):
        if first:
            total = jnp.zeros((1, rows), jnp.float32)
            mixed = jnp.zeros((head_dim, rows), jnp.float32)
        else:
            old_max, old_total = rest[0][h, 0:1, :], rest[0][h, 1:2, :]
            row_max = jnp.maximum(row_max, old_max)
            shrink = jnp.exp2((old_max - row_max) * scale)
            total = old_total * shrink
            mixed = rest[1][h] * shrink
        sums = jnp.zeros((8, rows), jnp.float32)
        for j, kv in enumerate(kv_refs):
            floor = row_max - bias_ref[j]
            weights = jnp.exp2((s_ref[h % 2, j * rows : (j + 1) * rows, :] - floor) * scale)
            sums = sums + jnp.sum(weights.reshape(rows // 8, 8, rows), axis=0)
            mixed = mixed + jnp.dot(
                values(kv), weights.astype(jnp.bfloat16), preferred_element_type=jnp.float32
            )
        total = total + jnp.sum(sums, axis=0, keepdims=True)
        if last:
            rest[-2][:, h * head_dim : (h + 1) * head_dim] = (mixed / total).T.astype(jnp.bfloat16)
        else:
            rest[-3][h] = jnp.concatenate([row_max, total] + [total] * 6, axis=0)
            rest[-2][h] = mixed

    ahead = score(0)
    for h in range(heads):
        now, ahead = ahead, score(h + 1) if h + 1 < heads else None
        mix(h, now)


def attend(rot_q, head_dim, kv_blocks, bias, state, last):
    rows, wide = rot_q.shape
    heads, blocks = wide // head_dim, len(kv_blocks)
    if last:
        out_shape, out_specs = jax.ShapeDtypeStruct((rows, wide), jnp.bfloat16), VMEM
    else:
        out_shape = (
            jax.ShapeDtypeStruct((heads, 8, rows), jnp.float32),
            jax.ShapeDtypeStruct((heads, head_dim, rows), jnp.float32),
        )
        out_specs = (VMEM, VMEM)
    return pl.pallas_call(
        functools.partial(attend_kernel, head_dim, blocks, not state, last),
        out_shape=out_shape,
        in_specs=[pl.BlockSpec(memory_space=pltpu.SMEM)] + [VMEM] * (1 + blocks + len(state)),
        out_specs=out_specs,
        scratch_shapes=[pltpu.VMEM((2, blocks * rows, rows), jnp.float32)],
        compiler_params=room(max(16, 2 * blocks)),
        name="attend",
    )(jnp.stack(bias), rot_q, *kv_blocks, *state)


def expert_kernel(x_ref, wg_ref, wu_ref, wd_ref, out_ref, hidden_ref):
    ff, width = wd_ref.shape
    part = 256 if ff % 256 == 0 else ff
    for i in range(0, ff, part):
        gate = jnp.dot(x_ref[...], wg_ref[:, i : i + part], preferred_element_type=jnp.float32)
        up = jnp.dot(x_ref[...], wu_ref[:, i : i + part], preferred_element_type=jnp.float32)
        hidden = (gate / (1.0 + jnp.exp(-gate))) * up
        hidden_ref[:, i : i + part] = hidden.astype(jnp.bfloat16)
    part = 512 if width % 512 == 0 else width
    for i in range(0, width, part):
        out_ref[:, i : i + part] = jnp.dot(
            hidden_ref[...], wd_ref[:, i : i + part], preferred_element_type=jnp.float32
        ).astype(jnp.bfloat16)


def run_experts(grouped, w_gate, w_up, w_down):
    experts, rows, width = grouped.shape
    made = [
        pl.pallas_call(
            expert_kernel,
            out_shape=jax.ShapeDtypeStruct((rows, width), jnp.bfloat16),
            in_specs=[VMEM] * 4,
            out_specs=VMEM,
            scratch_shapes=[pltpu.VMEM((rows, w_gate.shape[2]), jnp.bfloat16)],
            compiler_params=room(20),
            name="experts",
        )(grouped[e], w_gate[e], w_up[e], w_down[e])
        for e in range(experts)
    ]
    return made[0][None] if experts == 1 else jnp.stack(made)


def pairs(seq_count, head_count, step):
    made = []
    for s in range(seq_count):
        for h in range(head_count):
            to = step(s, h)
            if to is not None:
                made.append((s * head_count + h, to[0] * head_count + to[1]))
    return made


def split_exact(values):
    high = values.astype(jnp.bfloat16)
    low = (values - high.astype(jnp.float32)).astype(jnp.bfloat16)
    return high, low


def body(
    tokens,
    input_gain,
    w_query,
    w_key,
    w_value,
    query_gain,
    key_gain,
    w_out,
    post_gain,
    expert_ids,
    route_weights,
    w_gate,
    w_up,
    w_down,
):
    tok_rows, width = tokens.shape
    head_dim = query_gain.shape[0]
    heads_here = w_query.shape[1] // head_dim
    seq_count = lax.axis_size("seq")
    seq_index = lax.axis_index("seq")
    head_count = lax.axis_size("head")
    head_index = lax.axis_index("head")
    side = 2 if seq_count % 2 == 0 else 1
    line = seq_count // side
    cores = 2 if head_count % 2 == 0 else 1
    towers = head_count // cores
    line_index, side_index = seq_index // side, seq_index % side
    tower_index, core_index = head_index // cores, head_index % cores
    make_pairs = functools.partial(pairs, seq_count, head_count)

    half_dim = head_dim // 2
    offset = seq_index * tok_rows
    positions = (offset + jnp.arange(tok_rows, dtype=jnp.int32)).astype(jnp.float32)
    frequency = THETA ** (-jnp.arange(half_dim, dtype=jnp.float32) * 2.0 / head_dim)
    angles = positions[:, None] * frequency[None, :]
    cosine, sine = jnp.cos(angles), jnp.sin(angles)
    cos_table = jnp.concatenate([cosine, cosine], axis=1)
    sin_table = jnp.concatenate([-sine, sine], axis=1)

    normed, own_kv = pl.pallas_call(
        first_kernel,
        out_shape=(
            jax.ShapeDtypeStruct((tok_rows, width), jnp.bfloat16),
            jax.ShapeDtypeStruct((2 * tok_rows, head_dim), jnp.bfloat16),
        ),
        in_specs=[VMEM] * 7,
        out_specs=(VMEM, VMEM),
        compiler_params=room(12),
        name="norm_kv",
    )(tokens, input_gain[None], w_key, w_value, key_gain[None], cos_table, sin_table)

    kv_blocks, kv_bias = [own_kv], [jnp.float32(0.0)]
    for k in range(1, line):
        up = make_pairs(
            lambda s, h, k=k: (s + k * side, h) if s + k * side < seq_count else None
        )
        kv_blocks.append(lax.ppermute(own_kv, BOTH, up))
        kv_bias.append(jnp.where(line_index >= k, 0.0, NEGATIVE))
    if side == 2:
        swap = make_pairs(lambda s, h: (s ^ 1, h))
        for k in range(line):
            kv_blocks.append(lax.ppermute(kv_blocks[k], BOTH, swap))
            seen = line_index >= k if k else side_index == 1
            kv_bias.append(jnp.where(seen, 0.0, NEGATIVE))

    rows_here = tok_rows // head_count
    top_count = expert_ids.shape[1]
    halves = 2 if line % 2 == 0 else 1
    local_count = w_gate.shape[0]
    experts_all = local_count * seq_count * head_count
    experts_half = experts_all // halves
    members = seq_count * head_count // halves
    capacity = max(2, 3 * rows_here * top_count // (2 * experts_all))
    slots = experts_half * capacity
    first_expert = (seq_index // (seq_count // halves)) * experts_half
    mirror = make_pairs(lambda s, h: ((line - 1 - s // side) * side + s % side, h))
    mixing = route_weights / jnp.sum(route_weights, axis=1, keepdims=True)
    routes = [(expert_ids, mixing)]
    if halves == 2:
        sent = jnp.concatenate([expert_ids.astype(jnp.float32), mixing], axis=1)
        seen = lax.ppermute(sent, BOTH, mirror)
        routes.append((seen[:, :top_count].astype(jnp.int32), seen[:, top_count:]))

    def slot_tables(ids, weights):
        here = first_expert + jnp.arange(experts_half, dtype=jnp.int32)
        named = ids[:, :, None] == here[None, None, :]
        counts = jnp.sum(named, axis=1).astype(jnp.bfloat16)
        earlier = (
            jnp.arange(rows_here)[:, None] > jnp.arange(rows_here)[None, :]
        ).astype(jnp.bfloat16)
        rank_table = jnp.dot(earlier, counts, preferred_element_type=jnp.float32)
        mix_table = jnp.sum(jnp.where(named, weights[:, :, None], 0.0), axis=1)
        place = jnp.where(counts > 0, rank_table, -1.0).astype(jnp.int32)
        in_slot = place[:, :, None] == jnp.arange(capacity, dtype=jnp.int32)[None, None, :]
        pick = in_slot.astype(jnp.bfloat16).reshape(rows_here, slots)
        mix = jnp.where(in_slot, mix_table[:, :, None], 0.0).reshape(rows_here, slots)
        return pick, jnp.concatenate(split_exact(mix), axis=0)

    tables = [slot_tables(*route) for route in routes]
    query_step = 2 * head_dim if heads_here % 2 == 0 else head_dim
    rot_q = pl.pallas_call(
        functools.partial(query_kernel, head_dim, query_step),
        out_shape=jax.ShapeDtypeStruct((tok_rows, w_query.shape[1]), jnp.bfloat16),
        in_specs=[VMEM] * 5,
        out_specs=VMEM,
        compiler_params=room(12),
        name="queries",
    )(normed, w_query, query_gain[None], cos_table, sin_table)

    if side == 2:
        state = attend(rot_q, head_dim, kv_blocks[:line], kv_bias[:line], (), False)
        attended = attend(rot_q, head_dim, kv_blocks[line:], kv_bias[line:], state, True)
    else:
        attended = attend(rot_q, head_dim, kv_blocks, kv_bias, (), True)

    by_tower = attended.reshape(towers, cores * rows_here, attended.shape[1])
    core_swap = make_pairs(lambda s, h: (s, h ^ 1))

    def tower_sum(k):
        rows = lax.dynamic_index_in_dim(
            by_tower, (tower_index + k) % towers, 0, keepdims=False
        )
        part = jnp.dot(rows, w_out, preferred_element_type=jnp.float32).reshape(
            cores, rows_here, width
        )
        if cores == 1:
            return part[0]
        keep = lax.dynamic_index_in_dim(part, core_index, 0, keepdims=False)
        give = lax.dynamic_index_in_dim(part, 1 - core_index, 0, keepdims=False)
        came = lax.ppermute(give.astype(jnp.bfloat16), BOTH, core_swap)
        return keep + came.astype(jnp.float32)

    attn_part = None
    for k in range(1, towers):
        shift = make_pairs(lambda s, h, k=k: (s, (h + k * cores) % head_count))
        came = lax.ppermute(tower_sum(k).astype(jnp.bfloat16), BOTH, shift)
        came = came.astype(jnp.float32)
        attn_part = came if attn_part is None else attn_part + came
    own_sum = tower_sum(0)
    attn_part = own_sum if attn_part is None else own_sum + attn_part

    own_rows = lax.dynamic_slice_in_dim(tokens, head_index * rows_here, rows_here, 0)
    residual = own_rows.astype(jnp.float32) + attn_part
    routed = rms_scale(residual, post_gain).astype(jnp.bfloat16)

    groups = [list(range(g * members, (g + 1) * members)) for g in range(halves)]

    def exchange(rows):
        return lax.all_to_all(
            rows.reshape(members, local_count * capacity, width),
            BOTH,
            split_axis=0,
            concat_axis=0,
            axis_index_groups=groups,
            tiled=True,
        )

    def dispatch(rows, pick):
        outgoing = lax.dot_general(
            pick, rows, (((0,), (0,)), ((), ())), preferred_element_type=jnp.float32
        ).astype(jnp.bfloat16)
        return (
            exchange(outgoing)
            .reshape(members, local_count, capacity, width)
            .transpose(1, 0, 2, 3)
            .reshape(local_count, members * capacity, width)
        )

    def give_back(result, mix):
        came = exchange(
            result.reshape(local_count, members, capacity, width).transpose(1, 0, 2, 3)
        ).reshape(slots, width)
        both = jnp.dot(mix, came, preferred_element_type=jnp.float32)
        return both[:rows_here] + both[rows_here:]

    weights = (w_gate, w_up, w_down)
    if halves == 2:
        mirrored = lax.ppermute(routed, BOTH, mirror)
        own_rows_in = dispatch(routed, tables[0][0])
        far_rows_in = dispatch(mirrored, tables[1][0])
        own_result = run_experts(own_rows_in, *weights)
        far_result = run_experts(far_rows_in, *weights)
        foreign = give_back(far_result, tables[1][1]).astype(jnp.bfloat16)
        far_sum = lax.ppermute(foreign, BOTH, mirror)
        expert_sum = give_back(own_result, tables[0][1])
        expert_sum = expert_sum + far_sum.astype(jnp.float32)
    else:
        result = run_experts(dispatch(routed, tables[0][0]), *weights)
        expert_sum = give_back(result, tables[0][1])
    return (residual + expert_sum).astype(jnp.bfloat16)


def solution(mesh):
    placed = (
        P("seq", None),
        P(),
        P(None, "head"),
        P(None, "head"),
        P(None, "head"),
        P(),
        P(),
        P("head", None),
        P(),
        P(("seq", "head"), None),
        P(("seq", "head"), None),
        P(("seq", "head"), None, None),
        P(("seq", "head"), None, None),
        P(("seq", "head"), None, None),
    )

    return jax.shard_map(
        body, mesh=mesh, in_specs=placed, out_specs=P(("seq", "head"), None), check_vma=False
    )
```

```python
import functools

import jax
import jax.numpy as jnp
from jax import lax
from jax.experimental import pallas as pl
from jax.experimental.pallas import tpu as pltpu
from jax.sharding import PartitionSpec as P


EPSILON = 1e-06
THETA = 1000000.0
NEGATIVE = -1e30
LOG2E = 1.4426950408889634
BOTH = ("seq", "head")
VMEM = pl.BlockSpec(memory_space=pltpu.VMEM)
ANY = pl.BlockSpec(memory_space=pl.ANY)


def rms_scale(vectors, gain_vector):
    mean_sq = jnp.mean(vectors * vectors, axis=-1, keepdims=True)
    return vectors * lax.rsqrt(mean_sq + EPSILON) * gain_vector


def turn(vectors, cos_ref, sin_ref):
    half = vectors.shape[-1] // 2
    return vectors * cos_ref[...] + pltpu.roll(vectors, half, 1) * sin_ref[...]


def room(mib):
    return pltpu.CompilerParams(vmem_limit_bytes=mib * 2**20)


def first_kernel(
    x_hbm, wk_hbm, wv_hbm, gain_ref, kgain_ref, cos_ref, sin_ref, normed_ref, kv_ref, x_ref, wk_ref, wv_ref, sems
):
    rows, head_dim = x_ref.shape[0], wk_ref.shape[1]
    half = rows // 2
    copies = [
        pltpu.make_async_copy(x_hbm.at[pl.ds(0, half)], x_ref.at[pl.ds(0, half)], sems.at[0]),
        pltpu.make_async_copy(x_hbm.at[pl.ds(half, half)], x_ref.at[pl.ds(half, half)], sems.at[1]),
        pltpu.make_async_copy(wk_hbm, wk_ref, sems.at[2]),
        pltpu.make_async_copy(wv_hbm, wv_ref, sems.at[3]),
    ]
    for copy in copies:
        copy.start()
    for i in range(2):
        copies[i].wait()
        part = slice(i * half, (i + 1) * half)
        normed_ref[part, :] = rms_scale(x_ref[part, :].astype(jnp.float32), gain_ref[...]).astype(
            jnp.bfloat16
        )
    normed = normed_ref[...]
    copies[2].wait()
    keys = jnp.dot(normed, wk_ref[...], preferred_element_type=jnp.float32)
    keys = turn(rms_scale(keys, kgain_ref[...]), cos_ref, sin_ref)
    kv_ref[:rows, :] = keys.astype(jnp.bfloat16)
    copies[3].wait()
    values = jnp.dot(normed, wv_ref[...], preferred_element_type=jnp.float32)
    for i in range(0, rows, head_dim):
        kv_ref[rows + i : rows + i + head_dim, :] = values[i : i + head_dim, :].T.astype(jnp.bfloat16)


def query_kernel(head_dim, step, normed_ref, wq_ref, qgain_ref, cos_ref, sin_ref, q_ref):
    for start in range(0, wq_ref.shape[1], step):
        wide = jnp.dot(
            normed_ref[...], wq_ref[:, start : start + step], preferred_element_type=jnp.float32
        )
        for i in range(0, step, head_dim):
            q_ref[:, start + i : start + i + head_dim] = turn(
                rms_scale(wide[:, i : i + head_dim], qgain_ref[...]), cos_ref, sin_ref
            ).astype(jnp.bfloat16)


def attend_kernel(head_dim, blocks, first, last, bias_ref, q_ref, *rest):
    kv_refs, rest = rest[:blocks], rest[blocks:]
    s_ref = rest[-1]
    rows, heads = q_ref.shape[0], q_ref.shape[1] // head_dim
    scale = head_dim ** (-0.5) * LOG2E

    def values(kv):
        return jnp.concatenate(
            [kv[rows + i : rows + i + head_dim, :] for i in range(0, rows, head_dim)], axis=1
        )

    def score(h):
        queries = q_ref[:, h * head_dim : (h + 1) * head_dim]
        tops = []
        for j, kv in enumerate(kv_refs):
            raw = lax.dot_general(
                kv[:rows, :],
                queries,
                (((1,), (1,)), ((), ())),
                preferred_element_type=jnp.float32,
            )
            if first and j == 0:
                key = lax.broadcasted_iota(jnp.int32, raw.shape, 0)
                asked = lax.broadcasted_iota(jnp.int32, raw.shape, 1)
                raw = jnp.where(key <= asked, raw, NEGATIVE)
            s_ref[h % 2, j * rows : (j + 1) * rows, :] = raw
            tops.append(jnp.max(raw.reshape(rows // 8, 8, rows), axis=0) + bias_ref[j])
        return jnp.max(functools.reduce(jnp.maximum, tops), axis=0, keepdims=True)

    def mix(h, row_max):
        if first:
            total = jnp.zeros((1, rows), jnp.float32)
            mixed = jnp.zeros((head_dim, rows), jnp.float32)
        else:
            old_max, old_total = rest[0][h, 0:1, :], rest[0][h, 1:2, :]
            row_max = jnp.maximum(row_max, old_max)
            shrink = jnp.exp2((old_max - row_max) * scale)
            total = old_total * shrink
            mixed = rest[1][h] * shrink
        sums = jnp.zeros((8, rows), jnp.float32)
        for j, kv in enumerate(kv_refs):
            floor = row_max - bias_ref[j]
            weights = jnp.exp2((s_ref[h % 2, j * rows : (j + 1) * rows, :] - floor) * scale)
            sums = sums + jnp.sum(weights.reshape(rows // 8, 8, rows), axis=0)
            mixed = mixed + jnp.dot(
                values(kv), weights.astype(jnp.bfloat16), preferred_element_type=jnp.float32
            )
        total = total + jnp.sum(sums, axis=0, keepdims=True)
        if last:
            rest[-2][:, h * head_dim : (h + 1) * head_dim] = (mixed / total).T.astype(jnp.bfloat16)
        else:
            rest[-3][h] = jnp.concatenate([row_max, total] + [total] * 6, axis=0)
            rest[-2][h] = mixed

    ahead = score(0)
    for h in range(heads):
        now, ahead = ahead, score(h + 1) if h + 1 < heads else None
        mix(h, now)


def attend(rot_q, head_dim, kv_blocks, bias, state, last):
    rows, wide = rot_q.shape
    heads, blocks = wide // head_dim, len(kv_blocks)
    if last:
        out_shape, out_specs = jax.ShapeDtypeStruct((rows, wide), jnp.bfloat16), VMEM
    else:
        out_shape = (
            jax.ShapeDtypeStruct((heads, 8, rows), jnp.float32),
            jax.ShapeDtypeStruct((heads, head_dim, rows), jnp.float32),
        )
        out_specs = (VMEM, VMEM)
    return pl.pallas_call(
        functools.partial(attend_kernel, head_dim, blocks, not state, last),
        out_shape=out_shape,
        in_specs=[pl.BlockSpec(memory_space=pltpu.SMEM)] + [VMEM] * (1 + blocks + len(state)),
        out_specs=out_specs,
        scratch_shapes=[pltpu.VMEM((2, blocks * rows, rows), jnp.float32)],
        compiler_params=room(max(16, 2 * blocks)),
        name="attend",
    )(jnp.stack(bias), rot_q, *kv_blocks, *state)


def expert_kernel(
    x_hbm, wg_hbm, wu_hbm, wd_hbm, out_hbm, x_ref, wg_ref, wu_ref, wd_ref, hidden_ref, out_ref, sems
):
    rows, width = x_hbm.shape
    ins = [
        pltpu.make_async_copy(hbm, ref, sems.at[i])
        for i, (hbm, ref) in enumerate(
            ((x_hbm, x_ref), (wg_hbm, wg_ref), (wu_hbm, wu_ref), (wd_hbm, wd_ref))
        )
    ]
    for copy in ins:
        copy.start()
    ins[0].wait()
    ins[1].wait()
    gate = jnp.dot(x_ref[...], wg_ref[...], preferred_element_type=jnp.float32)
    gate = gate / (1.0 + jnp.exp(-gate))
    ins[2].wait()
    up = jnp.dot(x_ref[...], wu_ref[...], preferred_element_type=jnp.float32)
    hidden_ref[...] = (gate * up).astype(jnp.bfloat16)
    ins[3].wait()
    halves = 2 if rows % 32 == 0 else 1
    half = rows // halves
    part = 512 if width % 512 == 0 else width
    outs = []
    for k in range(halves):
        for i in range(0, width, part):
            out_ref[k * half : (k + 1) * half, i : i + part] = jnp.dot(
                hidden_ref[k * half : (k + 1) * half, :],
                wd_ref[:, i : i + part],
                preferred_element_type=jnp.float32,
            ).astype(jnp.bfloat16)
        outs.append(
            pltpu.make_async_copy(
                out_ref.at[pl.ds(k * half, half)], out_hbm.at[pl.ds(k * half, half)], sems.at[4 + k]
            )
        )
        outs[-1].start()
    for copy in outs:
        copy.wait()


def run_experts(grouped, w_gate, w_up, w_down):
    experts, rows, width = grouped.shape
    ff = w_gate.shape[2]
    held = ((rows, width), (width, ff), (width, ff), (ff, width), (rows, ff), (rows, width))
    made = [
        pl.pallas_call(
            expert_kernel,
            out_shape=jax.ShapeDtypeStruct((rows, width), jnp.bfloat16),
            in_specs=[ANY] * 4,
            out_specs=ANY,
            scratch_shapes=[pltpu.VMEM(shape, jnp.bfloat16) for shape in held]
            + [pltpu.SemaphoreType.DMA((6,))],
            name="experts",
        )(grouped[e], w_gate[e], w_up[e], w_down[e])
        for e in range(experts)
    ]
    return made[0][None] if experts == 1 else jnp.stack(made)


def pairs(seq_count, head_count, step):
    made = []
    for s in range(seq_count):
        for h in range(head_count):
            to = step(s, h)
            if to is not None:
                made.append((s * head_count + h, to[0] * head_count + to[1]))
    return made


def split_exact(values):
    high = values.astype(jnp.bfloat16)
    low = (values - high.astype(jnp.float32)).astype(jnp.bfloat16)
    return high, low


def body(
    tokens,
    input_gain,
    w_query,
    w_key,
    w_value,
    query_gain,
    key_gain,
    w_out,
    post_gain,
    expert_ids,
    route_weights,
    w_gate,
    w_up,
    w_down,
):
    tok_rows, width = tokens.shape
    head_dim = query_gain.shape[0]
    heads_here = w_query.shape[1] // head_dim
    seq_count = lax.axis_size("seq")
    seq_index = lax.axis_index("seq")
    head_count = lax.axis_size("head")
    head_index = lax.axis_index("head")
    side = 2 if seq_count % 2 == 0 else 1
    line = seq_count // side
    cores = 2 if head_count % 2 == 0 else 1
    towers = head_count // cores
    line_index, side_index = seq_index // side, seq_index % side
    tower_index, core_index = head_index // cores, head_index % cores
    make_pairs = functools.partial(pairs, seq_count, head_count)

    half_dim = head_dim // 2
    offset = seq_index * tok_rows
    positions = (offset + jnp.arange(tok_rows, dtype=jnp.int32)).astype(jnp.float32)
    frequency = THETA ** (-jnp.arange(half_dim, dtype=jnp.float32) * 2.0 / head_dim)
    angles = positions[:, None] * frequency[None, :]
    cosine, sine = jnp.cos(angles), jnp.sin(angles)
    cos_table = jnp.concatenate([cosine, cosine], axis=1)
    sin_table = jnp.concatenate([-sine, sine], axis=1)

    normed, own_kv = pl.pallas_call(
        first_kernel,
        out_shape=(
            jax.ShapeDtypeStruct((tok_rows, width), jnp.bfloat16),
            jax.ShapeDtypeStruct((2 * tok_rows, head_dim), jnp.bfloat16),
        ),
        in_specs=[ANY] * 3 + [VMEM] * 4,
        out_specs=(VMEM, VMEM),
        scratch_shapes=[
            pltpu.VMEM(tokens.shape, tokens.dtype),
            pltpu.VMEM(w_key.shape, w_key.dtype),
            pltpu.VMEM(w_value.shape, w_value.dtype),
            pltpu.SemaphoreType.DMA((4,)),
        ],
        name="norm_kv",
    )(tokens, w_key, w_value, input_gain[None], key_gain[None], cos_table, sin_table)

    kv_blocks, kv_bias = [own_kv], [jnp.float32(0.0)]
    for k in range(1, line):
        up = make_pairs(
            lambda s, h, k=k: (s + k * side, h) if s + k * side < seq_count else None
        )
        kv_blocks.append(lax.ppermute(own_kv, BOTH, up))
        kv_bias.append(jnp.where(line_index >= k, 0.0, NEGATIVE))
    if side == 2:
        swap = make_pairs(lambda s, h: (s ^ 1, h))
        for k in range(line):
            kv_blocks.append(lax.ppermute(kv_blocks[k], BOTH, swap))
            seen = line_index >= k if k else side_index == 1
            kv_bias.append(jnp.where(seen, 0.0, NEGATIVE))

    rows_here = tok_rows // head_count
    top_count = expert_ids.shape[1]
    halves = 2 if line % 2 == 0 else 1
    local_count = w_gate.shape[0]
    experts_all = local_count * seq_count * head_count
    experts_half = experts_all // halves
    members = seq_count * head_count // halves
    capacity = max(2, 3 * rows_here * top_count // (2 * experts_all))
    slots = experts_half * capacity
    first_expert = (seq_index // (seq_count // halves)) * experts_half
    mirror = make_pairs(lambda s, h: ((line - 1 - s // side) * side + s % side, h))
    mixing = route_weights / jnp.sum(route_weights, axis=1, keepdims=True)
    routes = [(expert_ids, mixing)]
    if halves == 2:
        sent = jnp.concatenate([expert_ids.astype(jnp.float32), mixing], axis=1)
        seen = lax.ppermute(sent, BOTH, mirror)
        routes.append((seen[:, :top_count].astype(jnp.int32), seen[:, top_count:]))

    def slot_tables(ids, weights):
        here = first_expert + jnp.arange(experts_half, dtype=jnp.int32)
        named = ids[:, :, None] == here[None, None, :]
        counts = jnp.sum(named, axis=1).astype(jnp.bfloat16)
        earlier = (
            jnp.arange(rows_here)[:, None] > jnp.arange(rows_here)[None, :]
        ).astype(jnp.bfloat16)
        rank_table = jnp.dot(earlier, counts, preferred_element_type=jnp.float32)
        mix_table = jnp.sum(jnp.where(named, weights[:, :, None], 0.0), axis=1)
        place = jnp.where(counts > 0, rank_table, -1.0).astype(jnp.int32)
        in_slot = place[:, :, None] == jnp.arange(capacity, dtype=jnp.int32)[None, None, :]
        pick = in_slot.astype(jnp.bfloat16).reshape(rows_here, slots)
        mix = jnp.where(in_slot, mix_table[:, :, None], 0.0).reshape(rows_here, slots)
        return pick, jnp.concatenate(split_exact(mix), axis=0)

    tables = [slot_tables(*route) for route in routes]
    query_step = 2 * head_dim if heads_here % 2 == 0 else head_dim
    rot_q = pl.pallas_call(
        functools.partial(query_kernel, head_dim, query_step),
        out_shape=jax.ShapeDtypeStruct((tok_rows, w_query.shape[1]), jnp.bfloat16),
        in_specs=[VMEM] * 5,
        out_specs=VMEM,
        compiler_params=room(12),
        name="queries",
    )(normed, w_query, query_gain[None], cos_table, sin_table)

    if side == 2:
        state = attend(rot_q, head_dim, kv_blocks[:line], kv_bias[:line], (), False)
        attended = attend(rot_q, head_dim, kv_blocks[line:], kv_bias[line:], state, True)
    else:
        attended = attend(rot_q, head_dim, kv_blocks, kv_bias, (), True)

    by_tower = attended.reshape(towers, cores * rows_here, attended.shape[1])
    core_swap = make_pairs(lambda s, h: (s, h ^ 1))

    def tower_sum(k):
        rows = lax.dynamic_index_in_dim(
            by_tower, (tower_index + k) % towers, 0, keepdims=False
        )
        part = jnp.dot(rows, w_out, preferred_element_type=jnp.float32).reshape(
            cores, rows_here, width
        )
        if cores == 1:
            return part[0]
        keep = lax.dynamic_index_in_dim(part, core_index, 0, keepdims=False)
        give = lax.dynamic_index_in_dim(part, 1 - core_index, 0, keepdims=False)
        came = lax.ppermute(give.astype(jnp.bfloat16), BOTH, core_swap)
        return keep + came.astype(jnp.float32)

    attn_part = None
    for k in range(1, towers):
        shift = make_pairs(lambda s, h, k=k: (s, (h + k * cores) % head_count))
        came = lax.ppermute(tower_sum(k).astype(jnp.bfloat16), BOTH, shift)
        came = came.astype(jnp.float32)
        attn_part = came if attn_part is None else attn_part + came
    own_sum = tower_sum(0)
    attn_part = own_sum if attn_part is None else own_sum + attn_part

    own_rows = lax.dynamic_slice_in_dim(tokens, head_index * rows_here, rows_here, 0)
    residual = own_rows.astype(jnp.float32) + attn_part
    routed = rms_scale(residual, post_gain).astype(jnp.bfloat16)

    groups = [list(range(g * members, (g + 1) * members)) for g in range(halves)]

    def exchange(rows):
        return lax.all_to_all(
            rows.reshape(members, local_count * capacity, width),
            BOTH,
            split_axis=0,
            concat_axis=0,
            axis_index_groups=groups,
            tiled=True,
        )

    def dispatch(rows, pick):
        outgoing = lax.dot_general(
            pick, rows, (((0,), (0,)), ((), ())), preferred_element_type=jnp.float32
        ).astype(jnp.bfloat16)
        return (
            exchange(outgoing)
            .reshape(members, local_count, capacity, width)
            .transpose(1, 0, 2, 3)
            .reshape(local_count, members * capacity, width)
        )

    def give_back(result, mix):
        came = exchange(
            result.reshape(local_count, members, capacity, width).transpose(1, 0, 2, 3)
        ).reshape(slots, width)
        both = jnp.dot(mix, came, preferred_element_type=jnp.float32)
        return both[:rows_here] + both[rows_here:]

    weights = (w_gate, w_up, w_down)
    if halves == 2:
        mirrored = lax.ppermute(routed, BOTH, mirror)
        own_rows_in = dispatch(routed, tables[0][0])
        far_rows_in = dispatch(mirrored, tables[1][0])
        own_result = run_experts(own_rows_in, *weights)
        far_result = run_experts(far_rows_in, *weights)
        foreign = give_back(far_result, tables[1][1]).astype(jnp.bfloat16)
        far_sum = lax.ppermute(foreign, BOTH, mirror)
        expert_sum = give_back(own_result, tables[0][1])
        expert_sum = expert_sum + far_sum.astype(jnp.float32)
    else:
        result = run_experts(dispatch(routed, tables[0][0]), *weights)
        expert_sum = give_back(result, tables[0][1])
    return (residual + expert_sum).astype(jnp.bfloat16)


def solution(mesh):
    placed = (
        P("seq", None),
        P(),
        P(None, "head"),
        P(None, "head"),
        P(None, "head"),
        P(),
        P(),
        P("head", None),
        P(),
        P(("seq", "head"), None),
        P(("seq", "head"), None),
        P(("seq", "head"), None, None),
        P(("seq", "head"), None, None),
        P(("seq", "head"), None, None),
    )

    return jax.shard_map(
        body, mesh=mesh, in_specs=placed, out_specs=P(("seq", "head"), None), check_vma=False
    )
```

```python
import functools

import jax
import jax.numpy as jnp
from jax import lax
from jax.experimental import pallas as pl
from jax.experimental.pallas import tpu as pltpu
from jax.sharding import PartitionSpec as P


EPSILON = 1e-06
THETA = 1000000.0
NEGATIVE = -1e30
LOG2E = 1.4426950408889634
BOTH = ("seq", "head")
VMEM = pl.BlockSpec(memory_space=pltpu.VMEM)
ANY = pl.BlockSpec(memory_space=pl.ANY)


def rms_scale(vectors, gain_vector):
    mean_sq = jnp.mean(vectors * vectors, axis=-1, keepdims=True)
    return vectors * lax.rsqrt(mean_sq + EPSILON) * gain_vector


def turn(vectors, cos_ref, sin_ref):
    half = vectors.shape[-1] // 2
    return vectors * cos_ref[...] + pltpu.roll(vectors, half, 1) * sin_ref[...]


def room(mib):
    return pltpu.CompilerParams(vmem_limit_bytes=mib * 2**20)


def first_kernel(*refs):
    hbm, (kv_ref,), held, sems = refs[:7], refs[7:8], refs[8:15], refs[15]
    x_ref, wk_ref, wv_ref, gain_ref, kgain_ref, cos_ref, sin_ref = held
    rows, head_dim = x_ref.shape[0], wk_ref.shape[1]
    copies = [pltpu.make_async_copy(a, b, sems.at[i]) for i, (a, b) in enumerate(zip(hbm, held))]
    for i in (0, 3, 1, 4, 5, 6, 2):
        copies[i].start()
    copies[0].wait()
    copies[3].wait()
    normed = rms_scale(x_ref[...].astype(jnp.float32), gain_ref[...]).astype(jnp.bfloat16)
    for i in (1, 4, 5, 6):
        copies[i].wait()
    keys = jnp.dot(normed, wk_ref[...], preferred_element_type=jnp.float32)
    keys = turn(rms_scale(keys, kgain_ref[...]), cos_ref, sin_ref)
    kv_ref[:rows, :] = keys.astype(jnp.bfloat16)
    copies[2].wait()
    values = jnp.dot(normed, wv_ref[...], preferred_element_type=jnp.float32)
    for i in range(0, rows, head_dim):
        kv_ref[rows + i : rows + i + head_dim, :] = values[i : i + head_dim, :].T.astype(jnp.bfloat16)


def query_kernel(head_dim, step, x_ref, gain_ref, wq_ref, qgain_ref, cos_ref, sin_ref, q_ref):
    normed = rms_scale(x_ref[...].astype(jnp.float32), gain_ref[...]).astype(jnp.bfloat16)
    for start in range(0, wq_ref.shape[1], step):
        wide = jnp.dot(
            normed, wq_ref[:, start : start + step], preferred_element_type=jnp.float32
        )
        for i in range(0, step, head_dim):
            q_ref[:, start + i : start + i + head_dim] = turn(
                rms_scale(wide[:, i : i + head_dim], qgain_ref[...]), cos_ref, sin_ref
            ).astype(jnp.bfloat16)


def attend_kernel(head_dim, blocks, first, last, bias_ref, q_ref, *rest):
    kv_refs, rest = rest[:blocks], rest[blocks:]
    s_ref = rest[-1]
    rows, heads = q_ref.shape[0], q_ref.shape[1] // head_dim
    scale = head_dim ** (-0.5) * LOG2E

    def values(kv):
        return jnp.concatenate(
            [kv[rows + i : rows + i + head_dim, :] for i in range(0, rows, head_dim)], axis=1
        )

    def score(h):
        queries = q_ref[:, h * head_dim : (h + 1) * head_dim]
        tops = []
        for j, kv in enumerate(kv_refs):
            raw = lax.dot_general(
                kv[:rows, :],
                queries,
                (((1,), (1,)), ((), ())),
                preferred_element_type=jnp.float32,
            )
            if first and j == 0:
                key = lax.broadcasted_iota(jnp.int32, raw.shape, 0)
                asked = lax.broadcasted_iota(jnp.int32, raw.shape, 1)
                raw = jnp.where(key <= asked, raw, NEGATIVE)
            s_ref[h % 2, j * rows : (j + 1) * rows, :] = raw
            tops.append(jnp.max(raw.reshape(rows // 8, 8, rows), axis=0) + bias_ref[j])
        return jnp.max(functools.reduce(jnp.maximum, tops), axis=0, keepdims=True)

    def mix(h, row_max):
        if first:
            total = jnp.zeros((1, rows), jnp.float32)
            mixed = jnp.zeros((head_dim, rows), jnp.float32)
        else:
            old_max, old_total = rest[0][h, 0:1, :], rest[0][h, 1:2, :]
            row_max = jnp.maximum(row_max, old_max)
            shrink = jnp.exp2((old_max - row_max) * scale)
            total = old_total * shrink
            mixed = rest[1][h] * shrink
        sums = jnp.zeros((8, rows), jnp.float32)
        for j, kv in enumerate(kv_refs):
            floor = row_max - bias_ref[j]
            weights = jnp.exp2((s_ref[h % 2, j * rows : (j + 1) * rows, :] - floor) * scale)
            sums = sums + jnp.sum(weights.reshape(rows // 8, 8, rows), axis=0)
            mixed = mixed + jnp.dot(
                values(kv), weights.astype(jnp.bfloat16), preferred_element_type=jnp.float32
            )
        total = total + jnp.sum(sums, axis=0, keepdims=True)
        if last:
            rest[-2][:, h * head_dim : (h + 1) * head_dim] = (mixed / total).T.astype(jnp.bfloat16)
        else:
            rest[-3][h] = jnp.concatenate([row_max, total] + [total] * 6, axis=0)
            rest[-2][h] = mixed

    ahead = score(0)
    for h in range(heads):
        now, ahead = ahead, score(h + 1) if h + 1 < heads else None
        mix(h, now)


def attend(rot_q, head_dim, kv_blocks, bias, state, last):
    rows, wide = rot_q.shape
    heads, blocks = wide // head_dim, len(kv_blocks)
    if last:
        out_shape, out_specs = jax.ShapeDtypeStruct((rows, wide), jnp.bfloat16), VMEM
    else:
        out_shape = (
            jax.ShapeDtypeStruct((heads, 8, rows), jnp.float32),
            jax.ShapeDtypeStruct((heads, head_dim, rows), jnp.float32),
        )
        out_specs = (VMEM, VMEM)
    return pl.pallas_call(
        functools.partial(attend_kernel, head_dim, blocks, not state, last),
        out_shape=out_shape,
        in_specs=[pl.BlockSpec(memory_space=pltpu.SMEM)] + [VMEM] * (1 + blocks + len(state)),
        out_specs=out_specs,
        scratch_shapes=[pltpu.VMEM((2, blocks * rows, rows), jnp.float32)],
        compiler_params=room(max(16, 2 * blocks)),
        name="attend",
    )(jnp.stack(bias), rot_q, *kv_blocks, *state)


def expert_kernel(
    x_hbm, wg_ref, wu_hbm, wd_hbm, out_hbm, x_ref, wu_ref, wd_ref, hidden_ref, out_ref, sems
):
    rows, width = x_hbm.shape
    ins = [
        pltpu.make_async_copy(hbm, ref, sems.at[i])
        for i, (hbm, ref) in enumerate(((x_hbm, x_ref), (wu_hbm, wu_ref), (wd_hbm, wd_ref)))
    ]
    for copy in ins:
        copy.start()
    ins[0].wait()
    gate = jnp.dot(x_ref[...], wg_ref[...], preferred_element_type=jnp.float32)
    gate = gate / (1.0 + jnp.exp(-gate))
    ins[1].wait()
    up = jnp.dot(x_ref[...], wu_ref[...], preferred_element_type=jnp.float32)
    hidden_ref[...] = (gate * up).astype(jnp.bfloat16)
    ins[2].wait()
    halves = 2 if rows % 32 == 0 else 1
    half = rows // halves
    part = 512 if width % 512 == 0 else width
    outs = []
    for k in range(halves):
        for i in range(0, width, part):
            out_ref[k * half : (k + 1) * half, i : i + part] = jnp.dot(
                hidden_ref[k * half : (k + 1) * half, :],
                wd_ref[:, i : i + part],
                preferred_element_type=jnp.float32,
            ).astype(jnp.bfloat16)
        outs.append(
            pltpu.make_async_copy(
                out_ref.at[pl.ds(k * half, half)], out_hbm.at[pl.ds(k * half, half)], sems.at[3 + k]
            )
        )
        outs[-1].start()
    for copy in outs:
        copy.wait()


def run_experts(grouped, w_gate, w_up, w_down):
    experts, rows, width = grouped.shape
    ff = w_gate.shape[2]
    held = ((rows, width), (width, ff), (ff, width), (rows, ff), (rows, width))
    gates = [pltpu.with_memory_space_constraint(w_gate[e], pltpu.VMEM) for e in range(experts)]
    made = [
        pl.pallas_call(
            expert_kernel,
            out_shape=jax.ShapeDtypeStruct((rows, width), jnp.bfloat16),
            in_specs=[ANY, VMEM, ANY, ANY],
            out_specs=ANY,
            scratch_shapes=[pltpu.VMEM(shape, jnp.bfloat16) for shape in held]
            + [pltpu.SemaphoreType.DMA((5,))],
            name="experts",
        )(grouped[e], gates[e], w_up[e], w_down[e])
        for e in range(experts)
    ]
    return made[0][None] if experts == 1 else jnp.stack(made)


def route_kernel(*refs):
    parts, (rows_ref, gain_ref, pick_ref, residual_ref, routed_ref, out_ref) = refs[:-6], refs[-6:]
    residual = rows_ref[...].astype(jnp.float32)
    for ref in parts:
        residual = residual + ref[...].astype(jnp.float32)
    residual_ref[...] = residual
    routed = rms_scale(residual, gain_ref[...]).astype(jnp.bfloat16)
    routed_ref[...] = routed
    out_ref[...] = jnp.dot(
        pick_ref[...], routed, preferred_element_type=jnp.float32
    ).astype(jnp.bfloat16)


def pairs(seq_count, head_count, step):
    made = []
    for s in range(seq_count):
        for h in range(head_count):
            to = step(s, h)
            if to is not None:
                made.append((s * head_count + h, to[0] * head_count + to[1]))
    return made


def split_exact(values):
    high = values.astype(jnp.bfloat16)
    low = (values - high.astype(jnp.float32)).astype(jnp.bfloat16)
    return high, low


def body(
    tokens,
    input_gain,
    w_query,
    w_key,
    w_value,
    query_gain,
    key_gain,
    w_out,
    post_gain,
    expert_ids,
    route_weights,
    w_gate,
    w_up,
    w_down,
):
    tok_rows, width = tokens.shape
    head_dim = query_gain.shape[0]
    heads_here = w_query.shape[1] // head_dim
    seq_count = lax.axis_size("seq")
    seq_index = lax.axis_index("seq")
    head_count = lax.axis_size("head")
    head_index = lax.axis_index("head")
    side = 2 if seq_count % 2 == 0 else 1
    line = seq_count // side
    cores = 2 if head_count % 2 == 0 else 1
    towers = head_count // cores
    line_index, side_index = seq_index // side, seq_index % side
    tower_index, core_index = head_index // cores, head_index % cores
    make_pairs = functools.partial(pairs, seq_count, head_count)

    half_dim = head_dim // 2
    offset = seq_index * tok_rows
    positions = (offset + jnp.arange(tok_rows, dtype=jnp.int32)).astype(jnp.float32)
    frequency = THETA ** (-jnp.arange(half_dim, dtype=jnp.float32) * 2.0 / head_dim)
    angles = positions[:, None] * frequency[None, :]
    cosine, sine = jnp.cos(angles), jnp.sin(angles)
    cos_table = jnp.concatenate([cosine, cosine], axis=1)
    sin_table = jnp.concatenate([-sine, sine], axis=1)

    first_in = (
        tokens, w_key, w_value, input_gain[None], key_gain[None], cos_table, sin_table
    )
    own_kv = pl.pallas_call(
        first_kernel,
        out_shape=jax.ShapeDtypeStruct((2 * tok_rows, head_dim), jnp.bfloat16),
        in_specs=[ANY] * len(first_in),
        out_specs=VMEM,
        scratch_shapes=[pltpu.VMEM(x.shape, x.dtype) for x in first_in]
        + [pltpu.SemaphoreType.DMA((len(first_in),))],
        name="norm_kv",
    )(*first_in)

    kv_blocks, kv_bias = [own_kv], [jnp.float32(0.0)]
    for k in range(1, line):
        up = make_pairs(
            lambda s, h, k=k: (s + k * side, h) if s + k * side < seq_count else None
        )
        kv_blocks.append(lax.ppermute(own_kv, BOTH, up))
        kv_bias.append(jnp.where(line_index >= k, 0.0, NEGATIVE))
    if side == 2:
        swap = make_pairs(lambda s, h: (s ^ 1, h))
        for k in range(line):
            kv_blocks.append(lax.ppermute(kv_blocks[k], BOTH, swap))
            seen = line_index >= k if k else side_index == 1
            kv_bias.append(jnp.where(seen, 0.0, NEGATIVE))

    rows_here = tok_rows // head_count
    top_count = expert_ids.shape[1]
    halves = 2 if line % 2 == 0 else 1
    local_count = w_gate.shape[0]
    experts_all = local_count * seq_count * head_count
    experts_half = experts_all // halves
    members = seq_count * head_count // halves
    capacity = max(2, 3 * rows_here * top_count // (2 * experts_all))
    slots = experts_half * capacity
    first_expert = (seq_index // (seq_count // halves)) * experts_half
    mirror = make_pairs(lambda s, h: ((line - 1 - s // side) * side + s % side, h))
    mixing = route_weights / jnp.sum(route_weights, axis=1, keepdims=True)
    routes = [(expert_ids, mixing)]
    if halves == 2:
        sent = jnp.concatenate([expert_ids.astype(jnp.float32), mixing], axis=1)
        seen = lax.ppermute(sent, BOTH, mirror)
        routes.append((seen[:, :top_count].astype(jnp.int32), seen[:, top_count:]))

    def slot_tables(ids, weights):
        here = first_expert + jnp.arange(experts_half, dtype=jnp.int32)
        named = ids[:, :, None] == here[None, None, :]
        counts = jnp.sum(named, axis=1).astype(jnp.bfloat16)
        earlier = (
            jnp.arange(rows_here)[:, None] > jnp.arange(rows_here)[None, :]
        ).astype(jnp.bfloat16)
        rank_table = jnp.dot(earlier, counts, preferred_element_type=jnp.float32)
        mix_table = jnp.sum(jnp.where(named, weights[:, :, None], 0.0), axis=1)
        place = jnp.where(counts > 0, rank_table, -1.0).astype(jnp.int32)
        in_slot = place[:, :, None] == jnp.arange(capacity, dtype=jnp.int32)[None, None, :]
        pick = in_slot.astype(jnp.bfloat16).reshape(rows_here, slots).T
        mix = jnp.where(in_slot, mix_table[:, :, None], 0.0).reshape(rows_here, slots)
        return pick, jnp.concatenate(split_exact(mix), axis=0)

    tables = [slot_tables(*route) for route in routes]
    query_step = 2 * head_dim if heads_here % 2 == 0 else head_dim
    rot_q = pl.pallas_call(
        functools.partial(query_kernel, head_dim, query_step),
        out_shape=jax.ShapeDtypeStruct((tok_rows, w_query.shape[1]), jnp.bfloat16),
        in_specs=[VMEM] * 6,
        out_specs=VMEM,
        compiler_params=room(12),
        name="queries",
    )(tokens, input_gain[None], w_query, query_gain[None], cos_table, sin_table)

    near = line // 2
    if side == 2:
        parts = [
            [*range(near), *range(line, line + near - 1)],
            [*range(near, line), *range(line + near - 1, line + near)],
            [*range(line + near, 2 * line)],
        ]
    else:
        parts = [[*range(near)], [*range(near, line)]]
    parts = [part for part in parts if part]
    state = ()
    for n, part in enumerate(parts):
        state = attend(
            rot_q,
            head_dim,
            [kv_blocks[k] for k in part],
            [kv_bias[k] for k in part],
            state,
            n == len(parts) - 1,
        )
    attended = state

    by_tower = attended.reshape(towers, cores * rows_here, attended.shape[1])
    core_swap = make_pairs(lambda s, h: (s, h ^ 1))

    def tower_sum(k):
        rows = lax.dynamic_index_in_dim(
            by_tower, (tower_index + k) % towers, 0, keepdims=False
        )
        part = jnp.dot(rows, w_out, preferred_element_type=jnp.float32).reshape(
            cores, rows_here, width
        )
        if cores == 1:
            return part[0]
        keep = lax.dynamic_index_in_dim(part, core_index, 0, keepdims=False)
        give = lax.dynamic_index_in_dim(part, 1 - core_index, 0, keepdims=False)
        came = lax.ppermute(give.astype(jnp.bfloat16), BOTH, core_swap)
        return keep + came.astype(jnp.float32)

    summed = []
    for k in range(1, towers):
        shift = make_pairs(lambda s, h, k=k: (s, (h + k * cores) % head_count))
        summed.append(lax.ppermute(tower_sum(k).astype(jnp.bfloat16), BOTH, shift))
    summed.append(tower_sum(0))

    own_rows = lax.dynamic_slice_in_dim(tokens, head_index * rows_here, rows_here, 0)
    residual, routed, outgoing = pl.pallas_call(
        route_kernel,
        out_shape=(
            jax.ShapeDtypeStruct((rows_here, width), jnp.float32),
            jax.ShapeDtypeStruct((rows_here, width), jnp.bfloat16),
            jax.ShapeDtypeStruct((slots, width), jnp.bfloat16),
        ),
        in_specs=[VMEM] * (len(summed) + 3),
        out_specs=(VMEM,) * 3,
        name="route",
    )(*summed, own_rows, post_gain[None], tables[0][0])

    groups = [list(range(g * members, (g + 1) * members)) for g in range(halves)]

    def exchange(rows):
        return lax.all_to_all(
            rows.reshape(members, local_count * capacity, width),
            BOTH,
            split_axis=0,
            concat_axis=0,
            axis_index_groups=groups,
            tiled=True,
        )

    def dispatch(outgoing):
        return (
            exchange(outgoing)
            .reshape(members, local_count, capacity, width)
            .transpose(1, 0, 2, 3)
            .reshape(local_count, members * capacity, width)
        )

    def give_back(result, mix):
        came = exchange(
            result.reshape(local_count, members, capacity, width).transpose(1, 0, 2, 3)
        ).reshape(slots, width)
        both = jnp.dot(mix, came, preferred_element_type=jnp.float32)
        return both[:rows_here] + both[rows_here:]

    weights = (w_gate, w_up, w_down)
    if halves == 2:
        mirrored = lax.ppermute(routed, BOTH, mirror)
        own_rows_in = dispatch(outgoing)
        far_rows_in = dispatch(
            jnp.dot(tables[1][0], mirrored, preferred_element_type=jnp.float32).astype(jnp.bfloat16)
        )
        own_result = run_experts(own_rows_in, *weights)
        far_result = run_experts(far_rows_in, *weights)
        foreign = give_back(far_result, tables[1][1]).astype(jnp.bfloat16)
        far_sum = lax.ppermute(foreign, BOTH, mirror)
        expert_sum = give_back(own_result, tables[0][1])
        expert_sum = expert_sum + far_sum.astype(jnp.float32)
    else:
        result = run_experts(dispatch(outgoing), *weights)
        expert_sum = give_back(result, tables[0][1])
    return (residual + expert_sum).astype(jnp.bfloat16)


def solution(mesh):
    placed = (
        P("seq", None),
        P(),
        P(None, "head"),
        P(None, "head"),
        P(None, "head"),
        P(),
        P(),
        P("head", None),
        P(),
        P(("seq", "head"), None),
        P(("seq", "head"), None),
        P(("seq", "head"), None, None),
        P(("seq", "head"), None, None),
        P(("seq", "head"), None, None),
    )

    return jax.shard_map(
        body, mesh=mesh, in_specs=placed, out_specs=P(("seq", "head"), None), check_vma=False
    )
```

```python
import functools

import jax
import jax.numpy as jnp
from jax import lax
from jax.experimental import pallas as pl
from jax.experimental.pallas import tpu as pltpu
from jax.sharding import PartitionSpec as P


EPSILON = 1e-06
THETA = 1000000.0
NEGATIVE = -1e30
LOG2E = 1.4426950408889634
BOTH = ("seq", "head")
VMEM = pl.BlockSpec(memory_space=pltpu.VMEM)
ANY = pl.BlockSpec(memory_space=pl.ANY)


def rms_scale(vectors, gain_vector):
    mean_sq = jnp.mean(vectors * vectors, axis=-1, keepdims=True)
    return vectors * lax.rsqrt(mean_sq + EPSILON) * gain_vector


def turn(vectors, cos_ref, sin_ref):
    half = vectors.shape[-1] // 2
    return vectors * cos_ref[...] + pltpu.roll(vectors, half, 1) * sin_ref[...]


def room(mib):
    return pltpu.CompilerParams(vmem_limit_bytes=mib * 2**20)


def first_kernel(*refs):
    hbm, (kv_ref,), held, sems = refs[:7], refs[7:8], refs[8:15], refs[15]
    x_ref, wk_ref, wv_ref, gain_ref, kgain_ref, cos_ref, sin_ref = held
    rows, head_dim = x_ref.shape[0], wk_ref.shape[1]
    half = rows // 2
    upper, lower = pl.ds(0, half), pl.ds(half, half)
    copies = [pltpu.make_async_copy(a, b, sems.at[i]) for i, (a, b) in enumerate(zip(hbm, held))]
    copies[0] = pltpu.make_async_copy(hbm[0].at[upper], x_ref.at[upper], sems.at[0])
    copies.append(pltpu.make_async_copy(hbm[0].at[lower], x_ref.at[lower], sems.at[7]))
    for i in (3, 0, 7, 1, 4, 5, 6, 2):
        copies[i].start()
    copies[3].wait()
    normed = []
    for i in (0, 7):
        copies[i].wait()
        part = x_ref[upper if i == 0 else lower, :].astype(jnp.float32)
        normed.append(rms_scale(part, gain_ref[...]).astype(jnp.bfloat16))
    normed = jnp.concatenate(normed, axis=0)
    for i in (1, 4, 5, 6):
        copies[i].wait()
    keys = jnp.dot(normed, wk_ref[...], preferred_element_type=jnp.float32)
    keys = turn(rms_scale(keys, kgain_ref[...]), cos_ref, sin_ref)
    kv_ref[:rows, :] = keys.astype(jnp.bfloat16)
    copies[2].wait()
    values = jnp.dot(normed, wv_ref[...], preferred_element_type=jnp.float32)
    for i in range(0, rows, head_dim):
        kv_ref[rows + i : rows + i + head_dim, :] = values[i : i + head_dim, :].T.astype(jnp.bfloat16)


def query_kernel(head_dim, step, x_ref, gain_ref, wq_ref, qgain_ref, cos_ref, sin_ref, q_ref):
    normed = rms_scale(x_ref[...].astype(jnp.float32), gain_ref[...]).astype(jnp.bfloat16)
    for start in range(0, wq_ref.shape[1], step):
        wide = jnp.dot(
            normed, wq_ref[:, start : start + step], preferred_element_type=jnp.float32
        )
        for i in range(0, step, head_dim):
            q_ref[:, start + i : start + i + head_dim] = turn(
                rms_scale(wide[:, i : i + head_dim], qgain_ref[...]), cos_ref, sin_ref
            ).astype(jnp.bfloat16)


def attend_kernel(head_dim, blocks, first, last, bias_ref, q_ref, *rest):
    kv_refs, rest = rest[:blocks], rest[blocks:]
    s_ref = rest[-1]
    rows, heads = q_ref.shape[0], q_ref.shape[1] // head_dim
    scale = head_dim ** (-0.5) * LOG2E

    def values(kv):
        return jnp.concatenate(
            [kv[rows + i : rows + i + head_dim, :] for i in range(0, rows, head_dim)], axis=1
        )

    def score(h):
        queries = q_ref[:, h * head_dim : (h + 1) * head_dim]
        tops = []
        for j, kv in enumerate(kv_refs):
            raw = lax.dot_general(
                kv[:rows, :],
                queries,
                (((1,), (1,)), ((), ())),
                preferred_element_type=jnp.float32,
            )
            if first and j == 0:
                key = lax.broadcasted_iota(jnp.int32, raw.shape, 0)
                asked = lax.broadcasted_iota(jnp.int32, raw.shape, 1)
                raw = jnp.where(key <= asked, raw, NEGATIVE)
            s_ref[h % 2, j * rows : (j + 1) * rows, :] = raw
            tops.append(jnp.max(raw.reshape(rows // 8, 8, rows), axis=0) + bias_ref[j])
        return jnp.max(functools.reduce(jnp.maximum, tops), axis=0, keepdims=True)

    def mix(h, row_max):
        if first:
            total = jnp.zeros((1, rows), jnp.float32)
            mixed = jnp.zeros((head_dim, rows), jnp.float32)
        else:
            old_max, old_total = rest[0][h, 0:1, :], rest[0][h, 1:2, :]
            row_max = jnp.maximum(row_max, old_max)
            shrink = jnp.exp2((old_max - row_max) * scale)
            total = old_total * shrink
            mixed = rest[1][h] * shrink
        sums = jnp.zeros((8, rows), jnp.float32)
        for j, kv in enumerate(kv_refs):
            floor = row_max - bias_ref[j]
            weights = jnp.exp2((s_ref[h % 2, j * rows : (j + 1) * rows, :] - floor) * scale)
            sums = sums + jnp.sum(weights.reshape(rows // 8, 8, rows), axis=0)
            mixed = mixed + jnp.dot(
                values(kv), weights.astype(jnp.bfloat16), preferred_element_type=jnp.float32
            )
        total = total + jnp.sum(sums, axis=0, keepdims=True)
        if last:
            rest[-2][:, h * head_dim : (h + 1) * head_dim] = (mixed / total).T.astype(jnp.bfloat16)
        else:
            rest[-3][h] = jnp.concatenate([row_max, total] + [total] * 6, axis=0)
            rest[-2][h] = mixed

    ahead = score(0)
    for h in range(heads):
        now, ahead = ahead, score(h + 1) if h + 1 < heads else None
        mix(h, now)


def attend(rot_q, head_dim, kv_blocks, bias, state, last):
    rows, wide = rot_q.shape
    heads, blocks = wide // head_dim, len(kv_blocks)
    if last:
        out_shape, out_specs = jax.ShapeDtypeStruct((rows, wide), jnp.bfloat16), VMEM
    else:
        out_shape = (
            jax.ShapeDtypeStruct((heads, 8, rows), jnp.float32),
            jax.ShapeDtypeStruct((heads, head_dim, rows), jnp.float32),
        )
        out_specs = (VMEM, VMEM)
    return pl.pallas_call(
        functools.partial(attend_kernel, head_dim, blocks, not state, last),
        out_shape=out_shape,
        in_specs=[pl.BlockSpec(memory_space=pltpu.SMEM)] + [VMEM] * (1 + blocks + len(state)),
        out_specs=out_specs,
        scratch_shapes=[pltpu.VMEM((2, blocks * rows, rows), jnp.float32)],
        compiler_params=room(max(16, 2 * blocks)),
        name="attend",
    )(jnp.stack(bias), rot_q, *kv_blocks, *state)


def expert_kernel(
    x_hbm, wg_ref, wu_hbm, wd_hbm, out_hbm, x_ref, wu_ref, wd_ref, hidden_ref, out_ref, sems
):
    rows, width = x_hbm.shape
    ins = [
        pltpu.make_async_copy(hbm, ref, sems.at[i])
        for i, (hbm, ref) in enumerate(((x_hbm, x_ref), (wu_hbm, wu_ref), (wd_hbm, wd_ref)))
    ]
    for copy in ins:
        copy.start()
    ins[0].wait()
    gate = jnp.dot(x_ref[...], wg_ref[...], preferred_element_type=jnp.float32)
    gate = gate / (1.0 + jnp.exp(-gate))
    ins[1].wait()
    up = jnp.dot(x_ref[...], wu_ref[...], preferred_element_type=jnp.float32)
    hidden_ref[...] = (gate * up).astype(jnp.bfloat16)
    ins[2].wait()
    halves = 2 if rows % 32 == 0 else 1
    half = rows // halves
    part = 512 if width % 512 == 0 else width
    outs = []
    for k in range(halves):
        for i in range(0, width, part):
            out_ref[k * half : (k + 1) * half, i : i + part] = jnp.dot(
                hidden_ref[k * half : (k + 1) * half, :],
                wd_ref[:, i : i + part],
                preferred_element_type=jnp.float32,
            ).astype(jnp.bfloat16)
        outs.append(
            pltpu.make_async_copy(
                out_ref.at[pl.ds(k * half, half)], out_hbm.at[pl.ds(k * half, half)], sems.at[3 + k]
            )
        )
        outs[-1].start()
    for copy in outs:
        copy.wait()


def run_experts(grouped, gates, w_up, w_down):
    experts, rows, width = grouped.shape
    ff = w_up.shape[2]
    held = ((rows, width), (width, ff), (ff, width), (rows, ff), (rows, width))
    made = [
        pl.pallas_call(
            expert_kernel,
            out_shape=jax.ShapeDtypeStruct((rows, width), jnp.bfloat16),
            in_specs=[ANY, VMEM, ANY, ANY],
            out_specs=ANY,
            scratch_shapes=[pltpu.VMEM(shape, jnp.bfloat16) for shape in held]
            + [pltpu.SemaphoreType.DMA((5,))],
            name="experts",
        )(
            pltpu.with_memory_space_constraint(grouped[e], pltpu.HBM), gates[e], w_up[e], w_down[e]
        )
        for e in range(experts)
    ]
    return made[0][None] if experts == 1 else jnp.stack(made)


def fill_kernel(rows_ref, pick_ref, gate_ref, out_ref):
    del gate_ref
    out_ref[...] = lax.dot_general(
        pick_ref[...], rows_ref[...], (((0,), (0,)), ((), ())), preferred_element_type=jnp.float32
    ).astype(jnp.bfloat16)


def pairs(seq_count, head_count, step):
    made = []
    for s in range(seq_count):
        for h in range(head_count):
            to = step(s, h)
            if to is not None:
                made.append((s * head_count + h, to[0] * head_count + to[1]))
    return made


def split_exact(values):
    high = values.astype(jnp.bfloat16)
    low = (values - high.astype(jnp.float32)).astype(jnp.bfloat16)
    return high, low


def body(
    tokens,
    input_gain,
    w_query,
    w_key,
    w_value,
    query_gain,
    key_gain,
    w_out,
    post_gain,
    expert_ids,
    route_weights,
    w_gate,
    w_up,
    w_down,
):
    tok_rows, width = tokens.shape
    head_dim = query_gain.shape[0]
    heads_here = w_query.shape[1] // head_dim
    seq_count = lax.axis_size("seq")
    seq_index = lax.axis_index("seq")
    head_count = lax.axis_size("head")
    head_index = lax.axis_index("head")
    side = 2 if seq_count % 2 == 0 else 1
    line = seq_count // side
    cores = 2 if head_count % 2 == 0 else 1
    towers = head_count // cores
    line_index, side_index = seq_index // side, seq_index % side
    tower_index, core_index = head_index // cores, head_index % cores
    make_pairs = functools.partial(pairs, seq_count, head_count)

    half_dim = head_dim // 2
    offset = seq_index * tok_rows
    positions = (offset + jnp.arange(tok_rows, dtype=jnp.int32)).astype(jnp.float32)
    frequency = THETA ** (-jnp.arange(half_dim, dtype=jnp.float32) * 2.0 / head_dim)
    angles = positions[:, None] * frequency[None, :]
    cosine, sine = jnp.cos(angles), jnp.sin(angles)
    cos_table = jnp.concatenate([cosine, cosine], axis=1)
    sin_table = jnp.concatenate([-sine, sine], axis=1)

    first_in = (
        tokens, w_key, w_value, input_gain[None], key_gain[None], cos_table, sin_table
    )
    own_kv = pl.pallas_call(
        first_kernel,
        out_shape=jax.ShapeDtypeStruct((2 * tok_rows, head_dim), jnp.bfloat16),
        in_specs=[ANY] * len(first_in),
        out_specs=VMEM,
        scratch_shapes=[pltpu.VMEM(x.shape, x.dtype) for x in first_in]
        + [pltpu.SemaphoreType.DMA((len(first_in) + 1,))],
        name="norm_kv",
    )(*first_in)

    kv_blocks, kv_bias = [own_kv], [jnp.float32(0.0)]
    for k in range(1, line):
        up = make_pairs(
            lambda s, h, k=k: (s + k * side, h) if s + k * side < seq_count else None
        )
        kv_blocks.append(lax.ppermute(own_kv, BOTH, up))
        kv_bias.append(jnp.where(line_index >= k, 0.0, NEGATIVE))
    if side == 2:
        swap = make_pairs(lambda s, h: (s ^ 1, h))
        for k in range(line):
            kv_blocks.append(lax.ppermute(kv_blocks[k], BOTH, swap))
            seen = line_index >= k if k else side_index == 1
            kv_bias.append(jnp.where(seen, 0.0, NEGATIVE))

    rows_here = tok_rows // head_count
    top_count = expert_ids.shape[1]
    halves = 2 if line % 2 == 0 else 1
    local_count = w_gate.shape[0]
    experts_all = local_count * seq_count * head_count
    experts_half = experts_all // halves
    members = seq_count * head_count // halves
    capacity = max(2, 3 * rows_here * top_count // (2 * experts_all))
    slots = experts_half * capacity
    first_expert = (seq_index // (seq_count // halves)) * experts_half
    mirror = make_pairs(lambda s, h: ((line - 1 - s // side) * side + s % side, h))
    mixing = route_weights / jnp.sum(route_weights, axis=1, keepdims=True)

    def slot_tables(ids, weights, zero):
        here = first_expert + zero + jnp.arange(experts_half, dtype=jnp.int32)
        named = ids[:, :, None] == here[None, None, :]
        counts = jnp.sum(named, axis=1).astype(jnp.bfloat16)
        earlier = (
            jnp.arange(rows_here)[:, None] > jnp.arange(rows_here)[None, :]
        ).astype(jnp.bfloat16)
        rank_table = jnp.dot(earlier, counts, preferred_element_type=jnp.float32)
        mix_table = jnp.sum(jnp.where(named, weights[:, :, None], 0.0), axis=1)
        place = jnp.where(counts > 0, rank_table, -1.0).astype(jnp.int32)
        in_slot = place[:, :, None] == (zero + jnp.arange(capacity, dtype=jnp.int32))[None, None, :]
        pick = in_slot.astype(jnp.bfloat16).reshape(rows_here, slots)
        mix = jnp.where(in_slot, mix_table[:, :, None], 0.0).reshape(rows_here, slots)
        return pick, jnp.concatenate(split_exact(mix), axis=0)

    tables = [slot_tables(expert_ids, mixing, jnp.int32(0))]

    query_step = 2 * head_dim if heads_here % 2 == 0 else head_dim
    rot_q = pl.pallas_call(
        functools.partial(query_kernel, head_dim, query_step),
        out_shape=jax.ShapeDtypeStruct((tok_rows, w_query.shape[1]), jnp.bfloat16),
        in_specs=[VMEM] * 6,
        out_specs=VMEM,
        compiler_params=room(12),
        name="queries",
    )(tokens, input_gain[None], w_query, query_gain[None], cos_table, sin_table)

    near = line // 2
    if side == 2:
        parts = [
            [*range(near), *range(line, line + near - 1)],
            [*range(near, line - 1), *range(line + near - 1, line + near)],
            [line - 1, *range(line + near, 2 * line - 1)],
            [2 * line - 1],
        ]
    else:
        parts = [[*range(near)], [*range(near, line)]]
    parts = [part for part in parts if part]
    state = ()
    for n, part in enumerate(parts):
        state = attend(
            rot_q,
            head_dim,
            [kv_blocks[k] for k in part],
            [kv_bias[k] for k in part],
            state,
            n == len(parts) - 1,
        )
    attended = state

    by_tower = attended.reshape(towers, cores * rows_here, attended.shape[1])
    core_swap = make_pairs(lambda s, h: (s, h ^ 1))

    def tower_sum(k):
        rows = lax.dynamic_index_in_dim(
            by_tower, (tower_index + k) % towers, 0, keepdims=False
        )
        part = jnp.dot(rows, w_out, preferred_element_type=jnp.float32).reshape(
            cores, rows_here, width
        )
        if cores == 1:
            return part[0]
        keep = lax.dynamic_index_in_dim(part, core_index, 0, keepdims=False)
        give = lax.dynamic_index_in_dim(part, 1 - core_index, 0, keepdims=False)
        came = lax.ppermute(give.astype(jnp.bfloat16), BOTH, core_swap)
        return keep + came.astype(jnp.float32)

    attn_part = None
    for k in range(1, towers):
        shift = make_pairs(lambda s, h, k=k: (s, (h + k * cores) % head_count))
        given = tower_sum(k).astype(jnp.bfloat16)
        came = lax.ppermute(given, BOTH, shift).astype(jnp.float32)
        attn_part = came if attn_part is None else attn_part + came
    own_sum = tower_sum(0)
    attn_part = own_sum if attn_part is None else own_sum + attn_part

    own_rows = lax.dynamic_slice_in_dim(tokens, head_index * rows_here, rows_here, 0)
    residual = own_rows.astype(jnp.float32) + attn_part
    routed = rms_scale(residual, post_gain).astype(jnp.bfloat16)

    groups = [list(range(g * members, (g + 1) * members)) for g in range(halves)]

    def exchange(rows):
        return lax.all_to_all(
            rows.reshape(members, local_count * capacity, width),
            BOTH,
            split_axis=0,
            concat_axis=0,
            axis_index_groups=groups,
            tiled=True,
        )

    def dispatch(outgoing):
        return (
            exchange(outgoing)
            .reshape(members, local_count, capacity, width)
            .transpose(1, 0, 2, 3)
            .reshape(local_count, members * capacity, width)
        )

    def fill_slots(rows, pick):
        return lax.dot_general(
            pick, rows, (((0,), (0,)), ((), ())), preferred_element_type=jnp.float32
        ).astype(jnp.bfloat16)

    def give_back(result, mix):
        came = exchange(
            result.reshape(local_count, members, capacity, width).transpose(1, 0, 2, 3)
        ).reshape(slots, width)
        both = jnp.dot(mix, came, preferred_element_type=jnp.float32)
        return both[:rows_here] + both[rows_here:]

    gates = [pltpu.with_memory_space_constraint(w_gate[e], pltpu.VMEM) for e in range(local_count)]
    weights = (gates, w_up, w_down)
    if halves == 2:
        spare = -3 * top_count % head_dim
        sent = jnp.concatenate(
            [
                routed,
                expert_ids.astype(jnp.bfloat16),
                *split_exact(mixing),
                jnp.zeros((rows_here, spare), jnp.bfloat16),
            ],
            axis=1,
        )
        came = lax.ppermute(sent, BOTH, mirror)
        own_rows_in = dispatch(fill_slots(routed, tables[0][0]))
        mirrored, beside = came[:, :width], came[:, width:].astype(jnp.float32)
        tables.append(
            slot_tables(
                beside[:, :top_count].astype(jnp.int32),
                beside[:, top_count : 2 * top_count]
                + beside[:, 2 * top_count : 3 * top_count],
                lax.optimization_barrier(jnp.int32(0)),
            )
        )
        filled = pl.pallas_call(
            fill_kernel,
            out_shape=jax.ShapeDtypeStruct((slots, width), jnp.bfloat16),
            in_specs=[VMEM] * 3,
            out_specs=VMEM,
            name="fill",
        )(mirrored, tables[1][0], gates[0])
        far_rows_in = dispatch(filled)
        own_result = run_experts(own_rows_in, *weights)
        far_result = run_experts(far_rows_in, *weights)
        foreign = give_back(far_result, tables[1][1]).astype(jnp.bfloat16)
        far_sum = lax.ppermute(foreign, BOTH, mirror)
        expert_sum = give_back(own_result, tables[0][1])
        expert_sum = expert_sum + far_sum.astype(jnp.float32)
    else:
        result = run_experts(dispatch(fill_slots(routed, tables[0][0])), *weights)
        expert_sum = give_back(result, tables[0][1])
    return (residual + expert_sum).astype(jnp.bfloat16)


def solution(mesh):
    placed = (
        P("seq", None),
        P(),
        P(None, "head"),
        P(None, "head"),
        P(None, "head"),
        P(),
        P(),
        P("head", None),
        P(),
        P(("seq", "head"), None),
        P(("seq", "head"), None),
        P(("seq", "head"), None, None),
        P(("seq", "head"), None, None),
        P(("seq", "head"), None, None),
    )

    return jax.shard_map(
        body, mesh=mesh, in_specs=placed, out_specs=P(("seq", "head"), None), check_vma=False
    )
```

```python
import functools

import jax
import jax.numpy as jnp
from jax import lax
from jax.experimental import pallas as pl
from jax.experimental.pallas import tpu as pltpu
from jax.sharding import PartitionSpec as P


EPSILON = 1e-06
THETA = 1000000.0
NEGATIVE = -1e30
LOG2E = 1.4426950408889634
BOTH = ("seq", "head")
VMEM = pl.BlockSpec(memory_space=pltpu.VMEM)
ANY = pl.BlockSpec(memory_space=pl.ANY)


def rms_scale(vectors, gain_vector):
    mean_sq = jnp.mean(vectors * vectors, axis=-1, keepdims=True)
    return vectors * lax.rsqrt(mean_sq + EPSILON) * gain_vector


def turn(vectors, cos_ref, sin_ref):
    half = vectors.shape[-1] // 2
    return vectors * cos_ref[...] + pltpu.roll(vectors, half, 1) * sin_ref[...]


def room(mib):
    return pltpu.CompilerParams(vmem_limit_bytes=mib * 2**20)


def first_kernel(*refs):
    hbm, (kv_ref,), held, sems = refs[:7], refs[7:8], refs[8:15], refs[15]
    x_ref, wk_ref, wv_ref, gain_ref, kgain_ref, cos_ref, sin_ref = held
    rows, head_dim = x_ref.shape[0], wk_ref.shape[1]
    half = rows // 2
    upper, lower = pl.ds(0, half), pl.ds(half, half)
    copies = [pltpu.make_async_copy(a, b, sems.at[i]) for i, (a, b) in enumerate(zip(hbm, held))]
    copies[0] = pltpu.make_async_copy(hbm[0].at[upper], x_ref.at[upper], sems.at[0])
    copies.append(pltpu.make_async_copy(hbm[0].at[lower], x_ref.at[lower], sems.at[7]))
    for i in (3, 0, 7, 1, 4, 5, 6, 2):
        copies[i].start()
    copies[3].wait()
    normed = []
    for i in (0, 7):
        copies[i].wait()
        part = x_ref[upper if i == 0 else lower, :].astype(jnp.float32)
        normed.append(rms_scale(part, gain_ref[...]).astype(jnp.bfloat16))
    normed = jnp.concatenate(normed, axis=0)
    for i in (1, 4, 5, 6):
        copies[i].wait()
    keys = jnp.dot(normed, wk_ref[...], preferred_element_type=jnp.float32)
    keys = turn(rms_scale(keys, kgain_ref[...]), cos_ref, sin_ref)
    kv_ref[:rows, :] = keys.astype(jnp.bfloat16)
    copies[2].wait()
    values = jnp.dot(normed, wv_ref[...], preferred_element_type=jnp.float32)
    for i in range(0, rows, head_dim):
        kv_ref[rows + i : rows + i + head_dim, :] = values[i : i + head_dim, :].T.astype(jnp.bfloat16)


def query_kernel(head_dim, step, x_ref, gain_ref, wq_ref, qgain_ref, cos_ref, sin_ref, q_ref):
    normed = rms_scale(x_ref[...].astype(jnp.float32), gain_ref[...]).astype(jnp.bfloat16)
    for start in range(0, wq_ref.shape[1], step):
        wide = jnp.dot(
            normed, wq_ref[:, start : start + step], preferred_element_type=jnp.float32
        )
        for i in range(0, step, head_dim):
            q_ref[:, start + i : start + i + head_dim] = turn(
                rms_scale(wide[:, i : i + head_dim], qgain_ref[...]), cos_ref, sin_ref
            ).astype(jnp.bfloat16)


def attend_kernel(head_dim, blocks, first, last, bias_ref, q_ref, *rest):
    kv_refs, rest = rest[:blocks], rest[blocks:]
    s_ref = rest[-1]
    rows, heads = q_ref.shape[0], q_ref.shape[1] // head_dim
    scale = head_dim ** (-0.5) * LOG2E

    def values(kv):
        return jnp.concatenate(
            [kv[rows + i : rows + i + head_dim, :] for i in range(0, rows, head_dim)], axis=1
        )

    def score(h):
        queries = q_ref[:, h * head_dim : (h + 1) * head_dim]
        tops = []
        for j, kv in enumerate(kv_refs):
            raw = lax.dot_general(
                kv[:rows, :],
                queries,
                (((1,), (1,)), ((), ())),
                preferred_element_type=jnp.float32,
            )
            if first and j == 0:
                key = lax.broadcasted_iota(jnp.int32, raw.shape, 0)
                asked = lax.broadcasted_iota(jnp.int32, raw.shape, 1)
                raw = jnp.where(key <= asked, raw, NEGATIVE)
            s_ref[h % 2, j * rows : (j + 1) * rows, :] = raw
            tops.append(jnp.max(raw.reshape(rows // 8, 8, rows), axis=0) + bias_ref[j])
        return jnp.max(functools.reduce(jnp.maximum, tops), axis=0, keepdims=True)

    def mix(h, row_max):
        if first:
            total = jnp.zeros((1, rows), jnp.float32)
            mixed = jnp.zeros((head_dim, rows), jnp.float32)
        else:
            old_max, old_total = rest[0][h, 0:1, :], rest[0][h, 1:2, :]
            row_max = jnp.maximum(row_max, old_max)
            shrink = jnp.exp2((old_max - row_max) * scale)
            total = old_total * shrink
            mixed = rest[1][h] * shrink
        sums = jnp.zeros((8, rows), jnp.float32)
        for j, kv in enumerate(kv_refs):
            floor = row_max - bias_ref[j]
            weights = jnp.exp2((s_ref[h % 2, j * rows : (j + 1) * rows, :] - floor) * scale)
            sums = sums + jnp.sum(weights.reshape(rows // 8, 8, rows), axis=0)
            mixed = mixed + jnp.dot(
                values(kv), weights.astype(jnp.bfloat16), preferred_element_type=jnp.float32
            )
        total = total + jnp.sum(sums, axis=0, keepdims=True)
        if last:
            rest[-2][:, h * head_dim : (h + 1) * head_dim] = (mixed / total).T.astype(jnp.bfloat16)
        else:
            rest[-3][h] = jnp.concatenate([row_max, total] + [total] * 6, axis=0)
            rest[-2][h] = mixed

    ahead = score(0)
    for h in range(heads):
        now, ahead = ahead, score(h + 1) if h + 1 < heads else None
        mix(h, now)


def attend(rot_q, head_dim, kv_blocks, bias, state, last):
    rows, wide = rot_q.shape
    heads, blocks = wide // head_dim, len(kv_blocks)
    if last:
        out_shape, out_specs = jax.ShapeDtypeStruct((rows, wide), jnp.bfloat16), VMEM
    else:
        out_shape = (
            jax.ShapeDtypeStruct((heads, 8, rows), jnp.float32),
            jax.ShapeDtypeStruct((heads, head_dim, rows), jnp.float32),
        )
        out_specs = (VMEM, VMEM)
    return pl.pallas_call(
        functools.partial(attend_kernel, head_dim, blocks, not state, last),
        out_shape=out_shape,
        in_specs=[pl.BlockSpec(memory_space=pltpu.SMEM)] + [VMEM] * (1 + blocks + len(state)),
        out_specs=out_specs,
        scratch_shapes=[pltpu.VMEM((2, blocks * rows, rows), jnp.float32)],
        compiler_params=room(max(16, 2 * blocks)),
        name="attend",
    )(jnp.stack(bias), rot_q, *kv_blocks, *state)


def expert_kernel(
    x_hbm, wg_ref, wu_hbm, wd_hbm, out_hbm, x_ref, wu_ref, wd_ref, hidden_ref, out_ref, sems
):
    rows, width = x_hbm.shape
    ins = [
        pltpu.make_async_copy(hbm, ref, sems.at[i])
        for i, (hbm, ref) in enumerate(((x_hbm, x_ref), (wu_hbm, wu_ref), (wd_hbm, wd_ref)))
    ]
    for copy in ins:
        copy.start()
    ins[0].wait()
    gate = jnp.dot(x_ref[...], wg_ref[...], preferred_element_type=jnp.float32)
    gate = gate / (1.0 + jnp.exp(-gate))
    ins[1].wait()
    up = jnp.dot(x_ref[...], wu_ref[...], preferred_element_type=jnp.float32)
    hidden_ref[...] = (gate * up).astype(jnp.bfloat16)
    ins[2].wait()
    halves = 2 if rows % 32 == 0 else 1
    half = rows // halves
    part = 512 if width % 512 == 0 else width
    outs = []
    for k in range(halves):
        for i in range(0, width, part):
            out_ref[k * half : (k + 1) * half, i : i + part] = jnp.dot(
                hidden_ref[k * half : (k + 1) * half, :],
                wd_ref[:, i : i + part],
                preferred_element_type=jnp.float32,
            ).astype(jnp.bfloat16)
        outs.append(
            pltpu.make_async_copy(
                out_ref.at[pl.ds(k * half, half)], out_hbm.at[pl.ds(k * half, half)], sems.at[3 + k]
            )
        )
        outs[-1].start()
    for copy in outs:
        copy.wait()


def run_experts(grouped, gates, w_up, w_down):
    experts, rows, width = grouped.shape
    ff = w_up.shape[2]
    held = ((rows, width), (width, ff), (ff, width), (rows, ff), (rows, width))
    made = [
        pl.pallas_call(
            expert_kernel,
            out_shape=jax.ShapeDtypeStruct((rows, width), jnp.bfloat16),
            in_specs=[ANY, VMEM, ANY, ANY],
            out_specs=ANY,
            scratch_shapes=[pltpu.VMEM(shape, jnp.bfloat16) for shape in held]
            + [pltpu.SemaphoreType.DMA((5,))],
            name="experts",
        )(
            pltpu.with_memory_space_constraint(grouped[e], pltpu.HBM), gates[e], w_up[e], w_down[e]
        )
        for e in range(experts)
    ]
    return made[0][None] if experts == 1 else jnp.stack(made)


def fill_kernel(rows_ref, pick_ref, gate_ref, out_ref):
    del gate_ref
    out_ref[...] = lax.dot_general(
        pick_ref[...], rows_ref[...], (((0,), (0,)), ((), ())), preferred_element_type=jnp.float32
    ).astype(jnp.bfloat16)


def pairs(seq_count, head_count, step):
    made = []
    for s in range(seq_count):
        for h in range(head_count):
            to = step(s, h)
            if to is not None:
                made.append((s * head_count + h, to[0] * head_count + to[1]))
    return made


def split_exact(values):
    high = values.astype(jnp.bfloat16)
    low = (values - high.astype(jnp.float32)).astype(jnp.bfloat16)
    return high, low


def body(
    tokens,
    input_gain,
    w_query,
    w_key,
    w_value,
    query_gain,
    key_gain,
    w_out,
    post_gain,
    expert_ids,
    route_weights,
    w_gate,
    w_up,
    w_down,
):
    tok_rows, width = tokens.shape
    head_dim = query_gain.shape[0]
    heads_here = w_query.shape[1] // head_dim
    seq_count = lax.axis_size("seq")
    seq_index = lax.axis_index("seq")
    head_count = lax.axis_size("head")
    head_index = lax.axis_index("head")
    side = 2 if seq_count % 2 == 0 else 1
    line = seq_count // side
    cores = 2 if head_count % 2 == 0 else 1
    towers = head_count // cores
    line_index, side_index = seq_index // side, seq_index % side
    tower_index, core_index = head_index // cores, head_index % cores
    make_pairs = functools.partial(pairs, seq_count, head_count)

    half_dim = head_dim // 2
    offset = seq_index * tok_rows
    positions = (offset + jnp.arange(tok_rows, dtype=jnp.int32)).astype(jnp.float32)
    frequency = THETA ** (-jnp.arange(half_dim, dtype=jnp.float32) * 2.0 / head_dim)
    angles = positions[:, None] * frequency[None, :]
    cosine, sine = jnp.cos(angles), jnp.sin(angles)
    cos_table = jnp.concatenate([cosine, cosine], axis=1)
    sin_table = jnp.concatenate([-sine, sine], axis=1)

    first_in = (
        tokens, w_key, w_value, input_gain[None], key_gain[None], cos_table, sin_table
    )
    own_kv = pl.pallas_call(
        first_kernel,
        out_shape=jax.ShapeDtypeStruct((2 * tok_rows, head_dim), jnp.bfloat16),
        in_specs=[ANY] * len(first_in),
        out_specs=VMEM,
        scratch_shapes=[pltpu.VMEM(x.shape, x.dtype) for x in first_in]
        + [pltpu.SemaphoreType.DMA((len(first_in) + 1,))],
        name="norm_kv",
    )(*first_in)

    kv_blocks, kv_bias = [own_kv], [jnp.float32(0.0)]
    for k in range(1, line):
        up = make_pairs(lambda s, h, k=k: ((s + k * side) % seq_count, h))
        kv_blocks.append(lax.ppermute(own_kv, BOTH, up))
        kv_bias.append(jnp.where(line_index >= k, 0.0, NEGATIVE))
    if side == 2:
        swap = make_pairs(lambda s, h: (s ^ 1, h))
        for k in range(line):
            kv_blocks.append(lax.ppermute(kv_blocks[k], BOTH, swap))
            seen = line_index >= k if k else side_index == 1
            kv_bias.append(jnp.where(seen, 0.0, NEGATIVE))

    rows_here = tok_rows // head_count
    top_count = expert_ids.shape[1]
    halves = 2 if line % 2 == 0 else 1
    local_count = w_gate.shape[0]
    experts_all = local_count * seq_count * head_count
    experts_half = experts_all // halves
    members = seq_count * head_count // halves
    capacity = max(2, 3 * rows_here * top_count // (2 * experts_all))
    slots = experts_half * capacity
    first_expert = (seq_index // (seq_count // halves)) * experts_half
    mirror = make_pairs(lambda s, h: ((line - 1 - s // side) * side + s % side, h))
    mixing = route_weights / jnp.sum(route_weights, axis=1, keepdims=True)

    def slot_tables(ids, weights, zero):
        here = first_expert + zero + jnp.arange(experts_half, dtype=jnp.int32)
        named = ids[:, :, None] == here[None, None, :]
        counts = jnp.sum(named, axis=1).astype(jnp.bfloat16)
        earlier = (
            jnp.arange(rows_here)[:, None] > jnp.arange(rows_here)[None, :]
        ).astype(jnp.bfloat16)
        rank_table = jnp.dot(earlier, counts, preferred_element_type=jnp.float32)
        mix_table = jnp.sum(jnp.where(named, weights[:, :, None], 0.0), axis=1)
        place = jnp.where(counts > 0, rank_table, -1.0).astype(jnp.int32)
        in_slot = place[:, :, None] == (zero + jnp.arange(capacity, dtype=jnp.int32))[None, None, :]
        pick = in_slot.astype(jnp.bfloat16).reshape(rows_here, slots)
        mix = jnp.where(in_slot, mix_table[:, :, None], 0.0).reshape(rows_here, slots)
        return pick, jnp.concatenate(split_exact(mix), axis=0)

    tables = [slot_tables(expert_ids, mixing, jnp.int32(0))]

    query_step = 2 * head_dim if heads_here % 2 == 0 else head_dim
    rot_q = pl.pallas_call(
        functools.partial(query_kernel, head_dim, query_step),
        out_shape=jax.ShapeDtypeStruct((tok_rows, w_query.shape[1]), jnp.bfloat16),
        in_specs=[VMEM] * 6,
        out_specs=VMEM,
        compiler_params=room(12),
        name="queries",
    )(tokens, input_gain[None], w_query, query_gain[None], cos_table, sin_table)

    near = line // 2
    if side == 2:
        parts = [
            [*range(near), *range(line, line + near - 1)],
            [*range(near, line - 1), *range(line + near - 1, line + near)],
            [line - 1, *range(line + near, 2 * line - 1)],
            [2 * line - 1],
        ]
    else:
        parts = [[*range(near)], [*range(near, line)]]
    parts = [part for part in parts if part]
    state = ()
    for n, part in enumerate(parts):
        state = attend(
            rot_q,
            head_dim,
            [kv_blocks[k] for k in part],
            [kv_bias[k] for k in part],
            state,
            n == len(parts) - 1,
        )
    attended = state

    by_tower = attended.reshape(towers, cores * rows_here, attended.shape[1])
    core_swap = make_pairs(lambda s, h: (s, h ^ 1))

    def tower_sum(k):
        rows = lax.dynamic_index_in_dim(
            by_tower, (tower_index + k) % towers, 0, keepdims=False
        )
        part = jnp.dot(rows, w_out, preferred_element_type=jnp.float32).reshape(
            cores, rows_here, width
        )
        if cores == 1:
            return part[0]
        keep = lax.dynamic_index_in_dim(part, core_index, 0, keepdims=False)
        give = lax.dynamic_index_in_dim(part, 1 - core_index, 0, keepdims=False)
        came = lax.ppermute(give.astype(jnp.bfloat16), BOTH, core_swap)
        return keep + came.astype(jnp.float32)

    attn_part = None
    for k in range(1, towers):
        shift = make_pairs(lambda s, h, k=k: (s, (h + k * cores) % head_count))
        given = tower_sum(k).astype(jnp.bfloat16)
        came = lax.ppermute(given, BOTH, shift).astype(jnp.float32)
        attn_part = came if attn_part is None else attn_part + came
    own_sum = tower_sum(0)
    attn_part = own_sum if attn_part is None else own_sum + attn_part

    own_rows = lax.dynamic_slice_in_dim(tokens, head_index * rows_here, rows_here, 0)
    residual = own_rows.astype(jnp.float32) + attn_part
    routed = rms_scale(residual, post_gain).astype(jnp.bfloat16)

    groups = [list(range(g * members, (g + 1) * members)) for g in range(halves)]

    def exchange(rows):
        return lax.all_to_all(
            rows.reshape(members, local_count * capacity, width),
            BOTH,
            split_axis=0,
            concat_axis=0,
            axis_index_groups=groups,
            tiled=True,
        )

    def dispatch(outgoing):
        return (
            exchange(outgoing)
            .reshape(members, local_count, capacity, width)
            .transpose(1, 0, 2, 3)
            .reshape(local_count, members * capacity, width)
        )

    def fill_slots(rows, pick):
        return lax.dot_general(
            pick, rows, (((0,), (0,)), ((), ())), preferred_element_type=jnp.float32
        ).astype(jnp.bfloat16)

    def give_back(result, mix):
        came = exchange(
            result.reshape(local_count, members, capacity, width).transpose(1, 0, 2, 3)
        ).reshape(slots, width)
        both = jnp.dot(mix, came, preferred_element_type=jnp.float32)
        return both[:rows_here] + both[rows_here:]

    gates = [pltpu.with_memory_space_constraint(w_gate[e], pltpu.VMEM) for e in range(local_count)]
    weights = (gates, w_up, w_down)
    if halves == 2:
        mirrored = lax.ppermute(routed, BOTH, mirror)
        own_rows_in = dispatch(fill_slots(routed, tables[0][0]))
        sent = jnp.concatenate([expert_ids.astype(jnp.float32), mixing], axis=1)
        seen = lax.ppermute(sent, BOTH, mirror)
        tables.append(
            slot_tables(
                seen[:, :top_count].astype(jnp.int32),
                seen[:, top_count:],
                lax.optimization_barrier(jnp.int32(0)),
            )
        )
        filled = pl.pallas_call(
            fill_kernel,
            out_shape=jax.ShapeDtypeStruct((slots, width), jnp.bfloat16),
            in_specs=[VMEM] * 3,
            out_specs=VMEM,
            name="fill",
        )(mirrored, tables[1][0], gates[0])
        far_rows_in = dispatch(filled)
        own_result = run_experts(own_rows_in, *weights)
        far_result = run_experts(far_rows_in, *weights)
        foreign = give_back(far_result, tables[1][1]).astype(jnp.bfloat16)
        far_sum = lax.ppermute(foreign, BOTH, mirror)
        expert_sum = give_back(own_result, tables[0][1])
        expert_sum = expert_sum + far_sum.astype(jnp.float32)
    else:
        result = run_experts(dispatch(fill_slots(routed, tables[0][0])), *weights)
        expert_sum = give_back(result, tables[0][1])
    return (residual + expert_sum).astype(jnp.bfloat16)


def solution(mesh):
    placed = (
        P("seq", None),
        P(),
        P(None, "head"),
        P(None, "head"),
        P(None, "head"),
        P(),
        P(),
        P("head", None),
        P(),
        P(("seq", "head"), None),
        P(("seq", "head"), None),
        P(("seq", "head"), None, None),
        P(("seq", "head"), None, None),
        P(("seq", "head"), None, None),
    )

    return jax.shard_map(
        body, mesh=mesh, in_specs=placed, out_specs=P(("seq", "head"), None), check_vma=False
    )
```

```python
import functools

import jax
import jax.numpy as jnp
import numpy as np
from jax import lax
from jax.experimental import pallas as pl
from jax.experimental.pallas import tpu as pltpu
from jax.sharding import PartitionSpec as P


EPSILON = 1e-06
THETA = 1000000.0
NEGATIVE = -1e30
LOG2E = 1.4426950408889634
BOTH = ("seq", "head")
VMEM = pl.BlockSpec(memory_space=pltpu.VMEM)
ANY = pl.BlockSpec(memory_space=pl.ANY)


def rms_scale(vectors, gain_vector):
    mean_sq = jnp.mean(vectors * vectors, axis=-1, keepdims=True)
    return vectors * lax.rsqrt(mean_sq + EPSILON) * gain_vector


def spread(table):
    half = table.shape[-1] // 2
    turned = pltpu.roll(table, half, 1)
    front = lax.broadcasted_iota(jnp.int32, table.shape, 1) < half
    return jnp.where(front, table, turned), jnp.where(front, -turned, table)


def turn(vectors, cosine, sine):
    return vectors * cosine + pltpu.roll(vectors, vectors.shape[-1] // 2, 1) * sine


def room(mib):
    return pltpu.CompilerParams(vmem_limit_bytes=mib * 2**20)


def first_kernel(*refs):
    hbm, kv_ref, held, sems = refs[:6], refs[6], refs[7:13], refs[13]
    x_ref, wk_ref, wv_ref, gain_ref, kgain_ref, table_ref = held
    rows, head_dim = x_ref.shape[0], wk_ref.shape[1]
    half = rows // 2
    upper, lower = pl.ds(0, half), pl.ds(half, half)
    mine = pl.ds(pl.multiple_of(lax.axis_index("seq") * rows, rows), rows)
    pieces = [
        (hbm[0].at[upper], x_ref.at[upper]),
        *zip(hbm[1:5], held[1:5]),
        (hbm[5].at[mine], table_ref),
        (hbm[0].at[lower], x_ref.at[lower]),
    ]
    copies = [pltpu.make_async_copy(a, b, sems.at[i]) for i, (a, b) in enumerate(pieces)]
    for i in (3, 0, 6, 1, 4, 5, 2):
        copies[i].start()
    copies[3].wait()
    normed = []
    for i in (0, 6):
        copies[i].wait()
        part = x_ref[upper if i == 0 else lower, :].astype(jnp.float32)
        normed.append(rms_scale(part, gain_ref[...]).astype(jnp.bfloat16))
    normed = jnp.concatenate(normed, axis=0)
    for i in (1, 4, 5):
        copies[i].wait()
    keys = jnp.dot(normed, wk_ref[...], preferred_element_type=jnp.float32)
    keys = turn(rms_scale(keys, kgain_ref[...]), *spread(table_ref[...]))
    kv_ref[:rows, :] = keys.astype(jnp.bfloat16)
    copies[2].wait()
    values = jnp.dot(normed, wv_ref[...], preferred_element_type=jnp.float32)
    for i in range(0, rows, head_dim):
        kv_ref[rows + i : rows + i + head_dim, :] = values[i : i + head_dim, :].T.astype(jnp.bfloat16)


def query_kernel(head_dim, step, x_ref, gain_ref, wq_ref, qgain_ref, table_ref, q_ref):
    rows = x_ref.shape[0]
    mine = pl.ds(pl.multiple_of(lax.axis_index("seq") * rows, rows), rows)
    cosine, sine = spread(table_ref[mine, :])
    normed = rms_scale(x_ref[...].astype(jnp.float32), gain_ref[...]).astype(jnp.bfloat16)
    for start in range(0, wq_ref.shape[1], step):
        wide = jnp.dot(
            normed, wq_ref[:, start : start + step], preferred_element_type=jnp.float32
        )
        for i in range(0, step, head_dim):
            q_ref[:, start + i : start + i + head_dim] = turn(
                rms_scale(wide[:, i : i + head_dim], qgain_ref[...]), cosine, sine
            ).astype(jnp.bfloat16)


def attend_kernel(head_dim, blocks, first, last, bias_ref, q_ref, *rest):
    kv_refs, rest = rest[:blocks], rest[blocks:]
    s_ref = rest[-1]
    rows, heads = q_ref.shape[0], q_ref.shape[1] // head_dim
    scale = head_dim ** (-0.5) * LOG2E

    def values(kv):
        return jnp.concatenate(
            [kv[rows + i : rows + i + head_dim, :] for i in range(0, rows, head_dim)], axis=1
        )

    def score(h):
        queries = q_ref[:, h * head_dim : (h + 1) * head_dim]
        tops = []
        for j, kv in enumerate(kv_refs):
            raw = lax.dot_general(
                kv[:rows, :],
                queries,
                (((1,), (1,)), ((), ())),
                preferred_element_type=jnp.float32,
            )
            if first and j == 0:
                key = lax.broadcasted_iota(jnp.int32, raw.shape, 0)
                asked = lax.broadcasted_iota(jnp.int32, raw.shape, 1)
                raw = jnp.where(key <= asked, raw, NEGATIVE)
            s_ref[h % 2, j * rows : (j + 1) * rows, :] = raw
            tops.append(jnp.max(raw.reshape(rows // 8, 8, rows), axis=0) + bias_ref[j])
        return jnp.max(functools.reduce(jnp.maximum, tops), axis=0, keepdims=True)

    def mix(h, row_max):
        if first:
            total = jnp.zeros((1, rows), jnp.float32)
            mixed = jnp.zeros((head_dim, rows), jnp.float32)
        else:
            old_max, old_total = rest[0][h, 0:1, :], rest[0][h, 1:2, :]
            row_max = jnp.maximum(row_max, old_max)
            shrink = jnp.exp2((old_max - row_max) * scale)
            total = old_total * shrink
            mixed = rest[1][h] * shrink
        sums = jnp.zeros((8, rows), jnp.float32)
        for j, kv in enumerate(kv_refs):
            floor = row_max - bias_ref[j]
            weights = jnp.exp2((s_ref[h % 2, j * rows : (j + 1) * rows, :] - floor) * scale)
            sums = sums + jnp.sum(weights.reshape(rows // 8, 8, rows), axis=0)
            mixed = mixed + jnp.dot(
                values(kv), weights.astype(jnp.bfloat16), preferred_element_type=jnp.float32
            )
        total = total + jnp.sum(sums, axis=0, keepdims=True)
        if last:
            rest[-2][:, h * head_dim : (h + 1) * head_dim] = (mixed / total).T.astype(jnp.bfloat16)
        else:
            rest[-3][h] = jnp.concatenate([row_max, total] + [total] * 6, axis=0)
            rest[-2][h] = mixed

    ahead = score(0)
    for h in range(heads):
        now, ahead = ahead, score(h + 1) if h + 1 < heads else None
        mix(h, now)


def attend(rot_q, head_dim, kv_blocks, bias, state, last):
    rows, wide = rot_q.shape
    heads, blocks = wide // head_dim, len(kv_blocks)
    if last:
        out_shape, out_specs = jax.ShapeDtypeStruct((rows, wide), jnp.bfloat16), VMEM
    else:
        out_shape = (
            jax.ShapeDtypeStruct((heads, 8, rows), jnp.float32),
            jax.ShapeDtypeStruct((heads, head_dim, rows), jnp.float32),
        )
        out_specs = (VMEM, VMEM)
    return pl.pallas_call(
        functools.partial(attend_kernel, head_dim, blocks, not state, last),
        out_shape=out_shape,
        in_specs=[pl.BlockSpec(memory_space=pltpu.SMEM)] + [VMEM] * (1 + blocks + len(state)),
        out_specs=out_specs,
        scratch_shapes=[pltpu.VMEM((2, blocks * rows, rows), jnp.float32)],
        compiler_params=room(max(16, 2 * blocks)),
        name="attend",
    )(jnp.stack(bias), rot_q, *kv_blocks, *state)


def expert_kernel(
    x_hbm, wg_ref, wu_hbm, wd_hbm, out_hbm, x_ref, wu_ref, wd_ref, hidden_ref, out_ref, sems
):
    rows, width = x_hbm.shape
    ins = [
        pltpu.make_async_copy(hbm, ref, sems.at[i])
        for i, (hbm, ref) in enumerate(((x_hbm, x_ref), (wu_hbm, wu_ref), (wd_hbm, wd_ref)))
    ]
    for copy in ins:
        copy.start()
    ins[0].wait()
    gate = jnp.dot(x_ref[...], wg_ref[...], preferred_element_type=jnp.float32)
    gate = gate / (1.0 + jnp.exp(-gate))
    ins[1].wait()
    up = jnp.dot(x_ref[...], wu_ref[...], preferred_element_type=jnp.float32)
    hidden_ref[...] = (gate * up).astype(jnp.bfloat16)
    ins[2].wait()
    halves = 2 if rows % 32 == 0 else 1
    half = rows // halves
    part = 512 if width % 512 == 0 else width
    outs = []
    for k in range(halves):
        for i in range(0, width, part):
            out_ref[k * half : (k + 1) * half, i : i + part] = jnp.dot(
                hidden_ref[k * half : (k + 1) * half, :],
                wd_ref[:, i : i + part],
                preferred_element_type=jnp.float32,
            ).astype(jnp.bfloat16)
        outs.append(
            pltpu.make_async_copy(
                out_ref.at[pl.ds(k * half, half)], out_hbm.at[pl.ds(k * half, half)], sems.at[3 + k]
            )
        )
        outs[-1].start()
    for copy in outs:
        copy.wait()


def run_experts(grouped, gates, w_up, w_down):
    experts, rows, width = grouped.shape
    ff = w_up.shape[2]
    held = ((rows, width), (width, ff), (ff, width), (rows, ff), (rows, width))
    made = [
        pl.pallas_call(
            expert_kernel,
            out_shape=jax.ShapeDtypeStruct((rows, width), jnp.bfloat16),
            in_specs=[ANY, VMEM, ANY, ANY],
            out_specs=ANY,
            scratch_shapes=[pltpu.VMEM(shape, jnp.bfloat16) for shape in held]
            + [pltpu.SemaphoreType.DMA((5,))],
            name="experts",
        )(
            pltpu.with_memory_space_constraint(grouped[e], pltpu.HBM), gates[e], w_up[e], w_down[e]
        )
        for e in range(experts)
    ]
    return made[0][None] if experts == 1 else jnp.stack(made)


def fill_kernel(rows_ref, pick_ref, gate_ref, out_ref):
    del gate_ref
    out_ref[...] = lax.dot_general(
        pick_ref[...], rows_ref[...], (((0,), (0,)), ((), ())), preferred_element_type=jnp.float32
    ).astype(jnp.bfloat16)


def pairs(seq_count, head_count, step):
    made = []
    for s in range(seq_count):
        for h in range(head_count):
            to = step(s, h)
            if to is not None:
                made.append((s * head_count + h, to[0] * head_count + to[1]))
    return made


def split_exact(values):
    high = values.astype(jnp.bfloat16)
    low = (values - high.astype(jnp.float32)).astype(jnp.bfloat16)
    return high, low


def body(
    tokens,
    input_gain,
    w_query,
    w_key,
    w_value,
    query_gain,
    key_gain,
    w_out,
    post_gain,
    expert_ids,
    route_weights,
    w_gate,
    w_up,
    w_down,
):
    tok_rows, width = tokens.shape
    head_dim = query_gain.shape[0]
    heads_here = w_query.shape[1] // head_dim
    seq_count = lax.axis_size("seq")
    seq_index = lax.axis_index("seq")
    head_count = lax.axis_size("head")
    head_index = lax.axis_index("head")
    side = 2 if seq_count % 2 == 0 else 1
    line = seq_count // side
    cores = 2 if head_count % 2 == 0 else 1
    towers = head_count // cores
    line_index, side_index = seq_index // side, seq_index % side
    tower_index, core_index = head_index // cores, head_index % cores
    make_pairs = functools.partial(pairs, seq_count, head_count)

    half_dim = head_dim // 2
    places = np.arange(seq_count * tok_rows, dtype=np.float32)
    frequency = np.float32(THETA) ** (
        -np.arange(half_dim, dtype=np.float32) * np.float32(2.0) / np.float32(head_dim)
    )
    angles = (places[:, None] * frequency[None, :]).astype(np.float64)
    table = jnp.asarray(np.concatenate([np.cos(angles), np.sin(angles)], axis=1), jnp.float32)

    first_in = (tokens, w_key, w_value, input_gain[None], key_gain[None], table)
    own_kv = pl.pallas_call(
        first_kernel,
        out_shape=jax.ShapeDtypeStruct((2 * tok_rows, head_dim), jnp.bfloat16),
        in_specs=[ANY] * len(first_in),
        out_specs=VMEM,
        scratch_shapes=[pltpu.VMEM(x.shape, x.dtype) for x in first_in[:-1]]
        + [pltpu.VMEM((tok_rows, head_dim), jnp.float32)]
        + [pltpu.SemaphoreType.DMA((len(first_in) + 1,))],
        name="norm_kv",
    )(*first_in)

    kv_blocks, kv_bias = [own_kv], [jnp.float32(0.0)]
    for k in range(1, line):
        up = make_pairs(lambda s, h, k=k: ((s + k * side) % seq_count, h))
        kv_blocks.append(lax.ppermute(own_kv, BOTH, up))
        kv_bias.append(jnp.where(line_index >= k, 0.0, NEGATIVE))
    if side == 2:
        swap = make_pairs(lambda s, h: (s ^ 1, h))
        for k in range(line):
            kv_blocks.append(lax.ppermute(kv_blocks[k], BOTH, swap))
            seen = line_index >= k if k else side_index == 1
            kv_bias.append(jnp.where(seen, 0.0, NEGATIVE))

    rows_here = tok_rows // head_count
    top_count = expert_ids.shape[1]
    halves = 2 if line % 2 == 0 else 1
    local_count = w_gate.shape[0]
    experts_all = local_count * seq_count * head_count
    experts_half = experts_all // halves
    members = seq_count * head_count // halves
    capacity = max(2, 3 * rows_here * top_count // (2 * experts_all))
    slots = experts_half * capacity
    first_expert = (seq_index // (seq_count // halves)) * experts_half
    mirror = make_pairs(lambda s, h: ((line - 1 - s // side) * side + s % side, h))
    mixing = route_weights / jnp.sum(route_weights, axis=1, keepdims=True)

    def slot_tables(ids, weights, zero):
        here = first_expert + zero + jnp.arange(experts_half, dtype=jnp.int32)
        named = ids[:, :, None] == here[None, None, :]
        counts = jnp.sum(named, axis=1).astype(jnp.bfloat16)
        earlier = (
            jnp.arange(rows_here)[:, None] > jnp.arange(rows_here)[None, :]
        ).astype(jnp.bfloat16)
        rank_table = jnp.dot(earlier, counts, preferred_element_type=jnp.float32)
        mix_table = jnp.sum(jnp.where(named, weights[:, :, None], 0.0), axis=1)
        place = jnp.where(counts > 0, rank_table, -1.0).astype(jnp.int32)
        in_slot = place[:, :, None] == (zero + jnp.arange(capacity, dtype=jnp.int32))[None, None, :]
        pick = in_slot.astype(jnp.bfloat16).reshape(rows_here, slots)
        mix = jnp.where(in_slot, mix_table[:, :, None], 0.0).reshape(rows_here, slots)
        return pick, jnp.concatenate(split_exact(mix), axis=0)

    tables = [slot_tables(expert_ids, mixing, jnp.int32(0))]

    query_step = 2 * head_dim if heads_here % 2 == 0 else head_dim
    rot_q = pl.pallas_call(
        functools.partial(query_kernel, head_dim, query_step),
        out_shape=jax.ShapeDtypeStruct((tok_rows, w_query.shape[1]), jnp.bfloat16),
        in_specs=[VMEM] * 5,
        out_specs=VMEM,
        compiler_params=room(16),
        name="queries",
    )(tokens, input_gain[None], w_query, query_gain[None], table)

    near = line // 2
    if side == 2:
        parts = [
            [*range(near), *range(line, line + near - 1)],
            [*range(near, line - 1), *range(line + near - 1, line + near)],
            [line - 1, *range(line + near, 2 * line - 1)],
            [2 * line - 1],
        ]
    else:
        parts = [[*range(near)], [*range(near, line)]]
    parts = [part for part in parts if part]
    state = ()
    for n, part in enumerate(parts):
        state = attend(
            rot_q,
            head_dim,
            [kv_blocks[k] for k in part],
            [kv_bias[k] for k in part],
            state,
            n == len(parts) - 1,
        )
    attended = state

    by_tower = attended.reshape(towers, cores * rows_here, attended.shape[1])
    core_swap = make_pairs(lambda s, h: (s, h ^ 1))

    def tower_sum(k):
        rows = lax.dynamic_index_in_dim(
            by_tower, (tower_index + k) % towers, 0, keepdims=False
        )
        part = jnp.dot(rows, w_out, preferred_element_type=jnp.float32).reshape(
            cores, rows_here, width
        )
        if cores == 1:
            return part[0]
        keep = lax.dynamic_index_in_dim(part, core_index, 0, keepdims=False)
        give = lax.dynamic_index_in_dim(part, 1 - core_index, 0, keepdims=False)
        came = lax.ppermute(give.astype(jnp.bfloat16), BOTH, core_swap)
        return keep + came.astype(jnp.float32)

    attn_part = None
    for k in range(1, towers):
        shift = make_pairs(lambda s, h, k=k: (s, (h + k * cores) % head_count))
        given = tower_sum(k).astype(jnp.bfloat16)
        came = lax.ppermute(given, BOTH, shift).astype(jnp.float32)
        attn_part = came if attn_part is None else attn_part + came
    own_sum = tower_sum(0)
    attn_part = own_sum if attn_part is None else own_sum + attn_part

    own_rows = lax.dynamic_slice_in_dim(tokens, head_index * rows_here, rows_here, 0)
    residual = own_rows.astype(jnp.float32) + attn_part
    routed = rms_scale(residual, post_gain).astype(jnp.bfloat16)

    groups = [list(range(g * members, (g + 1) * members)) for g in range(halves)]

    def exchange(rows):
        return lax.all_to_all(
            rows.reshape(members, local_count * capacity, width),
            BOTH,
            split_axis=0,
            concat_axis=0,
            axis_index_groups=groups,
            tiled=True,
        )

    def dispatch(outgoing):
        return (
            exchange(outgoing)
            .reshape(members, local_count, capacity, width)
            .transpose(1, 0, 2, 3)
            .reshape(local_count, members * capacity, width)
        )

    def fill_slots(rows, pick):
        return lax.dot_general(
            pick, rows, (((0,), (0,)), ((), ())), preferred_element_type=jnp.float32
        ).astype(jnp.bfloat16)

    def give_back(result, mix):
        came = exchange(
            result.reshape(local_count, members, capacity, width).transpose(1, 0, 2, 3)
        ).reshape(slots, width)
        both = jnp.dot(mix, came, preferred_element_type=jnp.float32)
        return both[:rows_here] + both[rows_here:]

    gates = [pltpu.with_memory_space_constraint(w_gate[e], pltpu.VMEM) for e in range(local_count)]
    weights = (gates, w_up, w_down)
    if halves == 2:
        mirrored = lax.ppermute(routed, BOTH, mirror)
        own_rows_in = dispatch(fill_slots(routed, tables[0][0]))
        sent = jnp.concatenate([expert_ids.astype(jnp.float32), mixing], axis=1)
        seen = lax.ppermute(sent, BOTH, mirror)
        tables.append(
            slot_tables(
                seen[:, :top_count].astype(jnp.int32),
                seen[:, top_count:],
                lax.optimization_barrier(jnp.int32(0)),
            )
        )
        filled = pl.pallas_call(
            fill_kernel,
            out_shape=jax.ShapeDtypeStruct((slots, width), jnp.bfloat16),
            in_specs=[VMEM] * 3,
            out_specs=VMEM,
            name="fill",
        )(mirrored, tables[1][0], gates[0])
        far_rows_in = dispatch(filled)
        own_result = run_experts(own_rows_in, *weights)
        far_result = run_experts(far_rows_in, *weights)
        foreign = give_back(far_result, tables[1][1]).astype(jnp.bfloat16)
        far_sum = lax.ppermute(foreign, BOTH, mirror)
        expert_sum = give_back(own_result, tables[0][1])
        expert_sum = expert_sum + far_sum.astype(jnp.float32)
    else:
        result = run_experts(dispatch(fill_slots(routed, tables[0][0])), *weights)
        expert_sum = give_back(result, tables[0][1])
    return (residual + expert_sum).astype(jnp.bfloat16)


def solution(mesh):
    placed = (
        P("seq", None),
        P(),
        P(None, "head"),
        P(None, "head"),
        P(None, "head"),
        P(),
        P(),
        P("head", None),
        P(),
        P(("seq", "head"), None),
        P(("seq", "head"), None),
        P(("seq", "head"), None, None),
        P(("seq", "head"), None, None),
        P(("seq", "head"), None, None),
    )

    return jax.shard_map(
        body, mesh=mesh, in_specs=placed, out_specs=P(("seq", "head"), None), check_vma=False
    )
```

```python
import functools

import jax
import jax.numpy as jnp
import numpy as np
from jax import lax
from jax.experimental import pallas as pl
from jax.experimental.pallas import tpu as pltpu
from jax.sharding import PartitionSpec as P


EPSILON = 1e-06
THETA = 1000000.0
NEGATIVE = -1e30
LOG2E = 1.4426950408889634
BOTH = ("seq", "head")
VMEM = pl.BlockSpec(memory_space=pltpu.VMEM)
ANY = pl.BlockSpec(memory_space=pl.ANY)


def rms_scale(vectors, gain_vector):
    mean_sq = jnp.mean(vectors * vectors, axis=-1, keepdims=True)
    return vectors * lax.rsqrt(mean_sq + EPSILON) * gain_vector


def spread(table):
    half = table.shape[-1] // 2
    turned = pltpu.roll(table, half, 1)
    front = lax.broadcasted_iota(jnp.int32, table.shape, 1) < half
    return jnp.where(front, table, turned), jnp.where(front, -turned, table)


def turn(vectors, cosine, sine):
    return vectors * cosine + pltpu.roll(vectors, vectors.shape[-1] // 2, 1) * sine


def room(mib):
    return pltpu.CompilerParams(vmem_limit_bytes=mib * 2**20)


def first_kernel(*refs):
    hbm, kv_ref, held, sems = refs[:6], refs[6], refs[7:13], refs[13]
    x_ref, wk_ref, wv_ref, gain_ref, kgain_ref, table_ref = held
    rows, head_dim = x_ref.shape[0], wk_ref.shape[1]
    half = rows // 2
    upper, lower = pl.ds(0, half), pl.ds(half, half)
    mine = pl.ds(pl.multiple_of(lax.axis_index("seq") * rows, rows), rows)
    pieces = [
        (hbm[0].at[upper], x_ref.at[upper]),
        *zip(hbm[1:5], held[1:5]),
        (hbm[5].at[mine], table_ref),
        (hbm[0].at[lower], x_ref.at[lower]),
    ]
    copies = [pltpu.make_async_copy(a, b, sems.at[i]) for i, (a, b) in enumerate(pieces)]
    for i in (3, 0, 6, 1, 4, 5, 2):
        copies[i].start()
    copies[3].wait()
    normed = []
    for i in (0, 6):
        copies[i].wait()
        part = x_ref[upper if i == 0 else lower, :].astype(jnp.float32)
        normed.append(rms_scale(part, gain_ref[...]).astype(jnp.bfloat16))
    normed = jnp.concatenate(normed, axis=0)
    for i in (1, 4, 5):
        copies[i].wait()
    keys = jnp.dot(normed, wk_ref[...], preferred_element_type=jnp.float32)
    keys = turn(rms_scale(keys, kgain_ref[...]), *spread(table_ref[...]))
    kv_ref[:rows, :] = keys.astype(jnp.bfloat16)
    copies[2].wait()
    values = jnp.dot(normed, wv_ref[...], preferred_element_type=jnp.float32)
    for i in range(0, rows, head_dim):
        kv_ref[rows + i : rows + i + head_dim, :] = values[i : i + head_dim, :].T.astype(jnp.bfloat16)


def query_kernel(head_dim, step, x_ref, gain_ref, wq_ref, qgain_ref, table_ref, q_ref):
    rows = x_ref.shape[0]
    mine = pl.ds(pl.multiple_of(lax.axis_index("seq") * rows, rows), rows)
    cosine, sine = spread(table_ref[mine, :])
    normed = rms_scale(x_ref[...].astype(jnp.float32), gain_ref[...]).astype(jnp.bfloat16)
    for start in range(0, wq_ref.shape[1], step):
        wide = jnp.dot(
            normed, wq_ref[:, start : start + step], preferred_element_type=jnp.float32
        )
        for i in range(0, step, head_dim):
            q_ref[:, start + i : start + i + head_dim] = turn(
                rms_scale(wide[:, i : i + head_dim], qgain_ref[...]), cosine, sine
            ).astype(jnp.bfloat16)


def attend_kernel(head_dim, blocks, first, last, bias_ref, q_ref, *rest):
    kv_refs, rest = rest[:blocks], rest[blocks:]
    s_ref = rest[-1]
    rows, heads = q_ref.shape[0], q_ref.shape[1] // head_dim
    scale = head_dim ** (-0.5) * LOG2E

    def values(kv):
        return jnp.concatenate(
            [kv[rows + i : rows + i + head_dim, :] for i in range(0, rows, head_dim)], axis=1
        )

    def score(h):
        queries = q_ref[:, h * head_dim : (h + 1) * head_dim]
        tops = []
        for j, kv in enumerate(kv_refs):
            raw = lax.dot_general(
                kv[:rows, :],
                queries,
                (((1,), (1,)), ((), ())),
                preferred_element_type=jnp.float32,
            )
            if first and j == 0:
                key = lax.broadcasted_iota(jnp.int32, raw.shape, 0)
                asked = lax.broadcasted_iota(jnp.int32, raw.shape, 1)
                raw = jnp.where(key <= asked, raw, NEGATIVE)
            s_ref[h % 2, j * rows : (j + 1) * rows, :] = raw
            tops.append(jnp.max(raw.reshape(rows // 8, 8, rows), axis=0) + bias_ref[j])
        return jnp.max(functools.reduce(jnp.maximum, tops), axis=0, keepdims=True)

    def mix(h, row_max):
        if first:
            total = jnp.zeros((1, rows), jnp.float32)
            mixed = jnp.zeros((head_dim, rows), jnp.float32)
        else:
            old_max, old_total = rest[0][h, 0:1, :], rest[0][h, 1:2, :]
            row_max = jnp.maximum(row_max, old_max)
            shrink = jnp.exp2((old_max - row_max) * scale)
            total = old_total * shrink
            mixed = rest[1][h] * shrink
        sums = jnp.zeros((8, rows), jnp.float32)
        for j, kv in enumerate(kv_refs):
            floor = row_max - bias_ref[j]
            weights = jnp.exp2((s_ref[h % 2, j * rows : (j + 1) * rows, :] - floor) * scale)
            sums = sums + jnp.sum(weights.reshape(rows // 8, 8, rows), axis=0)
            mixed = mixed + jnp.dot(
                values(kv), weights.astype(jnp.bfloat16), preferred_element_type=jnp.float32
            )
        total = total + jnp.sum(sums, axis=0, keepdims=True)
        if last:
            rest[-2][:, h * head_dim : (h + 1) * head_dim] = (mixed / total).T.astype(jnp.bfloat16)
        else:
            rest[-3][h] = jnp.concatenate([row_max, total] + [total] * 6, axis=0)
            rest[-2][h] = mixed

    ahead = score(0)
    for h in range(heads):
        now, ahead = ahead, score(h + 1) if h + 1 < heads else None
        mix(h, now)


def attend(rot_q, head_dim, kv_blocks, bias, state, last):
    rows, wide = rot_q.shape
    heads, blocks = wide // head_dim, len(kv_blocks)
    if last:
        out_shape, out_specs = jax.ShapeDtypeStruct((rows, wide), jnp.bfloat16), VMEM
    else:
        out_shape = (
            jax.ShapeDtypeStruct((heads, 8, rows), jnp.float32),
            jax.ShapeDtypeStruct((heads, head_dim, rows), jnp.float32),
        )
        out_specs = (VMEM, VMEM)
    return pl.pallas_call(
        functools.partial(attend_kernel, head_dim, blocks, not state, last),
        out_shape=out_shape,
        in_specs=[pl.BlockSpec(memory_space=pltpu.SMEM)] + [VMEM] * (1 + blocks + len(state)),
        out_specs=out_specs,
        scratch_shapes=[pltpu.VMEM((2, blocks * rows, rows), jnp.float32)],
        compiler_params=room(max(16, 2 * blocks)),
        name="attend",
    )(jnp.stack(bias), rot_q, *kv_blocks, *state)


def expert_kernel(
    x_hbm, wg_ref, wu_hbm, wd_hbm, out_hbm, x_ref, wu_ref, wd_ref, hidden_ref, out_ref, sems
):
    rows, width = x_hbm.shape
    ins = [
        pltpu.make_async_copy(hbm, ref, sems.at[i])
        for i, (hbm, ref) in enumerate(((x_hbm, x_ref), (wu_hbm, wu_ref), (wd_hbm, wd_ref)))
    ]
    for copy in ins:
        copy.start()
    ins[0].wait()
    gate = jnp.dot(x_ref[...], wg_ref[...], preferred_element_type=jnp.float32)
    gate = gate / (1.0 + jnp.exp(-gate))
    ins[1].wait()
    up = jnp.dot(x_ref[...], wu_ref[...], preferred_element_type=jnp.float32)
    hidden_ref[...] = (gate * up).astype(jnp.bfloat16)
    ins[2].wait()
    halves = 2 if rows % 32 == 0 else 1
    half = rows // halves
    part = 512 if width % 512 == 0 else width
    outs = []
    for k in range(halves):
        for i in range(0, width, part):
            out_ref[k * half : (k + 1) * half, i : i + part] = jnp.dot(
                hidden_ref[k * half : (k + 1) * half, :],
                wd_ref[:, i : i + part],
                preferred_element_type=jnp.float32,
            ).astype(jnp.bfloat16)
        outs.append(
            pltpu.make_async_copy(
                out_ref.at[pl.ds(k * half, half)], out_hbm.at[pl.ds(k * half, half)], sems.at[3 + k]
            )
        )
        outs[-1].start()
    for copy in outs:
        copy.wait()


def run_experts(grouped, gates, w_up, w_down):
    experts, rows, width = grouped.shape
    ff = w_up.shape[2]
    held = ((rows, width), (width, ff), (ff, width), (rows, ff), (rows, width))
    made = [
        pl.pallas_call(
            expert_kernel,
            out_shape=jax.ShapeDtypeStruct((rows, width), jnp.bfloat16),
            in_specs=[ANY, VMEM, ANY, ANY],
            out_specs=ANY,
            scratch_shapes=[pltpu.VMEM(shape, jnp.bfloat16) for shape in held]
            + [pltpu.SemaphoreType.DMA((5,))],
            name="experts",
        )(
            pltpu.with_memory_space_constraint(grouped[e], pltpu.HBM), gates[e], w_up[e], w_down[e]
        )
        for e in range(experts)
    ]
    return made[0][None] if experts == 1 else jnp.stack(made)


def finish_kernel(mix_ref, came_ref, far_ref, residual_ref, out_ref):
    rows = residual_ref.shape[0]
    both = jnp.dot(mix_ref[...], came_ref[...], preferred_element_type=jnp.float32)
    expert_sum = both[:rows] + both[rows:] + far_ref[...].astype(jnp.float32)
    out_ref[...] = (residual_ref[...] + expert_sum).astype(jnp.bfloat16)


def fill_kernel(rows_ref, pick_ref, gate_ref, out_ref):
    del gate_ref
    out_ref[...] = lax.dot_general(
        pick_ref[...], rows_ref[...], (((0,), (0,)), ((), ())), preferred_element_type=jnp.float32
    ).astype(jnp.bfloat16)


def pairs(seq_count, head_count, step):
    made = []
    for s in range(seq_count):
        for h in range(head_count):
            to = step(s, h)
            if to is not None:
                made.append((s * head_count + h, to[0] * head_count + to[1]))
    return made


def split_exact(values):
    high = values.astype(jnp.bfloat16)
    low = (values - high.astype(jnp.float32)).astype(jnp.bfloat16)
    return high, low


def body(
    tokens,
    input_gain,
    w_query,
    w_key,
    w_value,
    query_gain,
    key_gain,
    w_out,
    post_gain,
    expert_ids,
    route_weights,
    w_gate,
    w_up,
    w_down,
):
    tok_rows, width = tokens.shape
    head_dim = query_gain.shape[0]
    heads_here = w_query.shape[1] // head_dim
    seq_count = lax.axis_size("seq")
    seq_index = lax.axis_index("seq")
    head_count = lax.axis_size("head")
    head_index = lax.axis_index("head")
    side = 2 if seq_count % 2 == 0 else 1
    line = seq_count // side
    cores = 2 if head_count % 2 == 0 else 1
    towers = head_count // cores
    line_index, side_index = seq_index // side, seq_index % side
    tower_index, core_index = head_index // cores, head_index % cores
    make_pairs = functools.partial(pairs, seq_count, head_count)

    half_dim = head_dim // 2
    places = np.arange(seq_count * tok_rows, dtype=np.float32)
    frequency = np.float32(THETA) ** (
        -np.arange(half_dim, dtype=np.float32) * np.float32(2.0) / np.float32(head_dim)
    )
    angles = (places[:, None] * frequency[None, :]).astype(np.float64)
    table = jnp.asarray(np.concatenate([np.cos(angles), np.sin(angles)], axis=1), jnp.float32)

    first_in = (tokens, w_key, w_value, input_gain[None], key_gain[None], table)
    own_kv = pl.pallas_call(
        first_kernel,
        out_shape=jax.ShapeDtypeStruct((2 * tok_rows, head_dim), jnp.bfloat16),
        in_specs=[ANY] * len(first_in),
        out_specs=VMEM,
        scratch_shapes=[pltpu.VMEM(x.shape, x.dtype) for x in first_in[:-1]]
        + [pltpu.VMEM((tok_rows, head_dim), jnp.float32)]
        + [pltpu.SemaphoreType.DMA((len(first_in) + 1,))],
        name="norm_kv",
    )(*first_in)

    kv_blocks, kv_bias = [own_kv], [jnp.float32(0.0)]
    for k in range(1, line):
        up = make_pairs(lambda s, h, k=k: ((s + k * side) % seq_count, h))
        kv_blocks.append(lax.ppermute(own_kv, BOTH, up))
        kv_bias.append(jnp.where(line_index >= k, 0.0, NEGATIVE))
    if side == 2:
        swap = make_pairs(lambda s, h: (s ^ 1, h))
        for k in range(line):
            kv_blocks.append(lax.ppermute(kv_blocks[k], BOTH, swap))
            seen = line_index >= k if k else side_index == 1
            kv_bias.append(jnp.where(seen, 0.0, NEGATIVE))

    rows_here = tok_rows // head_count
    top_count = expert_ids.shape[1]
    halves = 2 if line % 2 == 0 else 1
    local_count = w_gate.shape[0]
    experts_all = local_count * seq_count * head_count
    experts_half = experts_all // halves
    members = seq_count * head_count // halves
    capacity = max(2, 3 * rows_here * top_count // (2 * experts_all))
    slots = experts_half * capacity
    first_expert = (seq_index // (seq_count // halves)) * experts_half
    mirror = make_pairs(lambda s, h: ((line - 1 - s // side) * side + s % side, h))
    mixing = route_weights / jnp.sum(route_weights, axis=1, keepdims=True)

    def slot_tables(ids, weights, zero):
        here = first_expert + zero + jnp.arange(experts_half, dtype=jnp.int32)
        named = ids[:, :, None] == here[None, None, :]
        counts = jnp.sum(named, axis=1).astype(jnp.bfloat16)
        earlier = (
            jnp.arange(rows_here)[:, None] > jnp.arange(rows_here)[None, :]
        ).astype(jnp.bfloat16)
        rank_table = jnp.dot(earlier, counts, preferred_element_type=jnp.float32)
        mix_table = jnp.sum(jnp.where(named, weights[:, :, None], 0.0), axis=1)
        place = jnp.where(counts > 0, rank_table, -1.0).astype(jnp.int32)
        in_slot = place[:, :, None] == (zero + jnp.arange(capacity, dtype=jnp.int32))[None, None, :]
        pick = in_slot.astype(jnp.bfloat16).reshape(rows_here, slots)
        mix = jnp.where(in_slot, mix_table[:, :, None], 0.0).reshape(rows_here, slots)
        return pick, jnp.concatenate(split_exact(mix), axis=0)

    tables = [slot_tables(expert_ids, mixing, jnp.int32(0))]

    query_step = 2 * head_dim if heads_here % 2 == 0 else head_dim
    rot_q = pl.pallas_call(
        functools.partial(query_kernel, head_dim, query_step),
        out_shape=jax.ShapeDtypeStruct((tok_rows, w_query.shape[1]), jnp.bfloat16),
        in_specs=[VMEM] * 5,
        out_specs=VMEM,
        compiler_params=room(16),
        name="queries",
    )(tokens, input_gain[None], w_query, query_gain[None], table)

    near = line // 2
    if side == 2:
        parts = [
            [*range(near), *range(line, line + near - 1)],
            [*range(near, line - 1), *range(line + near - 1, line + near)],
            [line - 1, *range(line + near, 2 * line - 1)],
            [2 * line - 1],
        ]
    else:
        parts = [[*range(near)], [*range(near, line)]]
    parts = [part for part in parts if part]
    state = ()
    for n, part in enumerate(parts):
        state = attend(
            rot_q,
            head_dim,
            [kv_blocks[k] for k in part],
            [kv_bias[k] for k in part],
            state,
            n == len(parts) - 1,
        )
    attended = state

    by_tower = attended.reshape(towers, cores * rows_here, attended.shape[1])
    core_swap = make_pairs(lambda s, h: (s, h ^ 1))

    def tower_sum(k):
        rows = lax.dynamic_index_in_dim(
            by_tower, (tower_index + k) % towers, 0, keepdims=False
        )
        part = jnp.dot(rows, w_out, preferred_element_type=jnp.float32).reshape(
            cores, rows_here, width
        )
        if cores == 1:
            return part[0]
        keep = lax.dynamic_index_in_dim(part, core_index, 0, keepdims=False)
        give = lax.dynamic_index_in_dim(part, 1 - core_index, 0, keepdims=False)
        came = lax.ppermute(give.astype(jnp.bfloat16), BOTH, core_swap)
        return keep + came.astype(jnp.float32)

    attn_part = None
    for k in range(1, towers):
        shift = make_pairs(lambda s, h, k=k: (s, (h + k * cores) % head_count))
        given = tower_sum(k).astype(jnp.bfloat16)
        came = lax.ppermute(given, BOTH, shift).astype(jnp.float32)
        attn_part = came if attn_part is None else attn_part + came
    own_sum = tower_sum(0)
    attn_part = own_sum if attn_part is None else own_sum + attn_part

    own_rows = lax.dynamic_slice_in_dim(tokens, head_index * rows_here, rows_here, 0)
    residual = own_rows.astype(jnp.float32) + attn_part
    routed = rms_scale(residual, post_gain).astype(jnp.bfloat16)

    groups = [list(range(g * members, (g + 1) * members)) for g in range(halves)]

    def exchange(rows):
        return lax.all_to_all(
            rows.reshape(members, local_count * capacity, width),
            BOTH,
            split_axis=0,
            concat_axis=0,
            axis_index_groups=groups,
            tiled=True,
        )

    def dispatch(outgoing):
        return (
            exchange(outgoing)
            .reshape(members, local_count, capacity, width)
            .transpose(1, 0, 2, 3)
            .reshape(local_count, members * capacity, width)
        )

    def fill_slots(rows, pick):
        return lax.dot_general(
            pick, rows, (((0,), (0,)), ((), ())), preferred_element_type=jnp.float32
        ).astype(jnp.bfloat16)

    def give_back(result, mix):
        came = exchange(
            result.reshape(local_count, members, capacity, width).transpose(1, 0, 2, 3)
        ).reshape(slots, width)
        both = jnp.dot(mix, came, preferred_element_type=jnp.float32)
        return both[:rows_here] + both[rows_here:]

    gates = [pltpu.with_memory_space_constraint(w_gate[e], pltpu.VMEM) for e in range(local_count)]
    weights = (gates, w_up, w_down)
    if halves == 2:
        mirrored = lax.ppermute(routed, BOTH, mirror)
        own_rows_in = dispatch(fill_slots(routed, tables[0][0]))
        sent = jnp.concatenate([expert_ids.astype(jnp.float32), mixing], axis=1)
        seen = lax.ppermute(sent, BOTH, mirror)
        tables.append(
            slot_tables(
                seen[:, :top_count].astype(jnp.int32),
                seen[:, top_count:],
                lax.optimization_barrier(jnp.int32(0)),
            )
        )
        filled = pl.pallas_call(
            fill_kernel,
            out_shape=jax.ShapeDtypeStruct((slots, width), jnp.bfloat16),
            in_specs=[VMEM] * 3,
            out_specs=VMEM,
            name="fill",
        )(mirrored, tables[1][0], gates[0])
        far_rows_in = dispatch(filled)
        own_result = run_experts(own_rows_in, *weights)
        far_result = run_experts(far_rows_in, *weights)
        foreign = give_back(far_result, tables[1][1]).astype(jnp.bfloat16)
        far_sum = lax.ppermute(foreign, BOTH, mirror)
        came_back = exchange(
            own_result.reshape(local_count, members, capacity, width).transpose(1, 0, 2, 3)
        ).reshape(slots, width)
        return pl.pallas_call(
            finish_kernel,
            out_shape=jax.ShapeDtypeStruct((rows_here, width), jnp.bfloat16),
            in_specs=[VMEM] * 4,
            out_specs=VMEM,
            compiler_params=room(16),
            name="finish",
        )(tables[0][1], came_back, far_sum, residual)
    else:
        result = run_experts(dispatch(fill_slots(routed, tables[0][0])), *weights)
        expert_sum = give_back(result, tables[0][1])
    return (residual + expert_sum).astype(jnp.bfloat16)


def solution(mesh):
    placed = (
        P("seq", None),
        P(),
        P(None, "head"),
        P(None, "head"),
        P(None, "head"),
        P(),
        P(),
        P("head", None),
        P(),
        P(("seq", "head"), None),
        P(("seq", "head"), None),
        P(("seq", "head"), None, None),
        P(("seq", "head"), None, None),
        P(("seq", "head"), None, None),
    )

    return jax.shard_map(
        body, mesh=mesh, in_specs=placed, out_specs=P(("seq", "head"), None), check_vma=False
    )
```
